32 devices in a mesh: seq: 8 (over y, x, core), head: 4 (over z).
Axes of the slice: x: 2, y: 2, z: 4, core: 2. Of those that a mesh axis runs over, the one named last changes fastest.
Arguments:
- layer_input: bfloat16 [4096, 1536], P('seq'), may hold values from -6 to 6
- output_grad: bfloat16 [4096, 1536], P('seq'), may hold values from -6 to 6
- norm_gain: float32 [1536], replicated, may hold values from 0.5 to 1.5
- proj_main: float32 [1536, 2, 3072], P(None, None, 'head'), may hold values from -0.15625 to 0.15625
- proj_state: float32 [1536, 2, 128], P(None, None, 'head'), may hold values from -0.15625 to 0.15625
- proj_step: float32 [1536, 48], P(None, 'head'), may hold values from -0.15625 to 0.15625
- conv_main: float32 [5, 3072], P(None, 'head'), may hold values from -3 to 3
- conv_state: float32 [5, 2, 128], P(None, None, 'head'), may hold values from -3 to 3
- head_coef: float32 [3, 48], P(None, 'head'), may hold values from -10 to 4, as said below
- gate_gain: float32 [3072], P('head'), may hold values from 0.5 to 1.5
- proj_out: float32 [3072, 1536], P('head'), may hold values from -0.109375 to 0.109375
- first_norm_gain: float32 [1536], replicated, may hold values from -20 to 20
- first_proj_main: float32 [1536, 2, 3072], P('seq', None, 'head'), may hold values from -20 to 20
- first_proj_state: float32 [1536, 2, 128], P('seq', None, 'head'), may hold values from -20 to 20
- first_proj_step: float32 [1536, 48], P('seq', 'head'), may hold values from -20 to 20
- first_conv_main: float32 [5, 3072], P(None, 'head'), may hold values from -20 to 20
- first_conv_state: float32 [5, 2, 128], P(None, None, 'head'), may hold values from -20 to 20
- first_head_coef: float32 [3, 48], P(None, 'head'), may hold values from -20 to 20
- first_gate_gain: float32 [3072], P('head'), may hold values from -20 to 20
- first_proj_out: float32 [3072, 1536], P('head', 'seq'), may hold values from -20 to 20
- second_norm_gain: float32 [1536], replicated, may hold values from 40.96 to 163.84
- second_proj_main: float32 [1536, 2, 3072], P('seq', None, 'head'), may hold values from 40.96 to 163.84
- second_proj_state: float32 [1536, 2, 128], P('seq', None, 'head'), may hold values from 40.96 to 163.84
- second_proj_step: float32 [1536, 48], P('seq', 'head'), may hold values from 40.96 to 163.84
- second_conv_main: float32 [5, 3072], P(None, 'head'), may hold values from 40.96 to 163.84
- second_conv_state: float32 [5, 2, 128], P(None, None, 'head'), may hold values from 40.96 to 163.84
- second_head_coef: float32 [3, 48], P(None, 'head'), may hold values from 40.96 to 163.84
- second_gate_gain: float32 [3072], P('head'), may hold values from 40.96 to 163.84
- second_proj_out: float32 [3072, 1536], P('head', 'seq'), may hold values from 40.96 to 163.84
Outputs:
- layer_output: bfloat16 [4096, 1536], P('seq', 'head')
- input_grad: bfloat16 [4096, 1536], P('seq')
- grad_norm_gain: float32 [1536], replicated
- grad_proj_main: float32 [1536, 2, 3072], P('seq', None, 'head')
- grad_proj_state: float32 [1536, 2, 128], P('seq', None, 'head')
- grad_proj_step: float32 [1536, 48], P('seq', 'head')
- grad_conv_main: float32 [5, 3072], P(None, 'head')
- grad_conv_state: float32 [5, 2, 128], P(None, None, 'head')
- grad_head_coef: float32 [3, 48], P(None, 'head')
- grad_gate_gain: float32 [3072], P('head')
- grad_proj_out: float32 [3072, 1536], P('head', 'seq')
- new_norm_gain: float32 [1536], replicated
- new_proj_main: float32 [1536, 2, 3072], P(None, None, 'head')
- new_proj_state: float32 [1536, 2, 128], P(None, None, 'head')
- new_proj_step: float32 [1536, 48], P(None, 'head')
- new_conv_main: float32 [5, 3072], P(None, 'head')
- new_conv_state: float32 [5, 2, 128], P(None, None, 'head')
- new_head_coef: float32 [3, 48], P(None, 'head')
- new_gate_gain: float32 [3072], P('head')
- new_proj_out: float32 [3072, 1536], P('head')
- new_first_norm_gain: float32 [1536], replicated
- new_first_proj_main: float32 [1536, 2, 3072], P('seq', None, 'head')
- new_first_proj_state: float32 [1536, 2, 128], P('seq', None, 'head')
- new_first_proj_step: float32 [1536, 48], P('seq', 'head')
- new_first_conv_main: float32 [5, 3072], P(None, 'head')
- new_first_conv_state: float32 [5, 2, 128], P(None, None, 'head')
- new_first_head_coef: float32 [3, 48], P(None, 'head')
- new_first_gate_gain: float32 [3072], P('head')
- new_first_proj_out: float32 [3072, 1536], P('head', 'seq')
- new_second_norm_gain: float32 [1536], replicated
- new_second_proj_main: float32 [1536, 2, 3072], P('seq', None, 'head')
- new_second_proj_state: float32 [1536, 2, 128], P('seq', None, 'head')
- new_second_proj_step: float32 [1536, 48], P('seq', 'head')
- new_second_conv_main: float32 [5, 3072], P(None, 'head')
- new_second_conv_state: float32 [5, 2, 128], P(None, None, 'head')
- new_second_head_coef: float32 [3, 48], P(None, 'head')
- new_second_gate_gain: float32 [3072], P('head')
- new_second_proj_out: float32 [3072, 1536], P('head', 'seq')
The draws below stay inside these ranges and needn't reach their ends.
Inputs may be any that keep to these rules, and one draw needn't show every extreme that they name: `head_coef`: row 0 holds each head's time-step bias, row 1 the logarithm of its decay coefficient, row 2 its skip weight.
All inputs are finite; a program needn't handle non-finite values.
Results may differ from the reference program's by a relative error of at most 0.006.
The reference program's roundings to bfloat16 on the way (of `normed`, `normal_out` and `back_main`) count: a program that leaves them out, or rounds other values in their place, can miss the bound.
Values sent between devices are 32-bit elements; how exact they have to be, the bound alone decides.
No kernel may reach another device: no remote copies, remote signals or barrier semaphores. Data moves between devices by JAX's collectives and lax.ppermute only.
A program may use at most 192 MiB of HBM per device.

```python
import math
import jax
import jax.numpy as jnp
from jax import lax

MODEL = 1536
HEADS = 48
HEAD_DIM = 64
STATE = 128
CONV = 4
SCAN_BLOCK = 256
INNER = 3072
SEQ_LEN = 4096


def draw_head_coef(key, part):
    subkeys = jax.random.split(key, 5)
    step_base = jnp.exp(jax.random.uniform(subkeys[0], (HEADS,), jnp.float32, jnp.log(0.001), jnp.log(0.1)))
    step_bias = jnp.log(jnp.expm1(step_base))
    keep_share = 0.5
    keeping = jax.random.bernoulli(subkeys[1], keep_share, (HEADS,))
    slow_rate = jnp.exp(jax.random.uniform(subkeys[2], (HEADS,), jnp.float32, jnp.log(0.2 / SEQ_LEN), jnp.log(2.0 / SEQ_LEN)))
    fast_rate = jnp.exp(jax.random.uniform(subkeys[3], (HEADS,), jnp.float32, jnp.log(1.0 / 200.0), jnp.log(1.0 / 30.0)))
    rate_value = jnp.where(keeping, slow_rate, fast_rate)
    skip_value = jax.random.uniform(subkeys[4], (HEADS,), jnp.float32, 0.5, 1.5)
    return jnp.stack([step_bias, jnp.log(rate_value / step_base), skip_value]).astype(jnp.float32)


def level_of(stream_key, extent, cuts, smallest, top_value):
    loudness, own = 1.0, jax.random.fold_in(stream_key, 6)
    for axis_at, parts in cuts:
        steps = jnp.exp(jax.random.uniform(jax.random.fold_in(own, axis_at), (parts,), jnp.float32, smallest / len(cuts), top_value / len(cuts)))
        loudness = loudness * jnp.repeat(steps, extent[axis_at] // parts).reshape([-1 if axis == axis_at else 1 for axis in range(len(extent))])
    return loudness


def bell_draw(own_key, shape, spread, most, shards=(), kind=jnp.bfloat16):
    level = level_of(own_key, shape, shards, -0.22, 0.18) if shards else 1.0
    drawn = jax.random.normal(own_key, shape, jnp.float32) * spread * level
    return jnp.minimum(jnp.maximum(drawn, -most), most).astype(kind)


def setup_inputs(seed: int = 0) -> dict:
    key_list = jax.random.split(jax.random.key(seed), 30)
    layer_input = bell_draw(key_list[0], (SEQ_LEN, MODEL), 1.0, 6.0, ((0, 8),))
    output_grad = bell_draw(key_list[1], (SEQ_LEN, MODEL), 1.0, 6.0, ((0, 8),))
    norm_gain = jnp.clip(1.0 + 0.1 * jax.random.normal(key_list[2], (MODEL,), jnp.float32), 0.5, 1.5)
    proj_main = bell_draw(key_list[3], (MODEL, 2, INNER), MODEL ** -0.5, 0.15625, ((2, 4),), jnp.float32)
    proj_state = bell_draw(key_list[4], (MODEL, 2, STATE), MODEL ** -0.5, 0.15625, ((2, 4),), jnp.float32)
    proj_step = bell_draw(key_list[5], (MODEL, HEADS), MODEL ** -0.5, 0.15625, ((1, 4),), jnp.float32)
    conv_main = bell_draw(key_list[6], (CONV + 1, INNER), CONV ** -0.5, 3.0, ((1, 4),), jnp.float32)
    conv_state = bell_draw(key_list[7], (CONV + 1, 2, STATE), CONV ** -0.5, 3.0, ((2, 4),), jnp.float32)
    head_coef = draw_head_coef(jax.random.fold_in(key_list[29], 71), 0)
    gate_gain = jnp.clip(1.0 + 0.1 * jax.random.normal(key_list[9], (INNER,), jnp.float32), 0.5, 1.5)
    proj_out = bell_draw(key_list[10], (INNER, MODEL), INNER ** -0.5, 0.109375, ((0, 4),), jnp.float32)
    first_norm_gain = bell_draw(key_list[11], (MODEL,), (0.05 * SEQ_LEN ** 0.5), 20.0, (), jnp.float32)
    first_proj_main = bell_draw(key_list[12], (MODEL, 2, INNER), (0.05 * SEQ_LEN ** 0.5), 20.0, ((0, 8), (2, 4)), jnp.float32)
    first_proj_state = bell_draw(key_list[13], (MODEL, 2, STATE), (0.05 * SEQ_LEN ** 0.5), 20.0, ((0, 8), (2, 4)), jnp.float32)
    first_proj_step = bell_draw(key_list[14], (MODEL, HEADS), (0.05 * SEQ_LEN ** 0.5), 20.0, ((0, 8), (1, 4)), jnp.float32)
    first_conv_main = bell_draw(key_list[15], (CONV + 1, INNER), (0.05 * SEQ_LEN ** 0.5), 20.0, ((1, 4),), jnp.float32)
    first_conv_state = bell_draw(key_list[16], (CONV + 1, 2, STATE), (0.05 * SEQ_LEN ** 0.5), 20.0, ((2, 4),), jnp.float32)
    first_head_coef = bell_draw(key_list[17], (3, HEADS), (0.05 * SEQ_LEN ** 0.5), 20.0, ((1, 4),), jnp.float32)
    first_gate_gain = bell_draw(key_list[18], (INNER,), (0.05 * SEQ_LEN ** 0.5), 20.0, ((0, 4),), jnp.float32)
    first_proj_out = bell_draw(key_list[19], (INNER, MODEL), (0.05 * SEQ_LEN ** 0.5), 20.0, ((0, 4), (1, 8)), jnp.float32)
    second_norm_gain = jnp.clip(jnp.exp(jax.random.uniform(key_list[20], (MODEL,), jnp.float32, math.log(40.96), math.log(163.84))), 40.96, 163.84)
    second_proj_main = jnp.clip(jnp.exp(math.log(163.84) - 1.3862944 * jax.random.uniform(key_list[21], (MODEL, 2, INNER), jnp.float32) ** level_of(key_list[21], (MODEL, 2, INNER), ((0, 8), (2, 4)), -0.2, 0.2)), 40.96, 163.84)
    second_proj_state = jnp.clip(jnp.exp(math.log(163.84) - 1.3862944 * jax.random.uniform(key_list[22], (MODEL, 2, STATE), jnp.float32) ** level_of(key_list[22], (MODEL, 2, STATE), ((0, 8), (2, 4)), -0.2, 0.2)), 40.96, 163.84)
    second_proj_step = jnp.clip(jnp.exp(math.log(163.84) - 1.3862944 * jax.random.uniform(key_list[23], (MODEL, HEADS), jnp.float32) ** level_of(key_list[23], (MODEL, HEADS), ((0, 8), (1, 4)), -0.2, 0.2)), 40.96, 163.84)
    second_conv_main = jnp.clip(jnp.exp(math.log(163.84) - 1.3862944 * jax.random.uniform(key_list[24], (CONV + 1, INNER), jnp.float32) ** level_of(key_list[24], (CONV + 1, INNER), ((1, 4),), -0.2, 0.2)), 40.96, 163.84)
    second_conv_state = jnp.clip(jnp.exp(math.log(163.84) - 1.3862944 * jax.random.uniform(key_list[25], (CONV + 1, 2, STATE), jnp.float32) ** level_of(key_list[25], (CONV + 1, 2, STATE), ((2, 4),), -0.2, 0.2)), 40.96, 163.84)
    second_head_coef = jnp.clip(jnp.exp(math.log(163.84) - 1.3862944 * jax.random.uniform(key_list[26], (3, HEADS), jnp.float32) ** level_of(key_list[26], (3, HEADS), ((1, 4),), -0.2, 0.2)), 40.96, 163.84)
    second_gate_gain = jnp.clip(jnp.exp(math.log(163.84) - 1.3862944 * jax.random.uniform(key_list[27], (INNER,), jnp.float32) ** level_of(key_list[27], (INNER,), ((0, 4),), -0.2, 0.2)), 40.96, 163.84)
    second_proj_out = jnp.clip(jnp.exp(math.log(163.84) - 1.3862944 * jax.random.uniform(key_list[28], (INNER, MODEL), jnp.float32) ** level_of(key_list[28], (INNER, MODEL), ((0, 4), (1, 8)), -0.2, 0.2)), 40.96, 163.84)
    return {"layer_input": layer_input, "output_grad": output_grad, "norm_gain": norm_gain, "proj_main": proj_main, "proj_state": proj_state, "proj_step": proj_step, "conv_main": conv_main, "conv_state": conv_state, "head_coef": head_coef, "gate_gain": gate_gain, "proj_out": proj_out, "first_norm_gain": first_norm_gain, "first_proj_main": first_proj_main, "first_proj_state": first_proj_state, "first_proj_step": first_proj_step, "first_conv_main": first_conv_main, "first_conv_state": first_conv_state, "first_head_coef": first_head_coef, "first_gate_gain": first_gate_gain, "first_proj_out": first_proj_out, "second_norm_gain": second_norm_gain, "second_proj_main": second_proj_main, "second_proj_state": second_proj_state, "second_proj_step": second_proj_step, "second_conv_main": second_conv_main, "second_conv_state": second_conv_state, "second_head_coef": second_head_coef, "second_gate_gain": second_gate_gain, "second_proj_out": second_proj_out}


precise = lax.Precision.HIGHEST
norm_epsilon = 1e-05
beta_first = 0.9
beta_second = 0.95
adam_epsilon = 1e-08
weight_decay = 0.1
adam_step = 2
rate_matrix = 0.005
rate_vector = 0.15
rate_coef = 0.6

def contract(left, right, left_dim, right_dim):
    return lax.dot_general(left, right, (((left_dim,), (right_dim,)), ((), ())), preferred_element_type=jnp.float32)

def input_norm(source, gain):
    return source * lax.rsqrt(lax.optimization_barrier(jnp.mean(source * source, axis=1, keepdims=True)) + norm_epsilon) * gain

def convolve(padded, tap_table):
    tap_count = tap_table.shape[0] - 1
    length = padded.shape[0] - tap_count + 1
    total = jnp.broadcast_to(tap_table[tap_count], (length, tap_table.shape[1]))
    for offset in range(tap_count):
        total = total + tap_table[offset] * padded[offset:offset + length]
    return jax.nn.silu(total)

def step_map(step_pre, coef_table):
    step_sizes = jax.nn.softplus(step_pre + coef_table[0])
    return (step_sizes, -jnp.exp(coef_table[1]) * step_sizes)

def segment_step(carry_state, pieces):
    head_values, state_input, state_output, step_sizes, log_decay = pieces
    cumulative = jnp.cumsum(log_decay, axis=0)
    scores = jnp.dot(state_output, state_input.T, precision=precise)
    gaps = cumulative.T[:, :, None] - cumulative.T[:, None, :]
    later_row = lax.broadcasted_iota(jnp.int32, gaps.shape, 1)
    early_col = lax.broadcasted_iota(jnp.int32, gaps.shape, 2)
    mixing = jnp.exp(jnp.where(later_row >= early_col, gaps, -jnp.inf)) * scores[None] * step_sizes.T[:, None, :]
    within = jnp.einsum('hts,shp->thp', mixing, head_values, precision=precise)
    across = jnp.exp(cumulative)[:, :, None] * jnp.einsum('tn,hpn->thp', state_output, carry_state, precision=precise)
    weighting = jnp.exp(cumulative[-1][None, :] - cumulative) * step_sizes
    new_state = jnp.exp(cumulative[-1])[:, None, None] * carry_state + jnp.einsum('shp,sn->hpn', head_values * weighting[:, :, None], state_input, precision=precise)
    return (new_state, within + across)

def state_pass(head_values, state_input, state_output, step_sizes, log_decay, start_state, block_len, stepper):
    length, local_heads, head_size = head_values.shape
    count_blocks = length // block_len
    pieces = (head_values.reshape(count_blocks, block_len, local_heads, head_size), state_input.reshape(count_blocks, block_len, state_input.shape[1]), state_output.reshape(count_blocks, block_len, state_output.shape[1]), step_sizes.reshape(count_blocks, block_len, local_heads), log_decay.reshape(count_blocks, block_len, local_heads))
    end_state, outputs = lax.scan(stepper, start_state, pieces)
    return (outputs.reshape(length, local_heads, head_size), end_state)

def middle(main_pre, state_pre, step_pre, rim_rows, start_state, tap_table, head_coef, gate_gain):
    length = main_pre.shape[0]
    gate_pre = main_pre[:, :INNER]
    conv_input = jnp.concatenate([main_pre[:, INNER:], state_pre], axis=1)
    activated = convolve(jnp.concatenate([rim_rows, conv_input], axis=0), tap_table)
    head_values = activated[:, :INNER].reshape(length, HEADS, HEAD_DIM)
    state_input = activated[:, INNER:INNER + STATE]
    state_output = activated[:, INNER + STATE:]
    step_sizes, log_decay = step_map(step_pre, head_coef)
    scan_out, end_state = state_pass(head_values, state_input, state_output, step_sizes, log_decay, start_state, SCAN_BLOCK, jax.checkpoint(segment_step))
    mixed = (scan_out + head_coef[2][None, :, None] * head_values).reshape(length, INNER)
    gated = mixed * jax.nn.silu(gate_pre)
    row_scale = lax.rsqrt(lax.optimization_barrier(jnp.mean(gated * gated, axis=1, keepdims=True)) + norm_epsilon)
    return (gated * row_scale * gate_gain, end_state)

def adam_update(weight, gradient, moment_one, moment_two, step_rate):
    first_new = beta_first * moment_one + (1.0 - beta_first) * gradient
    second_new = beta_second * moment_two + (1.0 - beta_second) * gradient * gradient
    first_hat = first_new / (1.0 - beta_first ** adam_step)
    second_hat = second_new / (1.0 - beta_second ** adam_step)
    updated = weight - step_rate * (first_hat / (jnp.sqrt(second_hat) + adam_epsilon) + weight_decay * weight)
    return (updated, first_new, second_new)

def reference(layer_input, output_grad, norm_gain, proj_main, proj_state, proj_step, conv_main, conv_state, head_coef, gate_gain, proj_out, first_norm_gain, first_proj_main, first_proj_state, first_proj_step, first_conv_main, first_conv_state, first_head_coef, first_gate_gain, first_proj_out, second_norm_gain, second_proj_main, second_proj_state, second_proj_step, second_conv_main, second_conv_state, second_head_coef, second_gate_gain, second_proj_out):
    block_rows = min(4096, SEQ_LEN)
    block_count = SEQ_LEN // block_rows
    main_weight = proj_main.reshape(MODEL, 2 * INNER).astype(jnp.bfloat16)
    state_weight = proj_state.reshape(MODEL, 2 * STATE).astype(jnp.bfloat16)
    step_weight = proj_step.astype(jnp.bfloat16)
    out_weight = proj_out.astype(jnp.bfloat16)
    tap_table = jnp.concatenate([conv_main, conv_state.reshape(CONV + 1, 2 * STATE)], axis=1)

    def project(row_block):
        source = row_block.astype(jnp.float32)
        normed = input_norm(source, norm_gain).astype(jnp.bfloat16)
        main_pre = jnp.dot(normed, main_weight, preferred_element_type=jnp.float32)
        state_pre = jnp.dot(normed, state_weight, preferred_element_type=jnp.float32)
        step_pre = jnp.dot(normed, step_weight, preferred_element_type=jnp.float32)
        return (source, normed, main_pre, state_pre, step_pre)

    def forward_step(carry, row_block):
        start_state, rim_rows = carry
        source, normed, main_pre, state_pre, step_pre = project(row_block)
        normal_float, end_state = middle(main_pre, state_pre, step_pre, rim_rows, start_state, tap_table, head_coef, gate_gain)
        normal_out = normal_float.astype(jnp.bfloat16)
        layer_rows = (source + jnp.dot(normal_out, out_weight, preferred_element_type=jnp.float32)).astype(jnp.bfloat16)
        conv_input = jnp.concatenate([main_pre[:, INNER:], state_pre], axis=1)
        return ((end_state, conv_input[block_rows - CONV + 1:]), (layer_rows, start_state, rim_rows))
    init_state = jnp.zeros((HEADS, HEAD_DIM, STATE), jnp.float32)
    init_rim = jnp.zeros((CONV - 1, INNER + 2 * STATE), jnp.float32)
    row_blocks = layer_input.reshape(block_count, block_rows, MODEL)
    grad_blocks = output_grad.reshape(block_count, block_rows, MODEL)
    _, (layer_blocks, start_states, rim_blocks) = lax.scan(forward_step, (init_state, init_rim), row_blocks)

    def backward_step(carry, pieces):
        state_grad, rim_grad, totals = carry
        row_block, grad_rows, start_state, rim_rows = pieces
        source, normed, main_pre, state_pre, step_pre = project(row_block)
        (normal_float, end_state), middle_pull = jax.vjp(middle, main_pre, state_pre, step_pre, rim_rows, start_state, tap_table, head_coef, gate_gain)
        normal_out = normal_float.astype(jnp.bfloat16)
        back_normal = contract(grad_rows, out_weight, 1, 1)
        back_main_pre, back_state_pre, back_step_pre, back_rim, back_start, back_taps, back_coef, back_gate = middle_pull((back_normal, state_grad))
        conv_back = jnp.concatenate([back_main_pre[:, INNER:], back_state_pre], axis=1)
        conv_back = conv_back + jnp.concatenate([jnp.zeros((block_rows - CONV + 1, conv_back.shape[1]), jnp.float32), rim_grad], axis=0)
        back_main = jnp.concatenate([back_main_pre[:, :INNER], conv_back[:, :INNER]], axis=1).astype(jnp.bfloat16)
        back_state = conv_back[:, INNER:].astype(jnp.bfloat16)
        back_step = back_step_pre.astype(jnp.bfloat16)
        back_normed = contract(back_main, main_weight, 1, 1) + contract(back_state, state_weight, 1, 1) + contract(back_step, step_weight, 1, 1)
        _, norm_pull = jax.vjp(input_norm, source, norm_gain)
        back_source, back_gain = norm_pull(back_normed)
        input_rows = (grad_rows.astype(jnp.float32) + back_source).astype(jnp.bfloat16)
        terms = (back_gain, contract(normed, back_main, 0, 0), contract(normed, back_state, 0, 0), contract(normed, back_step, 0, 0), back_taps, back_coef, back_gate, contract(normal_out, grad_rows, 0, 0))
        totals = jax.tree.map(jnp.add, totals, terms)
        return ((back_start, back_rim, totals), input_rows)
    zero_totals = (jnp.zeros((MODEL,), jnp.float32), jnp.zeros((MODEL, 2 * INNER), jnp.float32), jnp.zeros((MODEL, 2 * STATE), jnp.float32), jnp.zeros((MODEL, HEADS), jnp.float32), jnp.zeros((CONV + 1, INNER + 2 * STATE), jnp.float32), jnp.zeros((3, HEADS), jnp.float32), jnp.zeros((INNER,), jnp.float32), jnp.zeros((INNER, MODEL), jnp.float32))
    (_, _, totals), input_blocks = lax.scan(backward_step, (init_state, init_rim, zero_totals), (row_blocks, grad_blocks, start_states, rim_blocks), reverse=True)
    grad_gain, grad_main, grad_state, grad_step, grad_taps, grad_coef, grad_gate, grad_out = totals
    grad_main = grad_main.reshape(MODEL, 2, INNER)
    grad_state = grad_state.reshape(MODEL, 2, STATE)
    grad_conv_main = grad_taps[:, :INNER]
    grad_conv_state = grad_taps[:, INNER:].reshape(CONV + 1, 2, STATE)
    new_gain, first_gain, second_gain = adam_update(norm_gain, grad_gain, first_norm_gain, second_norm_gain, rate_vector)
    new_main, first_main, second_main = adam_update(proj_main, grad_main, first_proj_main, second_proj_main, rate_matrix)
    new_state, first_state, second_state = adam_update(proj_state, grad_state, first_proj_state, second_proj_state, rate_matrix)
    new_step, first_step, second_step = adam_update(proj_step, grad_step, first_proj_step, second_proj_step, rate_matrix)
    new_cmain, first_cmain, second_cmain = adam_update(conv_main, grad_conv_main, first_conv_main, second_conv_main, rate_vector)
    new_cstate, first_cstate, second_cstate = adam_update(conv_state, grad_conv_state, first_conv_state, second_conv_state, rate_vector)
    new_coef, first_coef, second_coef = adam_update(head_coef, grad_coef, first_head_coef, second_head_coef, rate_coef)
    new_gate, first_gate, second_gate = adam_update(gate_gain, grad_gate, first_gate_gain, second_gate_gain, rate_vector)
    new_out, first_out, second_out = adam_update(proj_out, grad_out, first_proj_out, second_proj_out, rate_matrix)
    return (layer_blocks.reshape(SEQ_LEN, MODEL), input_blocks.reshape(SEQ_LEN, MODEL), grad_gain, grad_main, grad_state, grad_step, grad_conv_main, grad_conv_state, grad_coef, grad_gate, grad_out, new_gain, new_main, new_state, new_step, new_cmain, new_cstate, new_coef, new_gate, new_out, first_gain, first_main, first_state, first_step, first_cmain, first_cstate, first_coef, first_gate, first_out, second_gain, second_main, second_state, second_step, second_cmain, second_cstate, second_coef, second_gate, second_out)
```

```python
import functools

import jax
import jax.numpy as jnp
from jax import lax
from jax.experimental import pallas as pl
from jax.experimental.pallas import tpu as pltpu
from jax.sharding import PartitionSpec as P


CHUNK = 128
LANES = 128
HEAD_ROWS = 16

norm_epsilon = 1e-05
beta_first = 0.9
beta_second = 0.95
adam_epsilon = 1e-08
weight_decay = 0.1
adam_step = 2
rate_matrix = 0.005
rate_vector = 0.15
rate_coef = 0.6

NN = ((1,), (0,))
NT = ((1,), (1,))


def swap(value, axis, bit):
    return lax.ppermute(value, axis, [(i, i ^ bit) for i in range(lax.axis_size(axis))])


def shift(value, axis, by):
    count = lax.axis_size(axis)
    return lax.ppermute(value, axis, [(i, (i + by) % count) for i in range(count)])


def from_behind(value, axis, by):
    devices = lax.axis_size(axis)
    pairs = [(i, i + by) for i in range(devices) if 0 <= i + by < devices]
    return lax.ppermute(value, axis, pairs)


def bits_of(axis):
    count, bits = lax.axis_size(axis), []
    while 2 ** len(bits) < count:
        bits.append(2 ** len(bits))
    return bits


def sum_all(value, axis):
    for bit in bits_of(axis):
        value = value + swap(value, axis, bit)
    return value


def bit_of(axis, bit):
    return (lax.axis_index(axis) // bit) % 2


def scatter_rows(value, axis):
    bits = bits_of(axis)
    places = len(bits)
    rows = value.shape[0] // 2**places
    cut = value.reshape((2,) * places + (rows,) + value.shape[1:])

    def halve(part, bit):
        dim = places - 1 - bits.index(bit)
        mine = bit_of(axis, bit)
        keep = lax.dynamic_slice_in_dim(part, mine, 1, dim)
        send = lax.dynamic_slice_in_dim(part, 1 - mine, 1, dim)
        return keep + swap(send, axis, bit)

    cut = halve(cut, bits[0])
    pieces = [
        lax.slice_in_dim(cut, 0, rows // 2, axis=places),
        lax.slice_in_dim(cut, rows // 2, rows, axis=places),
    ]
    orders = [bits[1:], bits[1:][::-1]]
    for step in range(places - 1):
        pieces = [halve(part, order[step]) for part, order in zip(pieces, orders)]
    return jnp.concatenate(pieces, axis=places).reshape((rows,) + value.shape[1:])


def gather_rows(value, axis):
    bits = bits_of(axis)
    places = len(bits)
    rows = value.shape[0]
    cut = value.reshape((1,) * places + value.shape)

    def double(part, bit):
        dim = places - 1 - bits.index(bit)
        other = swap(part, axis, bit)
        first = bit_of(axis, bit) == 0
        return jnp.concatenate(
            [jnp.where(first, part, other), jnp.where(first, other, part)], axis=dim
        )

    pieces = [
        lax.slice_in_dim(cut, 0, rows // 2, axis=places),
        lax.slice_in_dim(cut, rows // 2, rows, axis=places),
    ]
    orders = [bits[1:][::-1], bits[1:]]
    for step in range(places - 1):
        pieces = [double(part, order[step]) for part, order in zip(pieces, orders)]
    cut = double(jnp.concatenate(pieces, axis=places), bits[0])
    return cut.reshape((rows * 2**places,) + value.shape[1:])


def line_scatter(block_of, axis):
    count, place = lax.axis_size(axis), lax.axis_index(axis)
    right = block_of(lax.rem(place + count - 1, count))
    left = block_of(lax.rem(place + 1, count))
    for step in range(1, count):
        got_right = lax.ppermute(right, axis, [(i, i + 1) for i in range(step)])
        got_left = lax.ppermute(
            left, axis, [(count - 1 - i, count - 2 - i) for i in range(step)]
        )
        if step < count - 1:
            right = got_right + block_of(lax.rem(place + count - step - 1, count))
            left = got_left + block_of(lax.rem(place + step + 1, count))
    return block_of(place) + got_right + got_left


def line_gather(value, axis):
    count, place = lax.axis_size(axis), lax.axis_index(axis)
    right = left = value
    from_left, from_right = [], []
    for step in range(1, count):
        right = lax.ppermute(right, axis, [(i, i + 1) for i in range(step - 1, count - 1)])
        left = lax.ppermute(left, axis, [(i + 1, i) for i in range(count - step)])
        from_left.append(right)
        from_right.append(left)
    whole = jnp.zeros((count,) + value.shape, value.dtype)
    whole = lax.dynamic_update_index_in_dim(whole, value, place, 0)
    for step in range(1, count):
        block = jnp.where(place >= step, from_left[step - 1], from_right[count - step - 1])
        whole = lax.dynamic_update_index_in_dim(
            whole, block, lax.rem(place + count - step, count), 0
        )
    return whole


def ring_gather(value, axis):
    count, place = lax.axis_size(axis), lax.axis_index(axis)
    whole = jnp.zeros((count,) + value.shape, value.dtype)
    whole = lax.dynamic_update_index_in_dim(whole, value, place, 0)
    for by in range(1, count):
        whole = lax.dynamic_update_index_in_dim(
            whole, shift(value, axis, by), lax.rem(place + count - by, count), 0
        )
    return whole


def carried_state(decay, part, axis, reverse):
    total_decay, total = decay, part
    before = jnp.zeros_like(part)
    bits = bits_of(axis)
    for bit in bits:
        other = swap(total, axis, bit)
        other_decay = swap(total_decay, axis, bit)
        high = bit_of(axis, bit) == 1
        later = jnp.logical_not(high) if reverse else high
        if bit == bits[0]:
            before_decay = jnp.ones_like(decay)
        before = jnp.where(later, before + before_decay * other, before)
        before_decay = jnp.where(later, before_decay * other_decay, before_decay)
        if bit != bits[-1]:
            total = jnp.where(later, total + total_decay * other, other + other_decay * total)
            total_decay = total_decay * other_decay
    return before


def dot(left, right, dims):
    return lax.dot_general(left, right, (dims, ((), ())), preferred_element_type=jnp.float32)


def two(value):
    high = value.astype(jnp.bfloat16)
    return high, (value - high.astype(jnp.float32)).astype(jnp.bfloat16)


def three(value):
    high = value.astype(jnp.bfloat16)
    rest = value - high.astype(jnp.float32)
    mid = rest.astype(jnp.bfloat16)
    return high, mid, (rest - mid.astype(jnp.float32)).astype(jnp.bfloat16)


def mul(left, right, dims=NN):
    (lh, ll), (rh, rl) = two(left), two(right)
    return dot(lh, rh, dims) + (dot(lh, rl, dims) + dot(ll, rh, dims))


def mul_mask(mask, value, dims=NN):
    high, mid, low = three(value)
    return dot(mask, high, dims) + (dot(mask, mid, dims) + dot(mask, low, dims))


def mul_by_mask(value, mask, dims=NN):
    high, mid, low = three(value)
    return dot(high, mask, dims) + (dot(mid, mask, dims) + dot(low, mask, dims))


def head_mask(width, head_size):
    row = lax.broadcasted_iota(jnp.int32, (LANES, width), 0)
    col = lax.broadcasted_iota(jnp.int32, (LANES, width), 1)
    low = row * head_size
    return jnp.where((col >= low) & (col < low + head_size), 1.0, 0.0).astype(jnp.bfloat16)


def order_mask(size, upper):
    row = lax.broadcasted_iota(jnp.int32, (size, size), 0)
    col = lax.broadcasted_iota(jnp.int32, (size, size), 1)
    return (row <= col) if upper else (row >= col)


def soft_plus(value):
    return jnp.maximum(value, 0.0) + jnp.log1p(jnp.exp(-jnp.abs(value)))


def sigmoid(value):
    return 1.0 / (1.0 + jnp.exp(-value))


def states_kernel(
    head_size, x_ref, bt_ref, step_ref, coef_ref,
    dt_ref, dtx_ref, cumx_ref, cumt_ref, st_ref, pre_ref, post_ref,
):
    length, width = x_ref.shape
    count = length // CHUNK
    spread = head_mask(width, head_size)
    lower = jnp.where(order_mask(CHUNK, False), 1.0, 0.0).astype(jnp.bfloat16)
    state = jnp.zeros((bt_ref.shape[0], width), jnp.float32)
    run = jnp.zeros((1, width), jnp.float32)
    rate = -jnp.exp(coef_ref[1:2, :])
    bias = coef_ref[0:1, :]
    runs = []
    for c in range(count):
        at = slice(c * CHUNK, (c + 1) * CHUNK)
        steps = soft_plus(step_ref[at, :] + bias)
        cum = mul_mask(lower, rate * steps)
        dtx = mul_by_mask(steps, spread)
        cumx = mul_by_mask(cum, spread)
        dt_ref[at, :] = steps
        dtx_ref[at, :] = dtx
        cumx_ref[at, :] = cumx
        cumt_ref[:, at] = jnp.transpose(cum)[:HEAD_ROWS, :]
        total = cumx[CHUNK - 1 : CHUNK, :]
        st_ref[c] = state
        pre_ref[c] = jnp.broadcast_to(jnp.exp(run), (8, width))
        state = jnp.exp(total) * state + mul(
            bt_ref[:, at], x_ref[at, :] * dtx * jnp.exp(total - cumx)
        )
        run = run + total
        runs.append(total)
    st_ref[count] = state
    pre_ref[count] = jnp.broadcast_to(jnp.exp(run), (8, width))
    rest = jnp.zeros((1, width), jnp.float32)
    for c in range(count - 1, -1, -1):
        post_ref[c] = jnp.broadcast_to(jnp.exp(rest), (8, width))
        rest = rest + runs[c]


def lane_halves(size, width):
    return lax.broadcasted_iota(jnp.int32, (size, width), 1) < width // 2


def within_kernel(head_size, x_ref, bt_ref, ct_ref, dtx_ref, cumx_ref, cumt_ref, st_ref, y_ref):
    width = x_ref.shape[1]
    pair = 2 * head_size
    reads = jnp.transpose(ct_ref[...])
    scores = mul(reads, bt_ref[...])
    mask = order_mask(CHUNK, False)
    first = lane_halves(CHUNK, pair)
    for p in range(width // pair):
        at = slice(p * pair, (p + 1) * pair)
        cumx = cumx_ref[:, at]
        scaled = x_ref[:, at] * dtx_ref[:, at]
        mixing = []
        for h in range(2):
            row = cumt_ref[2 * p + h : 2 * p + h + 1, :]
            col = cumx[:, h * head_size : h * head_size + 1]
            mixing.append(jnp.exp(jnp.where(mask, col - row, -1e30)) * scores)
        stacked = jnp.concatenate(
            [jnp.where(first, scaled, 0.0), jnp.where(first, 0.0, scaled)], axis=0
        )
        inner = mul(jnp.concatenate(mixing, axis=1), stacked)
        y_ref[:, at] = inner + jnp.exp(cumx) * mul(reads, st_ref[0, :, at])


def gate_kernel(
    y_ref, ct_ref, cumx_ref, pre_ref, start_ref, x_ref, skip_ref, gate_ref, back_ref, gain_ref,
    mixed_ref, sums_ref,
):
    width = x_ref.shape[1]
    reads = jnp.transpose(ct_ref[...])
    carried = jnp.exp(cumx_ref[...]) * pre_ref[0, 0:1, :] * mul(reads, start_ref[...])
    mixed = y_ref[...] + carried + skip_ref[0:1, :] * x_ref[...]
    gate = gate_ref[...]
    gated = mixed * (gate * sigmoid(gate))
    mixed_ref[...] = mixed
    ones = jnp.ones((8, width), jnp.bfloat16)
    sums_ref[0:8, :] = mul_mask(ones, gated * gated, NT)
    sums_ref[8:16, :] = mul_mask(ones, back_ref[...] * gain_ref[0:1, :] * gated, NT)


def turn_kernel(
    full_inner, sums_ref, mixed_ref, gate_ref, back_ref, gain_ref, x_ref, cumx_ref, ct_ref,
    skip_ref,
    normal_ref, dy_ref, bgate_ref, ggate_ref, gskip_ref, g_ref, jump_ref, carry_ref,
):
    step = pl.program_id(0)

    @pl.when(step == 0)
    def _():
        carry_ref[...] = jnp.zeros_like(carry_ref)
        ggate_ref[...] = jnp.zeros_like(ggate_ref)
        gskip_ref[...] = jnp.zeros_like(gskip_ref)

    columns = jnp.transpose(sums_ref[...])
    scale = lax.rsqrt(columns[:, 0:1] / full_inner + norm_epsilon)
    inner = columns[:, 8:9] / full_inner
    mixed = mixed_ref[...]
    gate = gate_ref[...]
    share = sigmoid(gate)
    act = gate * share
    gated = mixed * act
    gain = gain_ref[0:1, :]
    back = back_ref[...]
    scaled = gated * scale
    normal_ref[...] = (scaled * gain).astype(jnp.bfloat16)
    back_gated = scale * (back * gain) - gated * (scale * scale * scale) * inner
    dy = back_gated * act
    dy_ref[...] = dy
    bgate_ref[...] = (back_gated * mixed * (share * (1.0 + gate * (1.0 - share)))).astype(
        jnp.bfloat16
    )
    ggate_ref[...] += jnp.broadcast_to(
        jnp.sum(back * scaled, axis=0, keepdims=True), ggate_ref.shape
    )
    gskip_ref[...] += jnp.broadcast_to(
        jnp.sum(dy * x_ref[...], axis=0, keepdims=True), gskip_ref.shape
    )
    carry = carry_ref[...]
    g_ref[0] = carry
    cumx = cumx_ref[...]
    carry = jnp.exp(cumx[CHUNK - 1 : CHUNK, :]) * carry + mul(ct_ref[...], dy * jnp.exp(cumx))
    carry_ref[...] = carry
    jump_ref[...] = carry


def back_within_kernel(
    head_size, x_ref, bt_ref, ct_ref, dtx_ref, cumx_ref, cumt_ref, st_ref, pre_ref, start_ref,
    dy_ref, g_ref,
    z_ref, db_ref, dc_ref,
):
    width = x_ref.shape[1]
    pair = 2 * head_size
    inputs = jnp.transpose(bt_ref[...])
    scores = mul(inputs, ct_ref[...])
    mask = order_mask(CHUNK, True)
    first = lane_halves(CHUNK, pair)
    grad_scores = jnp.zeros((CHUNK, CHUNK), jnp.float32)
    for p in range(width // pair):
        at = slice(p * pair, (p + 1) * pair)
        cumx = cumx_ref[:, at]
        dy = dy_ref[:, at]
        scaled = x_ref[:, at] * dtx_ref[:, at]
        products = mul(
            jnp.concatenate(
                [jnp.where(first, scaled, 0.0), jnp.where(first, 0.0, scaled)], axis=0
            ),
            dy,
            NT,
        )
        mixing = []
        for h in range(2):
            row = cumt_ref[2 * p + h : 2 * p + h + 1, :]
            col = cumx[:, h * head_size : h * head_size + 1]
            decay = jnp.exp(jnp.where(mask, row - col, -1e30))
            grad_scores = grad_scores + decay * products[h * CHUNK : (h + 1) * CHUNK, :]
            mixing.append(decay * scores)
        stacked = jnp.concatenate([jnp.where(first, dy, 0.0), jnp.where(first, 0.0, dy)], axis=0)
        inner = mul(jnp.concatenate(mixing, axis=1), stacked)
        decay_out = jnp.exp(cumx[CHUNK - 1 : CHUNK, :] - cumx)
        z_ref[:, at] = inner + decay_out * mul(inputs, g_ref[0, :, at])
    cumx = cumx_ref[...]
    scaled = x_ref[...] * dtx_ref[...] * jnp.exp(cumx[CHUNK - 1 : CHUNK, :] - cumx)
    entering = st_ref[0] + pre_ref[0, 0:1, :] * start_ref[...]
    reads = jnp.transpose(ct_ref[...])
    db_ref[...] = mul(grad_scores, reads) + mul(scaled, g_ref[0], NT)
    dc_ref[...] = mul(jnp.transpose(grad_scores), inputs) + mul(
        dy_ref[...] * jnp.exp(cumx), entering, NT
    )


def back_steps_kernel(
    head_size, x_ref, bt_ref, dtx_ref, cumx_ref, dt_ref, step_ref, coef_ref, skip_ref, mixed_ref,
    dy_ref, z_ref, db_ref, dc_ref, g_ref, later_ref, post_ref, end_ref, pre_ref, start_ref,
    dx_ref, dbt_ref, dct_ref, dstep_ref, gcoef_ref,
):
    width = x_ref.shape[1]

    @pl.when(pl.program_id(0) == 0)
    def _():
        gcoef_ref[...] = jnp.zeros_like(gcoef_ref)

    spread = head_mask(width, head_size)
    upper = jnp.where(order_mask(CHUNK, True), 1.0, 0.0).astype(jnp.bfloat16)
    x = x_ref[...]
    dy = dy_ref[...]
    cumx = cumx_ref[...]
    skip = skip_ref[0:1, :]
    dtx = dtx_ref[...]
    later = later_ref[...]
    post = post_ref[0, 0:1, :]
    inputs = jnp.transpose(bt_ref[...])
    decay_out = post * jnp.exp(cumx[CHUNK - 1 : CHUNK, :] - cumx)
    z = z_ref[...] + decay_out * mul(inputs, later)
    dx_ref[...] = dtx * z + skip * dy
    db = db_ref[...] + mul(x * dtx * decay_out, later, NT)
    dbt_ref[...] = jnp.transpose(db)
    dct_ref[...] = jnp.transpose(dc_ref[...])
    steps = dt_ref[...]
    by_step = mul_by_mask(x * z, spread, NT)
    by_out = mul_by_mask(dy * (mixed_ref[...] - skip * x), spread, NT)
    leaving = end_ref[0] + pre_ref[0, 0:1, :] * start_ref[...]
    held = jnp.sum((g_ref[0] + post * later) * leaving, axis=0, keepdims=True)
    held = mul_by_mask(jnp.broadcast_to(held, (8, width)), spread, NT)[0:1, :]
    by_decay = mul_mask(upper, by_out - steps * by_step) + held
    rate = -jnp.exp(coef_ref[1:2, :])
    back = (by_step + rate * by_decay) * sigmoid(step_ref[...] + coef_ref[0:1, :])
    dstep_ref[...] = back
    gcoef_ref[0:8, :] += jnp.broadcast_to(jnp.sum(back, axis=0, keepdims=True), (8, LANES))
    gcoef_ref[8:16, :] += jnp.broadcast_to(
        jnp.sum(by_decay * rate * steps, axis=0, keepdims=True), (8, LANES)
    )


def full(array_shape):
    zeros = (0,) * len(array_shape)
    return pl.BlockSpec(array_shape, lambda i: zeros)


def run(kernel, grid, in_specs, out_specs, out_shapes, args, scratch=(), flops=0):
    moved = sum(a.size * a.dtype.itemsize for a in args) + sum(
        s.size * s.dtype.itemsize for s in out_shapes
    )
    return pl.pallas_call(
        kernel,
        grid=grid,
        in_specs=in_specs,
        out_specs=out_specs,
        out_shape=out_shapes,
        scratch_shapes=scratch,
        cost_estimate=pl.CostEstimate(flops=flops, bytes_accessed=moved, transcendentals=0),
        compiler_params=pltpu.CompilerParams(
            dimension_semantics=("arbitrary",) * len(grid), vmem_limit_bytes=48 * 2**20
        ),
    )(*args)


def contract(left, right, left_dim, right_dim):
    return lax.dot_general(
        left, right, (((left_dim,), (right_dim,)), ((), ())), preferred_element_type=jnp.float32
    )


def input_norm(source, gain):
    return (
        source * lax.rsqrt(jnp.mean(source * source, axis=1, keepdims=True) + norm_epsilon) * gain
    )


def convolve(padded, tap_table):
    tap_count = tap_table.shape[0] - 1
    length = padded.shape[0] - tap_count + 1
    total = jnp.broadcast_to(tap_table[tap_count], (length, tap_table.shape[1]))
    for offset in range(tap_count):
        total = total + tap_table[offset] * padded[offset : offset + length]
    return jax.nn.silu(total)


def adam_update(weight, gradient, moment_one, moment_two, step_rate):
    first_new = beta_first * moment_one + (1.0 - beta_first) * gradient
    second_new = beta_second * moment_two + (1.0 - beta_second) * gradient * gradient
    first_hat = first_new / (1.0 - beta_first**adam_step)
    second_hat = second_new / (1.0 - beta_second**adam_step)
    updated = weight - step_rate * (
        first_hat / (jnp.sqrt(second_hat) + adam_epsilon) + weight_decay * weight
    )
    return (updated, first_new, second_new)


def rows_of_eight(vector):
    return jnp.broadcast_to(vector[None, :], (8, vector.shape[0]))


def per_device(
    layer_input, output_grad, norm_gain, proj_main, proj_state, proj_step, conv_main, conv_state,
    head_coef, gate_gain, proj_out, first_norm_gain, first_proj_main, first_proj_state,
    first_proj_step, first_conv_main, first_conv_state, first_head_coef, first_gate_gain,
    first_proj_out, second_norm_gain, second_proj_main, second_proj_state, second_proj_step,
    second_conv_main, second_conv_state, second_head_coef, second_gate_gain, second_proj_out,
):
    f32, bf16 = jnp.float32, jnp.bfloat16
    length, model_width = layer_input.shape
    local_heads = proj_step.shape[1]
    inner_width = proj_main.shape[2]
    head_size = inner_width // local_heads
    state_local = proj_state.shape[2]
    tap_count = conv_main.shape[0] - 1
    head_count = lax.axis_size("head")
    seq_count = lax.axis_size("seq")
    seq_index = lax.axis_index("seq")
    head_index = lax.axis_index("head")
    state_size = state_local * head_count
    full_inner = inner_width * head_count
    chunks = length // CHUNK
    chunk_row = pl.BlockSpec((CHUNK, inner_width), lambda i: (i, 0))
    chunk_lane = pl.BlockSpec((state_size, CHUNK), lambda i: (0, i))
    chunk_head = pl.BlockSpec((HEAD_ROWS, CHUNK), lambda i: (0, i))
    chunk_small = pl.BlockSpec((CHUNK, LANES), lambda i: (i, 0))
    chunk_state = pl.BlockSpec((CHUNK, state_size), lambda i: (i, 0))
    state_block = pl.BlockSpec((1, state_size, inner_width), lambda i: (i, 0, 0))
    next_state = pl.BlockSpec((1, state_size, inner_width), lambda i: (i + 1, 0, 0))
    row_block = pl.BlockSpec((1, 8, inner_width), lambda i: (i, 0, 0))
    next_row = pl.BlockSpec((1, 8, inner_width), lambda i: (i + 1, 0, 0))
    state_full = full((state_size, inner_width))
    row_full = full((8, inner_width))
    row_shape = jax.ShapeDtypeStruct((length, inner_width), f32)
    small_shape = jax.ShapeDtypeStruct((length, LANES), f32)
    state_shape = jax.ShapeDtypeStruct((state_size, inner_width), f32)
    scan_flops = 2 * 3 * length * inner_width * (2 * CHUNK + state_size)

    source = layer_input.astype(f32)
    normed_float, norm_pull = jax.vjp(input_norm, source, norm_gain)
    normed = normed_float.astype(bf16)
    state_weight = proj_state.reshape(model_width, 2 * state_local).astype(bf16)
    step_weight = proj_step.astype(bf16)
    step_wide = jnp.pad(step_weight, ((0, 0), (0, LANES - local_heads)))
    out_weight = proj_out.astype(bf16)
    main_weight = proj_main.reshape(model_width, 2 * inner_width).astype(bf16)
    coef_wide = jnp.pad(head_coef, ((0, 8 - head_coef.shape[0]), (0, LANES - local_heads)))
    skip_wide = rows_of_eight(jnp.repeat(head_coef[2], head_size))
    gain_wide = rows_of_eight(gate_gain)

    main_pre = jnp.dot(normed, main_weight, preferred_element_type=f32)
    state_pre = jnp.dot(normed, state_weight, preferred_element_type=f32)
    step_pre = jnp.dot(normed, step_wide, preferred_element_type=f32)
    gate_pre = main_pre[:, :inner_width]
    conv_input = jnp.concatenate([main_pre[:, inner_width:], state_pre], axis=1)
    rim_rows = from_behind(conv_input[length - tap_count + 1 :], "seq", 1)
    padded = jnp.concatenate([rim_rows, conv_input], axis=0)
    tap_table = jnp.concatenate(
        [conv_main, conv_state.reshape(tap_count + 1, 2 * state_local)], axis=1
    )
    activated, conv_pull = jax.vjp(convolve, padded, tap_table)
    values = activated[:, :inner_width]
    pair_lanes = ring_gather(activated[:, inner_width:].T, "head")
    pair_lanes = pair_lanes.reshape(head_count, 2, state_local, length)
    input_lanes = pair_lanes[:, 0].reshape(state_size, length)
    output_lanes = pair_lanes[:, 1].reshape(state_size, length)

    steps, steps_wide, cum_wide, cum_lanes, states, before, after = run(
        functools.partial(states_kernel, head_size),
        (1,),
        [full(a.shape) for a in (values, input_lanes, step_pre, coef_wide)],
        [
            full((length, LANES)),
            full((length, inner_width)),
            full((length, inner_width)),
            full((HEAD_ROWS, length)),
            full((chunks + 1, state_size, inner_width)),
            full((chunks + 1, 8, inner_width)),
            full((chunks, 8, inner_width)),
        ],
        [
            small_shape,
            row_shape,
            row_shape,
            jax.ShapeDtypeStruct((HEAD_ROWS, length), f32),
            jax.ShapeDtypeStruct((chunks + 1, state_size, inner_width), f32),
            jax.ShapeDtypeStruct((chunks + 1, 8, inner_width), f32),
            jax.ShapeDtypeStruct((chunks, 8, inner_width), f32),
        ],
        (values, input_lanes, step_pre, coef_wide),
        flops=scan_flops // 3,
    )
    through = before[chunks, 0:1]
    start_state = carried_state(through, states[chunks], "seq", False)
    local_out = run(
        functools.partial(within_kernel, head_size),
        (chunks,),
        [chunk_row, chunk_lane, chunk_lane, chunk_row, chunk_row, chunk_head, state_block],
        [chunk_row],
        [row_shape],
        (values, input_lanes, output_lanes, steps_wide, cum_wide, cum_lanes, states),
        flops=scan_flops,
    )[0]
    back_normal = contract(output_grad, out_weight, 1, 1)
    mixed, sums = run(
        gate_kernel,
        (chunks,),
        [
            chunk_row, chunk_lane, chunk_row, row_block, state_full, chunk_row, row_full,
            chunk_row, chunk_row, row_full,
        ],
        [chunk_row, pl.BlockSpec((16, CHUNK), lambda i: (0, i))],
        [row_shape, jax.ShapeDtypeStruct((16, length), f32)],
        (
            local_out, output_lanes, cum_wide, before, start_state, values, skip_wide,
            gate_pre, back_normal, gain_wide,
        ),
        flops=scan_flops // 4,
    )
    sums = sum_all(sums, "head")
    reverse_row = pl.BlockSpec((CHUNK, inner_width), lambda i: (chunks - 1 - i, 0))
    reverse_lane = pl.BlockSpec((state_size, CHUNK), lambda i: (0, chunks - 1 - i))
    normal_out, back_mixed, back_gate, grad_gate, grad_skip, later_local, state_jump = run(
        functools.partial(turn_kernel, float(full_inner)),
        (chunks,),
        [
            pl.BlockSpec((16, CHUNK), lambda i: (0, chunks - 1 - i)),
            reverse_row, reverse_row, reverse_row, row_full, reverse_row, reverse_row,
            reverse_lane, row_full,
        ],
        [
            reverse_row, reverse_row, reverse_row, row_full, row_full,
            pl.BlockSpec((1, state_size, inner_width), lambda i: (chunks - 1 - i, 0, 0)),
            state_full,
        ],
        [
            jax.ShapeDtypeStruct((length, inner_width), bf16),
            row_shape,
            jax.ShapeDtypeStruct((length, inner_width), bf16),
            jax.ShapeDtypeStruct((8, inner_width), f32),
            jax.ShapeDtypeStruct((8, inner_width), f32),
            jax.ShapeDtypeStruct((chunks, state_size, inner_width), f32),
            state_shape,
        ],
        (
            sums, mixed, gate_pre, back_normal, gain_wide, values, cum_wide, output_lanes,
            skip_wide,
        ),
        scratch=[pltpu.VMEM((state_size, inner_width), f32)],
        flops=scan_flops // 4,
    )
    later_grad = carried_state(through, state_jump, "seq", True)

    early = jnp.concatenate(
        [contract(normed, back_gate, 0, 0), contract(output_grad, normal_out, 0, 0)], axis=1
    )
    sum_early = scatter_rows(early, "seq")
    col_count = model_width // head_count

    def out_block(index):
        columns = lax.dynamic_slice_in_dim(out_weight, index * col_count, col_count, 1)
        return jnp.dot(normal_out, columns, preferred_element_type=f32)

    out_cols = line_scatter(out_block, "head")
    residual_cols = lax.dynamic_slice_in_dim(source, head_index * col_count, col_count, 1)
    layer_output = (residual_cols + out_cols).astype(bf16)

    z_local, db_local, dc_local = run(
        functools.partial(back_within_kernel, head_size),
        (chunks,),
        [
            chunk_row, chunk_lane, chunk_lane, chunk_row, chunk_row, chunk_head, state_block,
            row_block, state_full, chunk_row, state_block,
        ],
        [chunk_row, chunk_state, chunk_state],
        [
            row_shape,
            jax.ShapeDtypeStruct((length, state_size), f32),
            jax.ShapeDtypeStruct((length, state_size), f32),
        ],
        (
            values, input_lanes, output_lanes, steps_wide, cum_wide, cum_lanes, states, before,
            start_state, back_mixed, later_local,
        ),
        flops=2 * scan_flops,
    )
    back_values, back_in, back_out, back_step_pre, grad_coef_rows = run(
        functools.partial(back_steps_kernel, head_size),
        (chunks,),
        [
            chunk_row, chunk_lane, chunk_row, chunk_row, chunk_small, chunk_small,
            full(coef_wide.shape), row_full, chunk_row, chunk_row, chunk_row, chunk_state,
            chunk_state, state_block, state_full, row_block, next_state, next_row, state_full,
        ],
        [chunk_row, chunk_lane, chunk_lane, chunk_small, full((16, LANES))],
        [
            row_shape,
            jax.ShapeDtypeStruct((state_size, length), f32),
            jax.ShapeDtypeStruct((state_size, length), f32),
            small_shape,
            jax.ShapeDtypeStruct((16, LANES), f32),
        ],
        (
            values, input_lanes, steps_wide, cum_wide, steps, step_pre, coef_wide, skip_wide,
            mixed, back_mixed, z_local, db_local, dc_local, later_local, later_grad, after, states,
            before, start_state,
        ),
        flops=scan_flops // 2,
    )
    grad_coef = jnp.stack(
        [
            grad_coef_rows[0, :local_heads],
            grad_coef_rows[8, :local_heads],
            jnp.sum(grad_skip[0].reshape(local_heads, head_size), axis=1),
        ]
    )
    back_pair = jnp.stack([back_in, back_out]).reshape(2, head_count, state_local, length)

    def pair_block(index):
        return lax.dynamic_index_in_dim(back_pair, index, 1, False)

    back_local_pair = pair_block(head_index)
    for by in range(1, head_count):
        back_local_pair = back_local_pair + shift(
            pair_block(lax.rem(head_index + by, head_count)), "head", by
        )
    back_active = jnp.concatenate(
        [back_values, back_local_pair.reshape(2 * state_local, length).T], axis=1
    )
    back_padded, grad_taps = conv_pull(back_active)
    rim_back = from_behind(back_padded[: tap_count - 1], "seq", -1)
    back_conv = back_padded[tap_count - 1 :]
    rim_start = length - tap_count + 1
    back_conv = jnp.concatenate([back_conv[:rim_start], back_conv[rim_start:] + rim_back], axis=0)
    back_late = jnp.concatenate([back_conv, back_step_pre[:, :local_heads]], axis=1).astype(bf16)
    late_weight = jnp.concatenate(
        [main_weight[:, inner_width:], state_weight, step_weight], axis=1
    )
    gate_weight = main_weight[:, :inner_width]
    shard_rows = length // head_count

    def normed_block(index):
        gate_rows = lax.dynamic_slice_in_dim(back_gate, index * shard_rows, shard_rows, 0)
        late_rows = lax.dynamic_slice_in_dim(back_late, index * shard_rows, shard_rows, 0)
        return contract(gate_rows, gate_weight, 1, 1) + contract(late_rows, late_weight, 1, 1)

    back_normed = line_scatter(normed_block, "head")
    own_source = lax.dynamic_slice_in_dim(source, head_index * shard_rows, shard_rows, 0)
    _, norm_pull = jax.vjp(input_norm, own_source, norm_gain)
    back_source, grad_gain = norm_pull(back_normed)
    back_rows = line_gather(back_source, "head").reshape(length, model_width)
    input_grad = (output_grad.astype(f32) + back_rows).astype(bf16)

    late = contract(normed, back_late, 0, 0)
    sum_late = scatter_rows(late, "seq")

    def own_rows(array, along):
        piece_len = array.shape[along] // seq_count
        return lax.dynamic_slice_in_dim(array, seq_index * piece_len, piece_len, along)

    own_main = own_rows(proj_main, 0)
    sum_gate_half = sum_early[:, :inner_width]
    part_gate, first_gate_half, second_gate_half = adam_update(
        own_main[:, 0], sum_gate_half, first_proj_main[:, 0], second_proj_main[:, 0], rate_matrix
    )
    sum_out = sum_early[:, inner_width:].T
    part_out, first_out, second_out = adam_update(
        own_rows(proj_out, 1), sum_out, first_proj_out, second_proj_out, rate_matrix
    )
    new_early = gather_rows(jnp.concatenate([part_gate, part_out.T], axis=1), "seq")
    new_out = new_early[:, inner_width:].T

    sum_value = sum_late[:, :inner_width]
    part_value, first_value, second_value = adam_update(
        own_main[:, 1], sum_value, first_proj_main[:, 1], second_proj_main[:, 1], rate_matrix
    )
    sum_state = sum_late[:, inner_width : inner_width + 2 * state_local]
    part_state, first_state, second_state = adam_update(
        own_rows(proj_state, 0).reshape(-1, 2 * state_local),
        sum_state,
        first_proj_state.reshape(-1, 2 * state_local),
        second_proj_state.reshape(-1, 2 * state_local),
        rate_matrix,
    )
    sum_step = sum_late[:, inner_width + 2 * state_local :]
    part_step, first_step, second_step = adam_update(
        own_rows(proj_step, 0), sum_step, first_proj_step, second_proj_step, rate_matrix
    )
    new_late = gather_rows(
        jnp.concatenate([part_value, part_state, part_step], axis=1), "seq"
    )
    new_main = jnp.stack([new_early[:, :inner_width], new_late[:, :inner_width]], axis=1)
    new_state = new_late[:, inner_width : inner_width + 2 * state_local].reshape(
        model_width, 2, state_local
    )
    new_step = new_late[:, inner_width + 2 * state_local :]
    state_form = (-1, 2, state_local)
    sum_main = jnp.stack([sum_gate_half, sum_value], axis=1)
    first_main = jnp.stack([first_gate_half, first_value], axis=1)
    second_main = jnp.stack([second_gate_half, second_value], axis=1)

    taps_wide = inner_width + 2 * state_local
    small = jnp.concatenate(
        [
            grad_taps.reshape(-1),
            grad_gate[0],
            grad_coef.reshape(-1),
        ]
    )
    small_size = small.shape[0]
    padded_size = -(-small_size // 1024) * 1024
    small = jnp.pad(small, (0, padded_size - small_size)).reshape(8, padded_size // 8)
    small = sum_all(small, "seq").reshape(-1)
    taps_size = (tap_count + 1) * taps_wide
    sum_taps = small[:taps_size].reshape(tap_count + 1, taps_wide)
    sum_cmain = sum_taps[:, :inner_width]
    sum_cstate = sum_taps[:, inner_width:].reshape(tap_count + 1, 2, state_local)
    sum_gate = small[taps_size : taps_size + inner_width]
    sum_coef = small[taps_size + inner_width : small_size].reshape(3, local_heads)
    sum_gain = sum_all(sum_all(grad_gain, "head"), "seq")
    new_gain, first_gain, second_gain = adam_update(
        norm_gain, sum_gain, first_norm_gain, second_norm_gain, rate_vector
    )
    new_cmain, first_cmain, second_cmain = adam_update(
        conv_main, sum_cmain, first_conv_main, second_conv_main, rate_vector
    )
    new_cstate, first_cstate, second_cstate = adam_update(
        conv_state, sum_cstate, first_conv_state, second_conv_state, rate_vector
    )
    new_coef, first_coef, second_coef = adam_update(
        head_coef, sum_coef, first_head_coef, second_head_coef, rate_coef
    )
    new_gate, first_gate, second_gate = adam_update(
        gate_gain, sum_gate, first_gate_gain, second_gate_gain, rate_vector
    )
    return (
        layer_output, input_grad, sum_gain, sum_main, sum_state.reshape(state_form), sum_step,
        sum_cmain, sum_cstate, sum_coef, sum_gate, sum_out, new_gain, new_main, new_state,
        new_step, new_cmain, new_cstate, new_coef, new_gate, new_out, first_gain, first_main,
        first_state.reshape(state_form), first_step, first_cmain, first_cstate, first_coef,
        first_gate, first_out, second_gain, second_main, second_state.reshape(state_form),
        second_step, second_cmain, second_cstate, second_coef, second_gate, second_out,
    )


def solution(mesh):
    return jax.shard_map(
        per_device,
        mesh=mesh,
        in_specs=(
            P("seq", None),
            P("seq", None),
            P(),
            P(None, None, "head"),
            P(None, None, "head"),
            P(None, "head"),
            P(None, "head"),
            P(None, None, "head"),
            P(None, "head"),
            P("head"),
            P("head", None),
            P(),
            P("seq", None, "head"),
            P("seq", None, "head"),
            P("seq", "head"),
            P(None, "head"),
            P(None, None, "head"),
            P(None, "head"),
            P("head"),
            P("head", "seq"),
            P(),
            P("seq", None, "head"),
            P("seq", None, "head"),
            P("seq", "head"),
            P(None, "head"),
            P(None, None, "head"),
            P(None, "head"),
            P("head"),
            P("head", "seq"),
        ),
        out_specs=(
            P("seq", "head"),
            P("seq", None),
            P(),
            P("seq", None, "head"),
            P("seq", None, "head"),
            P("seq", "head"),
            P(None, "head"),
            P(None, None, "head"),
            P(None, "head"),
            P("head"),
            P("head", "seq"),
            P(),
            P(None, None, "head"),
            P(None, None, "head"),
            P(None, "head"),
            P(None, "head"),
            P(None, None, "head"),
            P(None, "head"),
            P("head"),
            P("head", None),
            P(),
            P("seq", None, "head"),
            P("seq", None, "head"),
            P("seq", "head"),
            P(None, "head"),
            P(None, None, "head"),
            P(None, "head"),
            P("head"),
            P("head", "seq"),
            P(),
            P("seq", None, "head"),
            P("seq", None, "head"),
            P("seq", "head"),
            P(None, "head"),
            P(None, None, "head"),
            P(None, "head"),
            P("head"),
            P("head", "seq"),
        ),
        check_vma=False,
    )
```

```python
import functools

import jax
import jax.numpy as jnp
from jax import lax
from jax.experimental import pallas as pl
from jax.experimental.pallas import tpu as pltpu
from jax.sharding import PartitionSpec as P


CHUNK = 128
LANES = 128
HEAD_ROWS = 16

norm_epsilon = 1e-05
beta_first = 0.9
beta_second = 0.95
adam_epsilon = 1e-08
weight_decay = 0.1
adam_step = 2
rate_matrix = 0.005
rate_vector = 0.15
rate_coef = 0.6

NN = ((1,), (0,))
NT = ((1,), (1,))


def swap(value, axis, bit):
    return lax.ppermute(value, axis, [(i, i ^ bit) for i in range(lax.axis_size(axis))])


def shift(value, axis, by):
    count = lax.axis_size(axis)
    return lax.ppermute(value, axis, [(i, (i + by) % count) for i in range(count)])


def from_behind(value, axis, by):
    devices = lax.axis_size(axis)
    pairs = [(i, i + by) for i in range(devices) if 0 <= i + by < devices]
    return lax.ppermute(value, axis, pairs)


def bits_of(axis):
    count, bits = lax.axis_size(axis), []
    while 2 ** len(bits) < count:
        bits.append(2 ** len(bits))
    return bits


def sum_all(value, axis):
    for bit in bits_of(axis):
        value = value + swap(value, axis, bit)
    return value


def bit_of(axis, bit):
    return (lax.axis_index(axis) // bit) % 2


def scatter_rows(value, axis):
    return lax.psum_scatter(value, axis, scatter_dimension=0, tiled=True)


def gather_rows(value, axis):
    return lax.all_gather(value, axis, axis=0, tiled=True)


def gather_small(value, axis):
    place = lax.axis_index(axis)
    rows = value.shape[0]
    whole = jnp.zeros((lax.axis_size(axis) * rows,) + value.shape[1:], value.dtype)
    whole = lax.dynamic_update_slice_in_dim(whole, value, place * rows, 0)
    for bit in bits_of(axis):
        base = (place // bit) * bit
        block = lax.dynamic_slice_in_dim(whole, base * rows, bit * rows, 0)
        other = swap(block, axis, bit)
        start = jnp.where(bit_of(axis, bit) == 0, base + bit, base - bit)
        whole = lax.dynamic_update_slice_in_dim(whole, other, start * rows, 0)
    return whole


def line_scatter(block_of, axis):
    count, place = lax.axis_size(axis), lax.axis_index(axis)
    right = block_of(lax.rem(place + count - 1, count))
    left = block_of(lax.rem(place + 1, count))
    for step in range(1, count):
        got_right = lax.ppermute(right, axis, [(i, i + 1) for i in range(step)])
        got_left = lax.ppermute(
            left, axis, [(count - 1 - i, count - 2 - i) for i in range(step)]
        )
        if step < count - 1:
            right = got_right + block_of(lax.rem(place + count - step - 1, count))
            left = got_left + block_of(lax.rem(place + step + 1, count))
    return block_of(place) + got_right + got_left


def line_gather(value, axis):
    count, place = lax.axis_size(axis), lax.axis_index(axis)
    right = left = value
    from_left, from_right = [], []
    for step in range(1, count):
        right = lax.ppermute(right, axis, [(i, i + 1) for i in range(step - 1, count - 1)])
        left = lax.ppermute(left, axis, [(i + 1, i) for i in range(count - step)])
        from_left.append(right)
        from_right.append(left)
    whole = jnp.zeros((count,) + value.shape, value.dtype)
    whole = lax.dynamic_update_index_in_dim(whole, value, place, 0)
    for step in range(1, count):
        block = jnp.where(place >= step, from_left[step - 1], from_right[count - step - 1])
        whole = lax.dynamic_update_index_in_dim(
            whole, block, lax.rem(place + count - step, count), 0
        )
    return whole


def ring_gather(value, axis):
    count, place = lax.axis_size(axis), lax.axis_index(axis)
    whole = jnp.zeros((count,) + value.shape, value.dtype)
    whole = lax.dynamic_update_index_in_dim(whole, value, place, 0)
    for by in range(1, count):
        whole = lax.dynamic_update_index_in_dim(
            whole, shift(value, axis, by), lax.rem(place + count - by, count), 0
        )
    return whole


def carried_state(decay, part, axis, reverse):
    total_decay, total = decay, part
    before = jnp.zeros_like(part)
    bits = bits_of(axis)
    for bit in bits:
        other = swap(total, axis, bit)
        other_decay = swap(total_decay, axis, bit)
        high = bit_of(axis, bit) == 1
        later = jnp.logical_not(high) if reverse else high
        if bit == bits[0]:
            before_decay = jnp.ones_like(decay)
        before = jnp.where(later, before + before_decay * other, before)
        before_decay = jnp.where(later, before_decay * other_decay, before_decay)
        if bit != bits[-1]:
            total = jnp.where(later, total + total_decay * other, other + other_decay * total)
            total_decay = total_decay * other_decay
    return before


def dot(left, right, dims):
    return lax.dot_general(left, right, (dims, ((), ())), preferred_element_type=jnp.float32)


def two(value):
    high = value.astype(jnp.bfloat16)
    return high, (value - high.astype(jnp.float32)).astype(jnp.bfloat16)


def three(value):
    high = value.astype(jnp.bfloat16)
    rest = value - high.astype(jnp.float32)
    mid = rest.astype(jnp.bfloat16)
    return high, mid, (rest - mid.astype(jnp.float32)).astype(jnp.bfloat16)


def mul(left, right, dims=NN):
    (lh, ll), (rh, rl) = two(left), two(right)
    return dot(lh, rh, dims) + (dot(lh, rl, dims) + dot(ll, rh, dims))


def mul_mask(mask, value, dims=NN):
    high, mid, low = three(value)
    return dot(mask, high, dims) + (dot(mask, mid, dims) + dot(mask, low, dims))


def mul_by_mask(value, mask, dims=NN):
    high, mid, low = three(value)
    return dot(high, mask, dims) + (dot(mid, mask, dims) + dot(low, mask, dims))


def head_mask(width, head_size):
    row = lax.broadcasted_iota(jnp.int32, (LANES, width), 0)
    col = lax.broadcasted_iota(jnp.int32, (LANES, width), 1)
    low = row * head_size
    return jnp.where((col >= low) & (col < low + head_size), 1.0, 0.0).astype(jnp.bfloat16)


def order_mask(size, upper):
    row = lax.broadcasted_iota(jnp.int32, (size, size), 0)
    col = lax.broadcasted_iota(jnp.int32, (size, size), 1)
    return (row <= col) if upper else (row >= col)


def soft_plus(value):
    return jnp.maximum(value, 0.0) + jnp.log1p(jnp.exp(-jnp.abs(value)))


def sigmoid(value):
    return 1.0 / (1.0 + jnp.exp(-value))


def states_kernel(
    head_size, x_ref, bt_ref, step_ref, coef_ref,
    dt_ref, dtx_ref, cumx_ref, cumt_ref, st_ref, pre_ref, post_ref,
):
    length, width = x_ref.shape
    count = length // CHUNK
    spread = head_mask(width, head_size)
    lower = jnp.where(order_mask(CHUNK, False), 1.0, 0.0).astype(jnp.bfloat16)
    state = jnp.zeros((bt_ref.shape[0], width), jnp.float32)
    run = jnp.zeros((1, width), jnp.float32)
    rate = -jnp.exp(coef_ref[1:2, :])
    bias = coef_ref[0:1, :]
    runs = []
    for c in range(count):
        at = slice(c * CHUNK, (c + 1) * CHUNK)
        steps = soft_plus(step_ref[at, :] + bias)
        cum = mul_mask(lower, rate * steps)
        dtx = mul_by_mask(steps, spread)
        cumx = mul_by_mask(cum, spread)
        dt_ref[at, :] = steps
        dtx_ref[at, :] = dtx
        cumx_ref[at, :] = cumx
        cumt_ref[:, at] = jnp.transpose(cum)[:HEAD_ROWS, :]
        total = cumx[CHUNK - 1 : CHUNK, :]
        st_ref[c] = state
        pre_ref[c] = jnp.broadcast_to(jnp.exp(run), (8, width))
        state = jnp.exp(total) * state + mul(
            bt_ref[:, at], x_ref[at, :] * dtx * jnp.exp(total - cumx)
        )
        run = run + total
        runs.append(total)
    st_ref[count] = state
    pre_ref[count] = jnp.broadcast_to(jnp.exp(run), (8, width))
    rest = jnp.zeros((1, width), jnp.float32)
    for c in range(count - 1, -1, -1):
        post_ref[c] = jnp.broadcast_to(jnp.exp(rest), (8, width))
        rest = rest + runs[c]


def lane_halves(size, width):
    return lax.broadcasted_iota(jnp.int32, (size, width), 1) < width // 2


def within_kernel(head_size, x_ref, bt_ref, ct_ref, dtx_ref, cumx_ref, cumt_ref, st_ref, y_ref):
    width = x_ref.shape[1]
    pair = 2 * head_size
    reads = jnp.transpose(ct_ref[...])
    scores = mul(reads, bt_ref[...])
    mask = order_mask(CHUNK, False)
    first = lane_halves(CHUNK, pair)
    for p in range(width // pair):
        at = slice(p * pair, (p + 1) * pair)
        cumx = cumx_ref[:, at]
        scaled = x_ref[:, at] * dtx_ref[:, at]
        mixing = []
        for h in range(2):
            row = cumt_ref[2 * p + h : 2 * p + h + 1, :]
            col = cumx[:, h * head_size : h * head_size + 1]
            mixing.append(jnp.exp(jnp.where(mask, col - row, -1e30)) * scores)
        stacked = jnp.concatenate(
            [jnp.where(first, scaled, 0.0), jnp.where(first, 0.0, scaled)], axis=0
        )
        inner = mul(jnp.concatenate(mixing, axis=1), stacked)
        y_ref[:, at] = inner + jnp.exp(cumx) * mul(reads, st_ref[0, :, at])


def gate_kernel(
    y_ref, ct_ref, cumx_ref, pre_ref, start_ref, x_ref, skip_ref, gate_ref, back_ref, gain_ref,
    mixed_ref, sums_ref,
):
    width = x_ref.shape[1]
    reads = jnp.transpose(ct_ref[...])
    carried = jnp.exp(cumx_ref[...]) * pre_ref[0, 0:1, :] * mul(reads, start_ref[...])
    mixed = y_ref[...] + carried + skip_ref[0:1, :] * x_ref[...]
    gate = gate_ref[...]
    gated = mixed * (gate * sigmoid(gate))
    mixed_ref[...] = mixed
    ones = jnp.ones((8, width), jnp.bfloat16)
    sums_ref[0:8, :] = mul_mask(ones, gated * gated, NT)
    sums_ref[8:16, :] = mul_mask(ones, back_ref[...] * gain_ref[0:1, :] * gated, NT)


def turn_kernel(
    full_inner, sums_ref, mixed_ref, gate_ref, back_ref, gain_ref, x_ref, cumx_ref, ct_ref,
    skip_ref,
    normal_ref, dy_ref, bgate_ref, ggate_ref, gskip_ref, g_ref, jump_ref, carry_ref,
):
    step = pl.program_id(0)

    @pl.when(step == 0)
    def _():
        carry_ref[...] = jnp.zeros_like(carry_ref)
        ggate_ref[...] = jnp.zeros_like(ggate_ref)
        gskip_ref[...] = jnp.zeros_like(gskip_ref)

    columns = jnp.transpose(sums_ref[...])
    scale = lax.rsqrt(columns[:, 0:1] / full_inner + norm_epsilon)
    inner = columns[:, 8:9] / full_inner
    mixed = mixed_ref[...]
    gate = gate_ref[...]
    share = sigmoid(gate)
    act = gate * share
    gated = mixed * act
    gain = gain_ref[0:1, :]
    back = back_ref[...]
    scaled = gated * scale
    normal_ref[...] = (scaled * gain).astype(jnp.bfloat16)
    back_gated = scale * (back * gain) - gated * (scale * scale * scale) * inner
    dy = back_gated * act
    dy_ref[...] = dy
    bgate_ref[...] = (back_gated * mixed * (share * (1.0 + gate * (1.0 - share)))).astype(
        jnp.bfloat16
    )
    ggate_ref[...] += jnp.broadcast_to(
        jnp.sum(back * scaled, axis=0, keepdims=True), ggate_ref.shape
    )
    gskip_ref[...] += jnp.broadcast_to(
        jnp.sum(dy * x_ref[...], axis=0, keepdims=True), gskip_ref.shape
    )
    carry = carry_ref[...]
    g_ref[0] = carry
    cumx = cumx_ref[...]
    carry = jnp.exp(cumx[CHUNK - 1 : CHUNK, :]) * carry + mul(ct_ref[...], dy * jnp.exp(cumx))
    carry_ref[...] = carry
    jump_ref[...] = carry


def back_within_kernel(
    head_size, x_ref, bt_ref, ct_ref, dtx_ref, cumx_ref, cumt_ref, st_ref, pre_ref, start_ref,
    dy_ref, g_ref,
    z_ref, db_ref, dc_ref,
):
    width = x_ref.shape[1]
    pair = 2 * head_size
    inputs = jnp.transpose(bt_ref[...])
    scores = mul(inputs, ct_ref[...])
    mask = order_mask(CHUNK, True)
    first = lane_halves(CHUNK, pair)
    grad_scores = jnp.zeros((CHUNK, CHUNK), jnp.float32)
    for p in range(width // pair):
        at = slice(p * pair, (p + 1) * pair)
        cumx = cumx_ref[:, at]
        dy = dy_ref[:, at]
        scaled = x_ref[:, at] * dtx_ref[:, at]
        products = mul(
            jnp.concatenate(
                [jnp.where(first, scaled, 0.0), jnp.where(first, 0.0, scaled)], axis=0
            ),
            dy,
            NT,
        )
        mixing = []
        for h in range(2):
            row = cumt_ref[2 * p + h : 2 * p + h + 1, :]
            col = cumx[:, h * head_size : h * head_size + 1]
            decay = jnp.exp(jnp.where(mask, row - col, -1e30))
            grad_scores = grad_scores + decay * products[h * CHUNK : (h + 1) * CHUNK, :]
            mixing.append(decay * scores)
        stacked = jnp.concatenate([jnp.where(first, dy, 0.0), jnp.where(first, 0.0, dy)], axis=0)
        inner = mul(jnp.concatenate(mixing, axis=1), stacked)
        decay_out = jnp.exp(cumx[CHUNK - 1 : CHUNK, :] - cumx)
        z_ref[:, at] = inner + decay_out * mul(inputs, g_ref[0, :, at])
    cumx = cumx_ref[...]
    scaled = x_ref[...] * dtx_ref[...] * jnp.exp(cumx[CHUNK - 1 : CHUNK, :] - cumx)
    entering = st_ref[0] + pre_ref[0, 0:1, :] * start_ref[...]
    reads = jnp.transpose(ct_ref[...])
    db_ref[...] = mul(grad_scores, reads) + mul(scaled, g_ref[0], NT)
    dc_ref[...] = mul(jnp.transpose(grad_scores), inputs) + mul(
        dy_ref[...] * jnp.exp(cumx), entering, NT
    )


def back_steps_kernel(
    head_size, x_ref, bt_ref, dtx_ref, cumx_ref, dt_ref, step_ref, coef_ref, skip_ref, mixed_ref,
    dy_ref, z_ref, db_ref, dc_ref, g_ref, later_ref, post_ref, end_ref, pre_ref, start_ref,
    dx_ref, dbt_ref, dct_ref, dstep_ref, gcoef_ref,
):
    width = x_ref.shape[1]

    @pl.when(pl.program_id(0) == 0)
    def _():
        gcoef_ref[...] = jnp.zeros_like(gcoef_ref)

    spread = head_mask(width, head_size)
    upper = jnp.where(order_mask(CHUNK, True), 1.0, 0.0).astype(jnp.bfloat16)
    x = x_ref[...]
    dy = dy_ref[...]
    cumx = cumx_ref[...]
    skip = skip_ref[0:1, :]
    dtx = dtx_ref[...]
    later = later_ref[...]
    post = post_ref[0, 0:1, :]
    inputs = jnp.transpose(bt_ref[...])
    decay_out = post * jnp.exp(cumx[CHUNK - 1 : CHUNK, :] - cumx)
    z = z_ref[...] + decay_out * mul(inputs, later)
    dx_ref[...] = dtx * z + skip * dy
    db = db_ref[...] + mul(x * dtx * decay_out, later, NT)
    dbt_ref[...] = jnp.transpose(db)
    dct_ref[...] = jnp.transpose(dc_ref[...])
    steps = dt_ref[...]
    by_step = mul_by_mask(x * z, spread, NT)
    by_out = mul_by_mask(dy * (mixed_ref[...] - skip * x), spread, NT)
    leaving = end_ref[0] + pre_ref[0, 0:1, :] * start_ref[...]
    held = jnp.sum((g_ref[0] + post * later) * leaving, axis=0, keepdims=True)
    held = mul_by_mask(jnp.broadcast_to(held, (8, width)), spread, NT)[0:1, :]
    by_decay = mul_mask(upper, by_out - steps * by_step) + held
    rate = -jnp.exp(coef_ref[1:2, :])
    back = (by_step + rate * by_decay) * sigmoid(step_ref[...] + coef_ref[0:1, :])
    dstep_ref[...] = back
    gcoef_ref[0:8, :] += jnp.broadcast_to(jnp.sum(back, axis=0, keepdims=True), (8, LANES))
    gcoef_ref[8:16, :] += jnp.broadcast_to(
        jnp.sum(by_decay * rate * steps, axis=0, keepdims=True), (8, LANES)
    )


def full(array_shape):
    zeros = (0,) * len(array_shape)
    return pl.BlockSpec(array_shape, lambda i: zeros)


def run(kernel, grid, in_specs, out_specs, out_shapes, args, scratch=(), flops=0):
    moved = sum(a.size * a.dtype.itemsize for a in args) + sum(
        s.size * s.dtype.itemsize for s in out_shapes
    )
    return pl.pallas_call(
        kernel,
        grid=grid,
        in_specs=in_specs,
        out_specs=out_specs,
        out_shape=out_shapes,
        scratch_shapes=scratch,
        cost_estimate=pl.CostEstimate(flops=flops, bytes_accessed=moved, transcendentals=0),
        compiler_params=pltpu.CompilerParams(
            dimension_semantics=("arbitrary",) * len(grid), vmem_limit_bytes=48 * 2**20
        ),
    )(*args)


def contract(left, right, left_dim, right_dim):
    return lax.dot_general(
        left, right, (((left_dim,), (right_dim,)), ((), ())), preferred_element_type=jnp.float32
    )


def input_norm(source, gain):
    return (
        source * lax.rsqrt(jnp.mean(source * source, axis=1, keepdims=True) + norm_epsilon) * gain
    )


def convolve(padded, tap_table):
    tap_count = tap_table.shape[0] - 1
    length = padded.shape[0] - tap_count + 1
    total = jnp.broadcast_to(tap_table[tap_count], (length, tap_table.shape[1]))
    for offset in range(tap_count):
        total = total + tap_table[offset] * padded[offset : offset + length]
    return jax.nn.silu(total)


def adam_update(weight, gradient, moment_one, moment_two, step_rate):
    first_new = beta_first * moment_one + (1.0 - beta_first) * gradient
    second_new = beta_second * moment_two + (1.0 - beta_second) * gradient * gradient
    first_hat = first_new / (1.0 - beta_first**adam_step)
    second_hat = second_new / (1.0 - beta_second**adam_step)
    updated = weight - step_rate * (
        first_hat / (jnp.sqrt(second_hat) + adam_epsilon) + weight_decay * weight
    )
    return (updated, first_new, second_new)


def adam_turned_kernel(grad_ref, weight_ref, one_ref, two_ref, part_ref, sum_ref, first_ref, second_ref):
    gradient = jnp.transpose(grad_ref[...])
    updated, first_new, second_new = adam_update(
        weight_ref[...], gradient, one_ref[...], two_ref[...], rate_matrix
    )
    part_ref[...] = jnp.transpose(updated)
    sum_ref[...] = gradient
    first_ref[...] = first_new
    second_ref[...] = second_new


def adam_turned(gradient, weight, moment_one, moment_two):
    rows, columns = weight.shape
    whole = [full((rows, columns))] * 3
    shape = jax.ShapeDtypeStruct((rows, columns), jnp.float32)
    return run(
        adam_turned_kernel,
        (1,),
        [full((columns, rows))] + whole,
        [full((columns, rows))] + whole,
        [jax.ShapeDtypeStruct((columns, rows), jnp.float32)] + [shape] * 3,
        (gradient, weight, moment_one, moment_two),
    )


def turn_block_kernel(in_ref, out_ref):
    out_ref[...] = jnp.transpose(in_ref[...])


def turned(array):
    rows, columns = array.shape
    block = 2 * CHUNK
    return run(
        turn_block_kernel,
        (rows // block,),
        [pl.BlockSpec((block, columns), lambda i: (i, 0))],
        [pl.BlockSpec((columns, block), lambda i: (0, i))],
        [jax.ShapeDtypeStruct((columns, rows), array.dtype)],
        (array,),
    )[0]


def rows_of_eight(vector):
    return jnp.broadcast_to(vector[None, :], (8, vector.shape[0]))


def per_device(
    layer_input, output_grad, norm_gain, proj_main, proj_state, proj_step, conv_main, conv_state,
    head_coef, gate_gain, proj_out, first_norm_gain, first_proj_main, first_proj_state,
    first_proj_step, first_conv_main, first_conv_state, first_head_coef, first_gate_gain,
    first_proj_out, second_norm_gain, second_proj_main, second_proj_state, second_proj_step,
    second_conv_main, second_conv_state, second_head_coef, second_gate_gain, second_proj_out,
):
    f32, bf16 = jnp.float32, jnp.bfloat16
    length, model_width = layer_input.shape
    local_heads = proj_step.shape[1]
    inner_width = proj_main.shape[2]
    head_size = inner_width // local_heads
    state_local = proj_state.shape[2]
    tap_count = conv_main.shape[0] - 1
    head_count = lax.axis_size("head")
    seq_count = lax.axis_size("seq")
    seq_index = lax.axis_index("seq")
    head_index = lax.axis_index("head")
    state_size = state_local * head_count
    full_inner = inner_width * head_count
    chunks = length // CHUNK
    chunk_row = pl.BlockSpec((CHUNK, inner_width), lambda i: (i, 0))
    chunk_lane = pl.BlockSpec((state_size, CHUNK), lambda i: (0, i))
    chunk_head = pl.BlockSpec((HEAD_ROWS, CHUNK), lambda i: (0, i))
    chunk_small = pl.BlockSpec((CHUNK, LANES), lambda i: (i, 0))
    chunk_state = pl.BlockSpec((CHUNK, state_size), lambda i: (i, 0))
    state_block = pl.BlockSpec((1, state_size, inner_width), lambda i: (i, 0, 0))
    next_state = pl.BlockSpec((1, state_size, inner_width), lambda i: (i + 1, 0, 0))
    row_block = pl.BlockSpec((1, 8, inner_width), lambda i: (i, 0, 0))
    next_row = pl.BlockSpec((1, 8, inner_width), lambda i: (i + 1, 0, 0))
    state_full = full((state_size, inner_width))
    row_full = full((8, inner_width))
    row_shape = jax.ShapeDtypeStruct((length, inner_width), f32)
    small_shape = jax.ShapeDtypeStruct((length, LANES), f32)
    state_shape = jax.ShapeDtypeStruct((state_size, inner_width), f32)
    scan_flops = 2 * 3 * length * inner_width * (2 * CHUNK + state_size)

    source = layer_input.astype(f32)
    normed_float, norm_pull = jax.vjp(input_norm, source, norm_gain)
    normed = normed_float.astype(bf16)
    state_weight = proj_state.reshape(model_width, 2 * state_local).astype(bf16)
    step_weight = proj_step.astype(bf16)
    step_wide = jnp.pad(step_weight, ((0, 0), (0, LANES - local_heads)))
    out_weight = proj_out.astype(bf16)
    gate_weight = proj_main[:, 0].astype(bf16)
    value_weight = proj_main[:, 1].astype(bf16)
    coef_wide = jnp.pad(head_coef, ((0, 8 - head_coef.shape[0]), (0, LANES - local_heads)))
    skip_wide = rows_of_eight(jnp.repeat(head_coef[2], head_size))
    gain_wide = rows_of_eight(gate_gain)

    state_pre = jnp.dot(normed, state_weight, preferred_element_type=f32)
    value_pre = jnp.dot(normed, value_weight, preferred_element_type=f32)
    step_pre = jnp.dot(normed, step_wide, preferred_element_type=f32)
    gate_pre = jnp.dot(normed, gate_weight, preferred_element_type=f32)
    conv_input = jnp.concatenate([value_pre, state_pre], axis=1)
    rim_rows = from_behind(conv_input[length - tap_count + 1 :], "seq", 1)
    padded = jnp.concatenate([rim_rows, conv_input], axis=0)
    tap_table = jnp.concatenate(
        [conv_main, conv_state.reshape(tap_count + 1, 2 * state_local)], axis=1
    )
    activated, conv_pull = jax.vjp(convolve, padded, tap_table)
    values = activated[:, :inner_width]
    pair_lanes = ring_gather(activated[:, inner_width:].T, "head")
    pair_lanes = pair_lanes.reshape(head_count, 2, state_local, length)
    input_lanes = pair_lanes[:, 0].reshape(state_size, length)
    output_lanes = pair_lanes[:, 1].reshape(state_size, length)

    steps, steps_wide, cum_wide, cum_lanes, states, before, after = run(
        functools.partial(states_kernel, head_size),
        (1,),
        [full(a.shape) for a in (values, input_lanes, step_pre, coef_wide)],
        [
            full((length, LANES)),
            full((length, inner_width)),
            full((length, inner_width)),
            full((HEAD_ROWS, length)),
            full((chunks + 1, state_size, inner_width)),
            full((chunks + 1, 8, inner_width)),
            full((chunks, 8, inner_width)),
        ],
        [
            small_shape,
            row_shape,
            row_shape,
            jax.ShapeDtypeStruct((HEAD_ROWS, length), f32),
            jax.ShapeDtypeStruct((chunks + 1, state_size, inner_width), f32),
            jax.ShapeDtypeStruct((chunks + 1, 8, inner_width), f32),
            jax.ShapeDtypeStruct((chunks, 8, inner_width), f32),
        ],
        (values, input_lanes, step_pre, coef_wide),
        flops=scan_flops // 3,
    )
    through = before[chunks, 0:1]
    start_state = carried_state(through, states[chunks], "seq", False)
    local_out = run(
        functools.partial(within_kernel, head_size),
        (chunks,),
        [chunk_row, chunk_lane, chunk_lane, chunk_row, chunk_row, chunk_head, state_block],
        [chunk_row],
        [row_shape],
        (values, input_lanes, output_lanes, steps_wide, cum_wide, cum_lanes, states),
        flops=scan_flops,
    )[0]
    back_normal = contract(output_grad, out_weight, 1, 1)
    mixed, sums = run(
        gate_kernel,
        (chunks,),
        [
            chunk_row, chunk_lane, chunk_row, row_block, state_full, chunk_row, row_full,
            chunk_row, chunk_row, row_full,
        ],
        [chunk_row, pl.BlockSpec((16, CHUNK), lambda i: (0, i))],
        [row_shape, jax.ShapeDtypeStruct((16, length), f32)],
        (
            local_out, output_lanes, cum_wide, before, start_state, values, skip_wide,
            gate_pre, back_normal, gain_wide,
        ),
        flops=scan_flops // 4,
    )
    sums = sum_all(sums, "head")
    reverse_row = pl.BlockSpec((CHUNK, inner_width), lambda i: (chunks - 1 - i, 0))
    reverse_lane = pl.BlockSpec((state_size, CHUNK), lambda i: (0, chunks - 1 - i))
    normal_out, back_mixed, back_gate, grad_gate, grad_skip, later_local, state_jump = run(
        functools.partial(turn_kernel, float(full_inner)),
        (chunks,),
        [
            pl.BlockSpec((16, CHUNK), lambda i: (0, chunks - 1 - i)),
            reverse_row, reverse_row, reverse_row, row_full, reverse_row, reverse_row,
            reverse_lane, row_full,
        ],
        [
            reverse_row, reverse_row, reverse_row, row_full, row_full,
            pl.BlockSpec((1, state_size, inner_width), lambda i: (chunks - 1 - i, 0, 0)),
            state_full,
        ],
        [
            jax.ShapeDtypeStruct((length, inner_width), bf16),
            row_shape,
            jax.ShapeDtypeStruct((length, inner_width), bf16),
            jax.ShapeDtypeStruct((8, inner_width), f32),
            jax.ShapeDtypeStruct((8, inner_width), f32),
            jax.ShapeDtypeStruct((chunks, state_size, inner_width), f32),
            state_shape,
        ],
        (
            sums, mixed, gate_pre, back_normal, gain_wide, values, cum_wide, output_lanes,
            skip_wide,
        ),
        scratch=[pltpu.VMEM((state_size, inner_width), f32)],
        flops=scan_flops // 4,
    )
    later_grad = carried_state(through, state_jump, "seq", True)

    sum_gate_half = scatter_rows(contract(normed, back_gate, 0, 0), "seq")
    sum_out_turned = scatter_rows(contract(output_grad, normal_out, 0, 0), "seq")
    col_count = model_width // head_count

    def out_block(index):
        columns = lax.dynamic_slice_in_dim(out_weight, index * col_count, col_count, 1)
        return jnp.dot(normal_out, columns, preferred_element_type=f32)

    out_cols = line_scatter(out_block, "head")
    residual_cols = lax.dynamic_slice_in_dim(source, head_index * col_count, col_count, 1)
    layer_output = (residual_cols + out_cols).astype(bf16)

    z_local, db_local, dc_local = run(
        functools.partial(back_within_kernel, head_size),
        (chunks,),
        [
            chunk_row, chunk_lane, chunk_lane, chunk_row, chunk_row, chunk_head, state_block,
            row_block, state_full, chunk_row, state_block,
        ],
        [chunk_row, chunk_state, chunk_state],
        [
            row_shape,
            jax.ShapeDtypeStruct((length, state_size), f32),
            jax.ShapeDtypeStruct((length, state_size), f32),
        ],
        (
            values, input_lanes, output_lanes, steps_wide, cum_wide, cum_lanes, states, before,
            start_state, back_mixed, later_local,
        ),
        flops=2 * scan_flops,
    )
    back_values, back_in, back_out, back_step_pre, grad_coef_rows = run(
        functools.partial(back_steps_kernel, head_size),
        (chunks,),
        [
            chunk_row, chunk_lane, chunk_row, chunk_row, chunk_small, chunk_small,
            full(coef_wide.shape), row_full, chunk_row, chunk_row, chunk_row, chunk_state,
            chunk_state, state_block, state_full, row_block, next_state, next_row, state_full,
        ],
        [chunk_row, chunk_lane, chunk_lane, chunk_small, full((16, LANES))],
        [
            row_shape,
            jax.ShapeDtypeStruct((state_size, length), f32),
            jax.ShapeDtypeStruct((state_size, length), f32),
            small_shape,
            jax.ShapeDtypeStruct((16, LANES), f32),
        ],
        (
            values, input_lanes, steps_wide, cum_wide, steps, step_pre, coef_wide, skip_wide,
            mixed, back_mixed, z_local, db_local, dc_local, later_local, later_grad, after, states,
            before, start_state,
        ),
        flops=scan_flops // 2,
    )
    grad_coef = jnp.stack(
        [
            grad_coef_rows[0, :local_heads],
            grad_coef_rows[8, :local_heads],
            jnp.sum(grad_skip[0].reshape(local_heads, head_size), axis=1),
        ]
    )
    back_pair = jnp.stack([back_in, back_out]).reshape(2, head_count, state_local, length)

    def pair_block(index):
        return lax.dynamic_index_in_dim(back_pair, index, 1, False)

    back_local_pair = pair_block(head_index)
    for by in range(1, head_count):
        back_local_pair = back_local_pair + shift(
            pair_block(lax.rem(head_index + by, head_count)), "head", by
        )
    back_active = jnp.concatenate(
        [back_values, back_local_pair.reshape(2 * state_local, length).T], axis=1
    )
    back_padded, grad_taps = conv_pull(back_active)
    rim_back = from_behind(back_padded[: tap_count - 1], "seq", -1)
    back_conv = back_padded[tap_count - 1 :]
    rim_start = length - tap_count + 1
    back_conv = jnp.concatenate([back_conv[:rim_start], back_conv[rim_start:] + rim_back], axis=0)
    back_late = jnp.concatenate([back_conv, back_step_pre[:, :local_heads]], axis=1).astype(bf16)
    late_weight = jnp.concatenate([value_weight, state_weight, step_weight], axis=1)
    shard_rows = length // head_count

    def normed_block(index):
        gate_rows = lax.dynamic_slice_in_dim(back_gate, index * shard_rows, shard_rows, 0)
        late_rows = lax.dynamic_slice_in_dim(back_late, index * shard_rows, shard_rows, 0)
        return contract(gate_rows, gate_weight, 1, 1) + contract(late_rows, late_weight, 1, 1)

    back_normed = line_scatter(normed_block, "head")
    own_source = lax.dynamic_slice_in_dim(source, head_index * shard_rows, shard_rows, 0)
    _, norm_pull = jax.vjp(input_norm, own_source, norm_gain)
    back_source, grad_gain = norm_pull(back_normed)
    back_rows = line_gather(back_source, "head").reshape(length, model_width)
    input_grad = (output_grad.astype(f32) + back_rows).astype(bf16)

    late = contract(normed, back_late, 0, 0)
    sum_late = scatter_rows(late, "seq")

    def own_rows(array, along):
        piece_len = array.shape[along] // seq_count
        return lax.dynamic_slice_in_dim(array, seq_index * piece_len, piece_len, along)

    part_out, sum_out, first_out, second_out = adam_turned(
        sum_out_turned, own_rows(proj_out, 1), first_proj_out, second_proj_out
    )
    new_out = turned(gather_rows(part_out, "seq"))

    sum_main = jnp.stack([sum_gate_half, sum_late[:, :inner_width]], axis=1)
    part_main, first_main, second_main = adam_update(
        own_rows(proj_main, 0), sum_main, first_proj_main, second_proj_main, rate_matrix
    )
    new_main = gather_rows(part_main, "seq")
    sum_state = sum_late[:, inner_width : inner_width + 2 * state_local]
    part_state, first_state, second_state = adam_update(
        own_rows(proj_state, 0).reshape(-1, 2 * state_local),
        sum_state,
        first_proj_state.reshape(-1, 2 * state_local),
        second_proj_state.reshape(-1, 2 * state_local),
        rate_matrix,
    )
    sum_step = sum_late[:, inner_width + 2 * state_local :]
    part_step, first_step, second_step = adam_update(
        own_rows(proj_step, 0), sum_step, first_proj_step, second_proj_step, rate_matrix
    )
    new_small = gather_small(jnp.concatenate([part_state, part_step], axis=1), "seq")
    new_state = new_small[:, : 2 * state_local].reshape(model_width, 2, state_local)
    new_step = new_small[:, 2 * state_local :]
    state_form = (-1, 2, state_local)

    taps_wide = inner_width + 2 * state_local
    gain_rows = grad_gain.reshape(8, model_width // 8)
    small = jnp.concatenate(
        [
            grad_taps.reshape(-1),
            grad_gate[0],
            grad_coef.reshape(-1),
        ]
    )
    small_size = small.shape[0]
    padded_size = -(-small_size // 1024) * 1024
    small = jnp.pad(small, (0, padded_size - small_size)).reshape(8, padded_size // 8)
    small = sum_all(jnp.concatenate([small, sum_all(gain_rows, "head")], axis=1), "seq")
    sum_gain = small[:, padded_size // 8 :].reshape(-1)
    small = small[:, : padded_size // 8].reshape(-1)
    taps_size = (tap_count + 1) * taps_wide
    sum_taps = small[:taps_size].reshape(tap_count + 1, taps_wide)
    sum_cmain = sum_taps[:, :inner_width]
    sum_cstate = sum_taps[:, inner_width:].reshape(tap_count + 1, 2, state_local)
    sum_gate = small[taps_size : taps_size + inner_width]
    sum_coef = small[taps_size + inner_width : small_size].reshape(3, local_heads)
    new_gain, first_gain, second_gain = adam_update(
        norm_gain, sum_gain, first_norm_gain, second_norm_gain, rate_vector
    )
    new_cmain, first_cmain, second_cmain = adam_update(
        conv_main, sum_cmain, first_conv_main, second_conv_main, rate_vector
    )
    new_cstate, first_cstate, second_cstate = adam_update(
        conv_state, sum_cstate, first_conv_state, second_conv_state, rate_vector
    )
    new_coef, first_coef, second_coef = adam_update(
        head_coef, sum_coef, first_head_coef, second_head_coef, rate_coef
    )
    new_gate, first_gate, second_gate = adam_update(
        gate_gain, sum_gate, first_gate_gain, second_gate_gain, rate_vector
    )
    return (
        layer_output, input_grad, sum_gain, sum_main, sum_state.reshape(state_form), sum_step,
        sum_cmain, sum_cstate, sum_coef, sum_gate, sum_out, new_gain, new_main, new_state,
        new_step, new_cmain, new_cstate, new_coef, new_gate, new_out, first_gain, first_main,
        first_state.reshape(state_form), first_step, first_cmain, first_cstate, first_coef,
        first_gate, first_out, second_gain, second_main, second_state.reshape(state_form),
        second_step, second_cmain, second_cstate, second_coef, second_gate, second_out,
    )


def solution(mesh):
    return jax.shard_map(
        per_device,
        mesh=mesh,
        in_specs=(
            P("seq", None),
            P("seq", None),
            P(),
            P(None, None, "head"),
            P(None, None, "head"),
            P(None, "head"),
            P(None, "head"),
            P(None, None, "head"),
            P(None, "head"),
            P("head"),
            P("head", None),
            P(),
            P("seq", None, "head"),
            P("seq", None, "head"),
            P("seq", "head"),
            P(None, "head"),
            P(None, None, "head"),
            P(None, "head"),
            P("head"),
            P("head", "seq"),
            P(),
            P("seq", None, "head"),
            P("seq", None, "head"),
            P("seq", "head"),
            P(None, "head"),
            P(None, None, "head"),
            P(None, "head"),
            P("head"),
            P("head", "seq"),
        ),
        out_specs=(
            P("seq", "head"),
            P("seq", None),
            P(),
            P("seq", None, "head"),
            P("seq", None, "head"),
            P("seq", "head"),
            P(None, "head"),
            P(None, None, "head"),
            P(None, "head"),
            P("head"),
            P("head", "seq"),
            P(),
            P(None, None, "head"),
            P(None, None, "head"),
            P(None, "head"),
            P(None, "head"),
            P(None, None, "head"),
            P(None, "head"),
            P("head"),
            P("head", None),
            P(),
            P("seq", None, "head"),
            P("seq", None, "head"),
            P("seq", "head"),
            P(None, "head"),
            P(None, None, "head"),
            P(None, "head"),
            P("head"),
            P("head", "seq"),
            P(),
            P("seq", None, "head"),
            P("seq", None, "head"),
            P("seq", "head"),
            P(None, "head"),
            P(None, None, "head"),
            P(None, "head"),
            P("head"),
            P("head", "seq"),
        ),
        check_vma=False,
    )
```

```python
import functools

import jax
import jax.numpy as jnp
from jax import lax
from jax.experimental import pallas as pl
from jax.experimental.pallas import tpu as pltpu
from jax.sharding import PartitionSpec as P


CHUNK = 128
LANES = 128
HEAD_ROWS = 16

norm_epsilon = 1e-05
beta_first = 0.9
beta_second = 0.95
adam_epsilon = 1e-08
weight_decay = 0.1
adam_step = 2
rate_matrix = 0.005
rate_vector = 0.15
rate_coef = 0.6

NN = ((1,), (0,))
NT = ((1,), (1,))


def swap(value, axis, bit):
    return lax.ppermute(value, axis, [(i, i ^ bit) for i in range(lax.axis_size(axis))])


def shift(value, axis, by):
    count = lax.axis_size(axis)
    return lax.ppermute(value, axis, [(i, (i + by) % count) for i in range(count)])


def from_behind(value, axis, by):
    devices = lax.axis_size(axis)
    pairs = [(i, i + by) for i in range(devices) if 0 <= i + by < devices]
    return lax.ppermute(value, axis, pairs)


def bits_of(axis):
    count, bits = lax.axis_size(axis), []
    while 2 ** len(bits) < count:
        bits.append(2 ** len(bits))
    return bits


def sum_all(value, axis):
    for bit in bits_of(axis):
        value = value + swap(value, axis, bit)
    return value


def bit_of(axis, bit):
    return (lax.axis_index(axis) // bit) % 2


def scatter_rows(value, axis):
    return lax.psum_scatter(value, axis, scatter_dimension=0, tiled=True)


def scatter_relative(keep, send, axis):
    bits = bits_of(axis)
    rows = keep.shape[1]
    got = swap(send, axis, bits[0])
    dims = (2,) * (len(bits) - 1)
    keep = keep.reshape(dims + keep.shape[1:])
    got = got.reshape(dims + got.shape[1:])
    cuts = [(0, rows // 2), (rows // 2, rows)]
    orders = [bits[1:], bits[1:][::-1]]
    pieces = []
    for (low, high), order in zip(cuts, orders):
        left = list(bits[1:])
        mine = [lax.slice_in_dim(a, low, high, axis=len(dims)) for a in (keep, got)]
        for bit in order:
            dim = len(left) - 1 - left.index(bit)
            sent = sum_of([lax.index_in_dim(a, 1, dim, False) for a in mine])
            held = [lax.index_in_dim(a, 0, dim, False) for a in mine]
            mine = [sum_of(held), swap(sent, axis, bit)]
            left.remove(bit)
        pieces.append(sum_of(mine))
    return jnp.concatenate(pieces, axis=0)


def sum_of(parts):
    return functools.reduce(jnp.add, parts)


def gather_rows(value, axis):
    return lax.all_gather(value, axis, axis=0, tiled=True)


def gather_small(value, axis):
    place = lax.axis_index(axis)
    rows = value.shape[0]
    whole = jnp.zeros((lax.axis_size(axis) * rows,) + value.shape[1:], value.dtype)
    whole = lax.dynamic_update_slice_in_dim(whole, value, place * rows, 0)
    for bit in bits_of(axis):
        base = (place // bit) * bit
        block = lax.dynamic_slice_in_dim(whole, base * rows, bit * rows, 0)
        other = swap(block, axis, bit)
        start = jnp.where(bit_of(axis, bit) == 0, base + bit, base - bit)
        whole = lax.dynamic_update_slice_in_dim(whole, other, start * rows, 0)
    return whole


def line_steps(block_of, axis):
    count, place = lax.axis_size(axis), lax.axis_index(axis)
    right = block_of(lax.rem(place + count - 1, count))
    left = block_of(lax.rem(place + 1, count))
    for step in range(1, count):
        got_right = lax.ppermute(right, axis, [(i, i + 1) for i in range(step)])
        got_left = lax.ppermute(
            left, axis, [(count - 1 - i, count - 2 - i) for i in range(step)]
        )
        got_right, got_left = yield (got_right, got_left)
        if step < count - 1:
            right = got_right + block_of(lax.rem(place + count - step - 1, count))
            left = got_left + block_of(lax.rem(place + step + 1, count))
    yield block_of(place) + got_right + got_left


def run_line(steps, got, count, ties=()):
    done = []
    for step in range(1, count):
        if len(done) < len(ties):
            tied = lax.optimization_barrier((ties[len(done)],) + tuple(got))
            done.append(tied[0])
            got = tied[1:]
        got = steps.send(tuple(got))
    return got, done


def line_gather(value, axis):
    count, place = lax.axis_size(axis), lax.axis_index(axis)
    right = left = value
    from_left, from_right = [], []
    for step in range(1, count):
        right = lax.ppermute(right, axis, [(i, i + 1) for i in range(step - 1, count - 1)])
        left = lax.ppermute(left, axis, [(i + 1, i) for i in range(count - step)])
        from_left.append(right)
        from_right.append(left)
    whole = jnp.zeros((count,) + value.shape, value.dtype)
    whole = lax.dynamic_update_index_in_dim(whole, value, place, 0)
    for step in range(1, count):
        block = jnp.where(place >= step, from_left[step - 1], from_right[count - step - 1])
        whole = lax.dynamic_update_index_in_dim(
            whole, block, lax.rem(place + count - step, count), 0
        )
    return whole


def ring_gather(value, axis):
    count, place = lax.axis_size(axis), lax.axis_index(axis)
    whole = jnp.zeros((count,) + value.shape, value.dtype)
    whole = lax.dynamic_update_index_in_dim(whole, value, place, 0)
    for by in range(1, count):
        whole = lax.dynamic_update_index_in_dim(
            whole, shift(value, axis, by), lax.rem(place + count - by, count), 0
        )
    return whole


def carried_state(decay, part, axis, reverse):
    bits = bits_of(axis)
    half = part.shape[0] // 2
    mine = bit_of(axis, bits[0])

    def later_of(bit):
        high = bit_of(axis, bit) == 1
        return jnp.logical_not(high) if reverse else high

    other = swap(part, axis, bits[0])
    other_decay = swap(decay, axis, bits[0])
    own_half = lax.dynamic_slice_in_dim(part, mine * half, half, 0)
    other_half = lax.dynamic_slice_in_dim(other, mine * half, half, 0)
    later = later_of(bits[0])
    total = jnp.where(
        later, own_half + decay * other_half, other_half + other_decay * own_half
    )
    total_decay = decay * other_decay
    before, before_decay = jnp.zeros_like(total), jnp.ones_like(decay)
    for bit in bits[1:]:
        got, got_decay = swap(total, axis, bit), swap(total_decay, axis, bit)
        ahead = later_of(bit)
        before = jnp.where(ahead, before + before_decay * got, before)
        before_decay = jnp.where(ahead, before_decay * got_decay, before_decay)
        if bit != bits[-1]:
            total = jnp.where(ahead, total + total_decay * got, got + got_decay * total)
            total_decay = total_decay * got_decay
    rest = swap(before, axis, bits[0])
    whole = jnp.concatenate(
        [jnp.where(mine == 0, before, rest), jnp.where(mine == 0, rest, before)], axis=0
    )
    return jnp.where(later, other + other_decay * whole, whole)


def dot(left, right, dims):
    return lax.dot_general(left, right, (dims, ((), ())), preferred_element_type=jnp.float32)


def two(value):
    high = value.astype(jnp.bfloat16)
    return high, (value - high.astype(jnp.float32)).astype(jnp.bfloat16)


def three(value):
    high = value.astype(jnp.bfloat16)
    rest = value - high.astype(jnp.float32)
    mid = rest.astype(jnp.bfloat16)
    return high, mid, (rest - mid.astype(jnp.float32)).astype(jnp.bfloat16)


def mul(left, right, dims=NN):
    (lh, ll), (rh, rl) = two(left), two(right)
    return dot(lh, rh, dims) + (dot(lh, rl, dims) + dot(ll, rh, dims))


def mul_mask(mask, value, dims=NN):
    high, mid, low = three(value)
    return dot(mask, high, dims) + (dot(mask, mid, dims) + dot(mask, low, dims))


def mul_by_mask(value, mask, dims=NN):
    high, mid, low = three(value)
    return dot(high, mask, dims) + (dot(mid, mask, dims) + dot(low, mask, dims))


def head_mask(width, head_size):
    row = lax.broadcasted_iota(jnp.int32, (LANES, width), 0)
    col = lax.broadcasted_iota(jnp.int32, (LANES, width), 1)
    low = row * head_size
    return jnp.where((col >= low) & (col < low + head_size), 1.0, 0.0).astype(jnp.bfloat16)


def order_mask(size, upper):
    row = lax.broadcasted_iota(jnp.int32, (size, size), 0)
    col = lax.broadcasted_iota(jnp.int32, (size, size), 1)
    return (row <= col) if upper else (row >= col)


def soft_plus(value):
    return jnp.maximum(value, 0.0) + jnp.log1p(jnp.exp(-jnp.abs(value)))


def sigmoid(value):
    return 1.0 / (1.0 + jnp.exp(-value))


def states_kernel(
    head_size, x_ref, bt_ref, step_ref, coef_ref,
    dt_ref, dtx_ref, cumx_ref, cumt_ref, st_ref, pre_ref, post_ref,
):
    length, width = x_ref.shape
    count = length // CHUNK
    spread = head_mask(width, head_size)
    lower = jnp.where(order_mask(CHUNK, False), 1.0, 0.0).astype(jnp.bfloat16)
    state = jnp.zeros((bt_ref.shape[0], width), jnp.float32)
    run = jnp.zeros((1, width), jnp.float32)
    rate = -jnp.exp(coef_ref[1:2, :])
    bias = coef_ref[0:1, :]
    runs = []
    for c in range(count):
        at = slice(c * CHUNK, (c + 1) * CHUNK)
        steps = soft_plus(step_ref[at, :] + bias)
        cum = mul_mask(lower, rate * steps)
        dtx = mul_by_mask(steps, spread)
        cumx = mul_by_mask(cum, spread)
        dt_ref[at, :] = steps
        dtx_ref[at, :] = dtx
        cumx_ref[at, :] = cumx
        cumt_ref[:, at] = jnp.transpose(cum)[:HEAD_ROWS, :]
        total = cumx[CHUNK - 1 : CHUNK, :]
        st_ref[c] = state
        pre_ref[c] = jnp.broadcast_to(jnp.exp(run), (8, width))
        state = jnp.exp(total) * state + mul(
            bt_ref[:, at], x_ref[at, :] * dtx * jnp.exp(total - cumx)
        )
        run = run + total
        runs.append(total)
    st_ref[count] = state
    pre_ref[count] = jnp.broadcast_to(jnp.exp(run), (8, width))
    rest = jnp.zeros((1, width), jnp.float32)
    for c in range(count - 1, -1, -1):
        post_ref[c] = jnp.broadcast_to(jnp.exp(rest), (8, width))
        rest = rest + runs[c]


def lane_halves(size, width):
    return lax.broadcasted_iota(jnp.int32, (size, width), 1) < width // 2


def within_kernel(head_size, x_ref, bt_ref, ct_ref, dtx_ref, cumx_ref, cumt_ref, st_ref, y_ref):
    width = x_ref.shape[1]
    pair = 2 * head_size
    reads = jnp.transpose(ct_ref[...])
    scores = mul(reads, bt_ref[...])
    mask = order_mask(CHUNK, False)
    first = lane_halves(CHUNK, pair)
    for p in range(width // pair):
        at = slice(p * pair, (p + 1) * pair)
        cumx = cumx_ref[:, at]
        scaled = x_ref[:, at] * dtx_ref[:, at]
        mixing = []
        for h in range(2):
            row = cumt_ref[2 * p + h : 2 * p + h + 1, :]
            col = cumx[:, h * head_size : h * head_size + 1]
            mixing.append(jnp.exp(jnp.where(mask, col - row, -1e30)) * scores)
        stacked = jnp.concatenate(
            [jnp.where(first, scaled, 0.0), jnp.where(first, 0.0, scaled)], axis=0
        )
        inner = mul(jnp.concatenate(mixing, axis=1), stacked)
        y_ref[:, at] = inner + jnp.exp(cumx) * mul(reads, st_ref[0, :, at])


def gate_kernel(
    y_ref, ct_ref, cumx_ref, pre_ref, start_ref, x_ref, skip_ref, gate_ref, back_ref, gain_ref,
    mixed_ref, sums_ref,
):
    width = x_ref.shape[1]
    reads = jnp.transpose(ct_ref[...])
    carried = jnp.exp(cumx_ref[...]) * pre_ref[0, 0:1, :] * mul(reads, start_ref[...])
    mixed = y_ref[...] + carried + skip_ref[0:1, :] * x_ref[...]
    gate = gate_ref[...]
    gated = mixed * (gate * sigmoid(gate))
    mixed_ref[...] = mixed
    ones = jnp.ones((8, width), jnp.bfloat16)
    sums_ref[0:8, :] = mul_mask(ones, gated * gated, NT)
    sums_ref[8:16, :] = mul_mask(ones, back_ref[...] * gain_ref[0:1, :] * gated, NT)


def turn_kernel(
    full_inner, sums_ref, mixed_ref, gate_ref, back_ref, gain_ref, x_ref, cumx_ref, ct_ref,
    skip_ref,
    normal_ref, dy_ref, bgate_ref, ggate_ref, gskip_ref, g_ref, jump_ref, carry_ref,
):
    step = pl.program_id(0)

    @pl.when(step == 0)
    def _():
        carry_ref[...] = jnp.zeros_like(carry_ref)
        ggate_ref[...] = jnp.zeros_like(ggate_ref)
        gskip_ref[...] = jnp.zeros_like(gskip_ref)

    columns = jnp.transpose(sums_ref[...])
    scale = lax.rsqrt(columns[:, 0:1] / full_inner + norm_epsilon)
    inner = columns[:, 8:9] / full_inner
    mixed = mixed_ref[...]
    gate = gate_ref[...]
    share = sigmoid(gate)
    act = gate * share
    gated = mixed * act
    gain = gain_ref[0:1, :]
    back = back_ref[...]
    scaled = gated * scale
    normal_ref[...] = (scaled * gain).astype(jnp.bfloat16)
    back_gated = scale * (back * gain) - gated * (scale * scale * scale) * inner
    dy = back_gated * act
    dy_ref[...] = dy
    bgate_ref[...] = (back_gated * mixed * (share * (1.0 + gate * (1.0 - share)))).astype(
        jnp.bfloat16
    )
    ggate_ref[...] += jnp.broadcast_to(
        jnp.sum(back * scaled, axis=0, keepdims=True), ggate_ref.shape
    )
    gskip_ref[...] += jnp.broadcast_to(
        jnp.sum(dy * x_ref[...], axis=0, keepdims=True), gskip_ref.shape
    )
    carry = carry_ref[...]
    g_ref[0] = carry
    cumx = cumx_ref[...]
    carry = jnp.exp(cumx[CHUNK - 1 : CHUNK, :]) * carry + mul(ct_ref[...], dy * jnp.exp(cumx))
    carry_ref[...] = carry
    jump_ref[...] = carry


def back_within_kernel(
    head_size, x_ref, bt_ref, ct_ref, dtx_ref, cumx_ref, cumt_ref, st_ref, pre_ref, start_ref,
    dy_ref, g_ref,
    z_ref, db_ref, dc_ref,
):
    width = x_ref.shape[1]
    pair = 2 * head_size
    inputs = jnp.transpose(bt_ref[...])
    scores = mul(inputs, ct_ref[...])
    mask = order_mask(CHUNK, True)
    first = lane_halves(CHUNK, pair)
    grad_scores = jnp.zeros((CHUNK, CHUNK), jnp.float32)
    for p in range(width // pair):
        at = slice(p * pair, (p + 1) * pair)
        cumx = cumx_ref[:, at]
        dy = dy_ref[:, at]
        scaled = x_ref[:, at] * dtx_ref[:, at]
        products = mul(
            jnp.concatenate(
                [jnp.where(first, scaled, 0.0), jnp.where(first, 0.0, scaled)], axis=0
            ),
            dy,
            NT,
        )
        mixing = []
        for h in range(2):
            row = cumt_ref[2 * p + h : 2 * p + h + 1, :]
            col = cumx[:, h * head_size : h * head_size + 1]
            decay = jnp.exp(jnp.where(mask, row - col, -1e30))
            grad_scores = grad_scores + decay * products[h * CHUNK : (h + 1) * CHUNK, :]
            mixing.append(decay * scores)
        stacked = jnp.concatenate([jnp.where(first, dy, 0.0), jnp.where(first, 0.0, dy)], axis=0)
        inner = mul(jnp.concatenate(mixing, axis=1), stacked)
        decay_out = jnp.exp(cumx[CHUNK - 1 : CHUNK, :] - cumx)
        z_ref[:, at] = inner + decay_out * mul(inputs, g_ref[0, :, at])
    cumx = cumx_ref[...]
    scaled = x_ref[...] * dtx_ref[...] * jnp.exp(cumx[CHUNK - 1 : CHUNK, :] - cumx)
    entering = st_ref[0] + pre_ref[0, 0:1, :] * start_ref[...]
    reads = jnp.transpose(ct_ref[...])
    db_ref[...] = mul(grad_scores, reads) + mul(scaled, g_ref[0], NT)
    dc_ref[...] = mul(jnp.transpose(grad_scores), inputs) + mul(
        dy_ref[...] * jnp.exp(cumx), entering, NT
    )


def back_steps_kernel(
    head_size, x_ref, bt_ref, dtx_ref, cumx_ref, dt_ref, step_ref, coef_ref, skip_ref, mixed_ref,
    dy_ref, z_ref, db_ref, dc_ref, g_ref, later_ref, post_ref, end_ref, pre_ref, start_ref,
    dx_ref, dbt_ref, dct_ref, dstep_ref, gcoef_ref,
):
    width = x_ref.shape[1]

    @pl.when(pl.program_id(0) == 0)
    def _():
        gcoef_ref[...] = jnp.zeros_like(gcoef_ref)

    spread = head_mask(width, head_size)
    upper = jnp.where(order_mask(CHUNK, True), 1.0, 0.0).astype(jnp.bfloat16)
    x = x_ref[...]
    dy = dy_ref[...]
    cumx = cumx_ref[...]
    skip = skip_ref[0:1, :]
    dtx = dtx_ref[...]
    later = later_ref[...]
    post = post_ref[0, 0:1, :]
    inputs = jnp.transpose(bt_ref[...])
    decay_out = post * jnp.exp(cumx[CHUNK - 1 : CHUNK, :] - cumx)
    z = z_ref[...] + decay_out * mul(inputs, later)
    dx_ref[...] = dtx * z + skip * dy
    db = db_ref[...] + mul(x * dtx * decay_out, later, NT)
    dbt_ref[...] = jnp.transpose(db)
    dct_ref[...] = jnp.transpose(dc_ref[...])
    steps = dt_ref[...]
    by_step = mul_by_mask(x * z, spread, NT)
    by_out = mul_by_mask(dy * (mixed_ref[...] - skip * x), spread, NT)
    leaving = end_ref[0] + pre_ref[0, 0:1, :] * start_ref[...]
    held = jnp.sum((g_ref[0] + post * later) * leaving, axis=0, keepdims=True)
    held = mul_by_mask(jnp.broadcast_to(held, (8, width)), spread, NT)[0:1, :]
    by_decay = mul_mask(upper, by_out - steps * by_step) + held
    rate = -jnp.exp(coef_ref[1:2, :])
    back = (by_step + rate * by_decay) * sigmoid(step_ref[...] + coef_ref[0:1, :])
    dstep_ref[...] = back
    gcoef_ref[0:8, :] += jnp.broadcast_to(jnp.sum(back, axis=0, keepdims=True), (8, LANES))
    gcoef_ref[8:16, :] += jnp.broadcast_to(
        jnp.sum(by_decay * rate * steps, axis=0, keepdims=True), (8, LANES)
    )


def full(array_shape):
    zeros = (0,) * len(array_shape)
    return pl.BlockSpec(array_shape, lambda i: zeros)


def run(kernel, grid, in_specs, out_specs, out_shapes, args, scratch=(), flops=0):
    moved = sum(a.size * a.dtype.itemsize for a in args) + sum(
        s.size * s.dtype.itemsize for s in out_shapes
    )
    return pl.pallas_call(
        kernel,
        grid=grid,
        in_specs=in_specs,
        out_specs=out_specs,
        out_shape=out_shapes,
        scratch_shapes=scratch,
        cost_estimate=pl.CostEstimate(flops=flops, bytes_accessed=moved, transcendentals=0),
        compiler_params=pltpu.CompilerParams(
            dimension_semantics=("arbitrary",) * len(grid), vmem_limit_bytes=48 * 2**20
        ),
    )(*args)


def contract(left, right, left_dim, right_dim):
    return lax.dot_general(
        left, right, (((left_dim,), (right_dim,)), ((), ())), preferred_element_type=jnp.float32
    )


def input_norm(source, gain):
    return (
        source * lax.rsqrt(jnp.mean(source * source, axis=1, keepdims=True) + norm_epsilon) * gain
    )


def convolve(padded, tap_table):
    tap_count = tap_table.shape[0] - 1
    length = padded.shape[0] - tap_count + 1
    total = jnp.broadcast_to(tap_table[tap_count], (length, tap_table.shape[1]))
    for offset in range(tap_count):
        total = total + tap_table[offset] * padded[offset : offset + length]
    return jax.nn.silu(total)


def adam_update(weight, gradient, moment_one, moment_two, step_rate):
    first_new = beta_first * moment_one + (1.0 - beta_first) * gradient
    second_new = beta_second * moment_two + (1.0 - beta_second) * gradient * gradient
    first_hat = first_new / (1.0 - beta_first**adam_step)
    second_hat = second_new / (1.0 - beta_second**adam_step)
    updated = weight - step_rate * (
        first_hat / (jnp.sqrt(second_hat) + adam_epsilon) + weight_decay * weight
    )
    return (updated, first_new, second_new)


def early_kernel(normed_ref, back_ref, grad_ref, normal_ref, out_ref):
    width = back_ref.shape[1]
    out_ref[:, :width] = dot(jnp.transpose(normed_ref[...]), back_ref[...], NN)
    out_ref[:, width:] = dot(jnp.transpose(grad_ref[...]), normal_ref[...], NN)


def early_gradients(normed, back_gate, output_grad, normal_out):
    length, rows = normed.shape
    width = back_gate.shape[1]
    block = 2 * CHUNK
    columns = pl.BlockSpec((length, block), lambda i: (0, i))
    return run(
        early_kernel,
        (rows // block,),
        [columns, full((length, width)), columns, full((length, width))],
        [pl.BlockSpec((block, 2 * width), lambda i: (i, 0))],
        [jax.ShapeDtypeStruct((rows, 2 * width), jnp.float32)],
        (normed, back_gate, output_grad, normal_out),
        flops=4 * length * rows * width,
    )[0]


def late_kernel(place_ref, normed_ref, back_ref, keep_ref, send_ref):
    product = dot(normed_ref[...], back_ref[...], NN)
    odd = lax.rem(pl.program_id(0), 2) == 1

    @pl.when(odd)
    def _():
        send_ref[0] = product

    @pl.when(jnp.logical_not(odd))
    def _():
        keep_ref[0] = product


def late_gradients(place, count, normed_lanes, back_late):
    rows, length = normed_lanes.shape
    width = back_late.shape[1]
    block = rows // count
    half = jax.ShapeDtypeStruct((count // 2, block, width), jnp.float32)
    half_spec = pl.BlockSpec((1, block, width), lambda i, place_ref: (i // 2, 0, 0))
    return pl.pallas_call(
        late_kernel,
        grid_spec=pltpu.PrefetchScalarGridSpec(
            num_scalar_prefetch=1,
            grid=(count,),
            in_specs=[
                pl.BlockSpec((block, length), lambda i, place_ref: (place_ref[0] ^ i, 0)),
                pl.BlockSpec((length, width), lambda i, place_ref: (0, 0)),
            ],
            out_specs=[half_spec, half_spec],
        ),
        out_shape=[half, half],
        cost_estimate=pl.CostEstimate(
            flops=2 * rows * length * width,
            bytes_accessed=4 * rows * width + 2 * length * (rows + width),
            transcendentals=0,
        ),
        compiler_params=pltpu.CompilerParams(
            dimension_semantics=("arbitrary",), vmem_limit_bytes=48 * 2**20
        ),
    )(jnp.full((1,), place, jnp.int32), normed_lanes, back_late)


def adam_turned_kernel(grad_ref, weight_ref, one_ref, two_ref, part_ref, sum_ref, first_ref, second_ref):
    gradient = jnp.transpose(grad_ref[...])
    updated, first_new, second_new = adam_update(
        weight_ref[...], gradient, one_ref[...], two_ref[...], rate_matrix
    )
    part_ref[...] = jnp.transpose(updated)
    sum_ref[...] = gradient
    first_ref[...] = first_new
    second_ref[...] = second_new


def adam_turned(gradient, weight, moment_one, moment_two):
    rows, columns = weight.shape
    whole = [full((rows, columns))] * 3
    shape = jax.ShapeDtypeStruct((rows, columns), jnp.float32)
    return run(
        adam_turned_kernel,
        (1,),
        [full((columns, rows))] + whole,
        [full((columns, rows))] + whole,
        [jax.ShapeDtypeStruct((columns, rows), jnp.float32)] + [shape] * 3,
        (gradient, weight, moment_one, moment_two),
    )


def turn_block_kernel(in_ref, out_ref):
    out_ref[...] = jnp.transpose(in_ref[...])


def turned(array):
    rows, columns = array.shape
    block = 2 * CHUNK
    return run(
        turn_block_kernel,
        (rows // block,),
        [pl.BlockSpec((block, columns), lambda i: (i, 0))],
        [pl.BlockSpec((columns, block), lambda i: (0, i))],
        [jax.ShapeDtypeStruct((columns, rows), array.dtype)],
        (array,),
    )[0]


def rows_of_eight(vector):
    return jnp.broadcast_to(vector[None, :], (8, vector.shape[0]))


def per_device(
    layer_input, output_grad, norm_gain, proj_main, proj_state, proj_step, conv_main, conv_state,
    head_coef, gate_gain, proj_out, first_norm_gain, first_proj_main, first_proj_state,
    first_proj_step, first_conv_main, first_conv_state, first_head_coef, first_gate_gain,
    first_proj_out, second_norm_gain, second_proj_main, second_proj_state, second_proj_step,
    second_conv_main, second_conv_state, second_head_coef, second_gate_gain, second_proj_out,
):
    f32, bf16 = jnp.float32, jnp.bfloat16
    length, model_width = layer_input.shape
    local_heads = proj_step.shape[1]
    inner_width = proj_main.shape[2]
    head_size = inner_width // local_heads
    state_local = proj_state.shape[2]
    tap_count = conv_main.shape[0] - 1
    head_count = lax.axis_size("head")
    seq_count = lax.axis_size("seq")
    seq_index = lax.axis_index("seq")
    head_index = lax.axis_index("head")
    state_size = state_local * head_count
    full_inner = inner_width * head_count
    chunks = length // CHUNK
    chunk_row = pl.BlockSpec((CHUNK, inner_width), lambda i: (i, 0))
    chunk_lane = pl.BlockSpec((state_size, CHUNK), lambda i: (0, i))
    chunk_head = pl.BlockSpec((HEAD_ROWS, CHUNK), lambda i: (0, i))
    chunk_small = pl.BlockSpec((CHUNK, LANES), lambda i: (i, 0))
    chunk_state = pl.BlockSpec((CHUNK, state_size), lambda i: (i, 0))
    state_block = pl.BlockSpec((1, state_size, inner_width), lambda i: (i, 0, 0))
    next_state = pl.BlockSpec((1, state_size, inner_width), lambda i: (i + 1, 0, 0))
    row_block = pl.BlockSpec((1, 8, inner_width), lambda i: (i, 0, 0))
    next_row = pl.BlockSpec((1, 8, inner_width), lambda i: (i + 1, 0, 0))
    state_full = full((state_size, inner_width))
    row_full = full((8, inner_width))
    row_shape = jax.ShapeDtypeStruct((length, inner_width), f32)
    small_shape = jax.ShapeDtypeStruct((length, LANES), f32)
    state_shape = jax.ShapeDtypeStruct((state_size, inner_width), f32)
    scan_flops = 2 * 3 * length * inner_width * (2 * CHUNK + state_size)

    halo = 16
    rim = halo - (tap_count - 1)
    source = layer_input.astype(f32)
    rim_source = from_behind(source[length - halo :], "seq", 1)
    normed = input_norm(source, norm_gain).astype(bf16)
    normed_long = jnp.concatenate([input_norm(rim_source, norm_gain).astype(bf16), normed], axis=0)
    state_weight = proj_state.reshape(model_width, 2 * state_local).astype(bf16)
    step_weight = proj_step.astype(bf16)
    step_wide = jnp.pad(step_weight, ((0, 0), (0, LANES - local_heads)))
    out_weight = proj_out.astype(bf16)
    gate_weight = proj_main[:, 0].astype(bf16)
    value_weight = proj_main[:, 1].astype(bf16)
    coef_wide = jnp.pad(head_coef, ((0, 8 - head_coef.shape[0]), (0, LANES - local_heads)))
    skip_wide = rows_of_eight(jnp.repeat(head_coef[2], head_size))
    gain_wide = rows_of_eight(gate_gain)

    state_pre = jnp.dot(normed_long, state_weight, preferred_element_type=f32)
    state_taps = conv_state.reshape(tap_count + 1, 2 * state_local)
    state_active, state_pull = jax.vjp(convolve, state_pre[rim:], state_taps)
    pair_lanes = ring_gather(state_active.T, "head")
    value_pre = jnp.dot(normed_long, value_weight, preferred_element_type=f32)
    values, value_pull = jax.vjp(convolve, value_pre[rim:], conv_main)
    step_pre = jnp.dot(normed, step_wide, preferred_element_type=f32)
    gate_pre = jnp.dot(normed, gate_weight, preferred_element_type=f32)
    pair_lanes = pair_lanes.reshape(head_count, 2, state_local, length)
    input_lanes = pair_lanes[:, 0].reshape(state_size, length)
    output_lanes = pair_lanes[:, 1].reshape(state_size, length)

    steps, steps_wide, cum_wide, cum_lanes, states, before, after = run(
        functools.partial(states_kernel, head_size),
        (1,),
        [full(a.shape) for a in (values, input_lanes, step_pre, coef_wide)],
        [
            full((length, LANES)),
            full((length, inner_width)),
            full((length, inner_width)),
            full((HEAD_ROWS, length)),
            full((chunks + 1, state_size, inner_width)),
            full((chunks + 1, 8, inner_width)),
            full((chunks, 8, inner_width)),
        ],
        [
            small_shape,
            row_shape,
            row_shape,
            jax.ShapeDtypeStruct((HEAD_ROWS, length), f32),
            jax.ShapeDtypeStruct((chunks + 1, state_size, inner_width), f32),
            jax.ShapeDtypeStruct((chunks + 1, 8, inner_width), f32),
            jax.ShapeDtypeStruct((chunks, 8, inner_width), f32),
        ],
        (values, input_lanes, step_pre, coef_wide),
        flops=scan_flops // 3,
    )
    through = before[chunks, 0:1]
    start_state = carried_state(through, states[chunks], "seq", False)
    local_out = run(
        functools.partial(within_kernel, head_size),
        (chunks,),
        [chunk_row, chunk_lane, chunk_lane, chunk_row, chunk_row, chunk_head, state_block],
        [chunk_row],
        [row_shape],
        (values, input_lanes, output_lanes, steps_wide, cum_wide, cum_lanes, states),
        flops=scan_flops,
    )[0]
    back_normal = contract(output_grad, out_weight, 1, 1)
    mixed, sums = run(
        gate_kernel,
        (chunks,),
        [
            chunk_row, chunk_lane, chunk_row, row_block, state_full, chunk_row, row_full,
            chunk_row, chunk_row, row_full,
        ],
        [chunk_row, pl.BlockSpec((16, CHUNK), lambda i: (0, i))],
        [row_shape, jax.ShapeDtypeStruct((16, length), f32)],
        (
            local_out, output_lanes, cum_wide, before, start_state, values, skip_wide,
            gate_pre, back_normal, gain_wide,
        ),
        flops=scan_flops // 4,
    )
    sums = sum_all(sums, "head")
    reverse_row = pl.BlockSpec((CHUNK, inner_width), lambda i: (chunks - 1 - i, 0))
    reverse_lane = pl.BlockSpec((state_size, CHUNK), lambda i: (0, chunks - 1 - i))
    normal_out, back_mixed, back_gate, grad_gate, grad_skip, later_local, state_jump = run(
        functools.partial(turn_kernel, float(full_inner)),
        (chunks,),
        [
            pl.BlockSpec((16, CHUNK), lambda i: (0, chunks - 1 - i)),
            reverse_row, reverse_row, reverse_row, row_full, reverse_row, reverse_row,
            reverse_lane, row_full,
        ],
        [
            reverse_row, reverse_row, reverse_row, row_full, row_full,
            pl.BlockSpec((1, state_size, inner_width), lambda i: (chunks - 1 - i, 0, 0)),
            state_full,
        ],
        [
            jax.ShapeDtypeStruct((length, inner_width), bf16),
            row_shape,
            jax.ShapeDtypeStruct((length, inner_width), bf16),
            jax.ShapeDtypeStruct((8, inner_width), f32),
            jax.ShapeDtypeStruct((8, inner_width), f32),
            jax.ShapeDtypeStruct((chunks, state_size, inner_width), f32),
            state_shape,
        ],
        (
            sums, mixed, gate_pre, back_normal, gain_wide, values, cum_wide, output_lanes,
            skip_wide,
        ),
        scratch=[pltpu.VMEM((state_size, inner_width), f32)],
        flops=scan_flops // 4,
    )
    later_grad = carried_state(through, state_jump, "seq", True)

    sum_early = scatter_rows(early_gradients(normed, back_gate, output_grad, normal_out), "seq")
    col_count = model_width // head_count

    def out_block(index):
        columns = lax.dynamic_slice_in_dim(out_weight, index * col_count, col_count, 1)
        return jnp.dot(normal_out, columns, preferred_element_type=f32)

    out_steps = line_steps(out_block, "head")
    out_got = next(out_steps)
    tied = lax.optimization_barrier((back_mixed,) + tuple(out_got))
    back_tied, out_got = tied[0], out_steps.send(tuple(tied[1:]))
    z_local, db_local, dc_local = run(
        functools.partial(back_within_kernel, head_size),
        (chunks,),
        [
            chunk_row, chunk_lane, chunk_lane, chunk_row, chunk_row, chunk_head, state_block,
            row_block, state_full, chunk_row, state_block,
        ],
        [chunk_row, chunk_state, chunk_state],
        [
            row_shape,
            jax.ShapeDtypeStruct((length, state_size), f32),
            jax.ShapeDtypeStruct((length, state_size), f32),
        ],
        (
            values, input_lanes, output_lanes, steps_wide, cum_wide, cum_lanes, states, before,
            start_state, back_tied, later_local,
        ),
        flops=2 * scan_flops,
    )
    tied = lax.optimization_barrier((z_local,) + tuple(out_got))
    z_local, out_got = tied[0], out_steps.send(tuple(tied[1:]))
    back_values, back_in, back_out, back_step_pre, grad_coef_rows = run(
        functools.partial(back_steps_kernel, head_size),
        (chunks,),
        [
            chunk_row, chunk_lane, chunk_row, chunk_row, chunk_small, chunk_small,
            full(coef_wide.shape), row_full, chunk_row, chunk_row, chunk_row, chunk_state,
            chunk_state, state_block, state_full, row_block, next_state, next_row, state_full,
        ],
        [chunk_row, chunk_lane, chunk_lane, chunk_small, full((16, LANES))],
        [
            row_shape,
            jax.ShapeDtypeStruct((state_size, length), f32),
            jax.ShapeDtypeStruct((state_size, length), f32),
            small_shape,
            jax.ShapeDtypeStruct((16, LANES), f32),
        ],
        (
            values, input_lanes, steps_wide, cum_wide, steps, step_pre, coef_wide, skip_wide,
            mixed, back_mixed, z_local, db_local, dc_local, later_local, later_grad, after, states,
            before, start_state,
        ),
        flops=scan_flops // 2,
    )
    grad_coef = jnp.stack(
        [
            grad_coef_rows[0, :local_heads],
            grad_coef_rows[8, :local_heads],
            jnp.sum(grad_skip[0].reshape(local_heads, head_size), axis=1),
        ]
    )
    back_pair = jnp.stack([back_in, back_out]).reshape(2, head_count, state_local, length)

    def pair_block(index):
        return lax.dynamic_index_in_dim(back_pair, index, 1, False)

    back_local_pair = pair_block(head_index)
    for by in range(1, head_count):
        back_local_pair = back_local_pair + shift(
            pair_block(lax.rem(head_index + by, head_count)), "head", by
        )
    value_padded, value_taps_grad = value_pull(back_values)
    state_padded, state_taps_grad = state_pull(
        back_local_pair.reshape(2 * state_local, length).T
    )
    grad_taps = jnp.concatenate([value_taps_grad, state_taps_grad], axis=1)
    back_padded = jnp.concatenate([value_padded, state_padded], axis=1)
    rim_back = from_behind(back_padded[: tap_count - 1], "seq", -1)
    back_conv = back_padded[tap_count - 1 :]
    rim_start = length - tap_count + 1
    back_conv = jnp.concatenate([back_conv[:rim_start], back_conv[rim_start:] + rim_back], axis=0)
    back_late = jnp.concatenate([back_conv, back_step_pre[:, :local_heads]], axis=1).astype(bf16)
    out_cols, tied = run_line(out_steps, out_got, head_count - 2, (back_late,))
    back_late = tied[0]
    residual_cols = lax.dynamic_slice_in_dim(source, head_index * col_count, col_count, 1)
    layer_output = (residual_cols + out_cols).astype(bf16)
    late_weight = jnp.concatenate([value_weight, state_weight, step_weight], axis=1)
    shard_rows = length // head_count

    def normed_block(index):
        gate_rows = lax.dynamic_slice_in_dim(back_gate, index * shard_rows, shard_rows, 0)
        late_rows = lax.dynamic_slice_in_dim(back_late, index * shard_rows, shard_rows, 0)
        return contract(gate_rows, gate_weight, 1, 1) + contract(late_rows, late_weight, 1, 1)

    normed_steps = line_steps(normed_block, "head")
    normed_got = next(normed_steps)
    late_keep, late_send = late_gradients(seq_index, seq_count, normed.T, back_late)
    sum_late = scatter_relative(late_keep, late_send, "seq")
    back_normed, tied = run_line(normed_steps, normed_got, head_count, (sum_early,))
    sum_early = tied[0]
    sum_gate_half = sum_early[:, :inner_width]
    sum_out_turned = sum_early[:, inner_width:]
    own_source = lax.dynamic_slice_in_dim(source, head_index * shard_rows, shard_rows, 0)
    _, norm_pull = jax.vjp(input_norm, own_source, norm_gain)
    back_source, grad_gain = norm_pull(back_normed)
    back_rows = line_gather(back_source, "head").reshape(length, model_width)
    input_grad = (output_grad.astype(f32) + back_rows).astype(bf16)

    def own_rows(array, along):
        piece_len = array.shape[along] // seq_count
        return lax.dynamic_slice_in_dim(array, seq_index * piece_len, piece_len, along)

    part_out, sum_out, first_out, second_out = adam_turned(
        sum_out_turned, own_rows(proj_out, 1), first_proj_out, second_proj_out
    )
    new_out = turned(gather_rows(part_out, "seq"))

    sum_main = jnp.stack([sum_gate_half, sum_late[:, :inner_width]], axis=1)
    part_main, first_main, second_main = adam_update(
        own_rows(proj_main, 0), sum_main, first_proj_main, second_proj_main, rate_matrix
    )
    new_main = gather_rows(part_main, "seq")
    sum_state = sum_late[:, inner_width : inner_width + 2 * state_local]
    part_state, first_state, second_state = adam_update(
        own_rows(proj_state, 0).reshape(-1, 2 * state_local),
        sum_state,
        first_proj_state.reshape(-1, 2 * state_local),
        second_proj_state.reshape(-1, 2 * state_local),
        rate_matrix,
    )
    sum_step = sum_late[:, inner_width + 2 * state_local :]
    part_step, first_step, second_step = adam_update(
        own_rows(proj_step, 0), sum_step, first_proj_step, second_proj_step, rate_matrix
    )
    new_small = gather_small(jnp.concatenate([part_state, part_step], axis=1), "seq")
    new_state = new_small[:, : 2 * state_local].reshape(model_width, 2, state_local)
    new_step = new_small[:, 2 * state_local :]
    state_form = (-1, 2, state_local)

    taps_wide = inner_width + 2 * state_local
    gain_rows = grad_gain.reshape(8, model_width // 8)
    small = jnp.concatenate(
        [
            grad_taps.reshape(-1),
            grad_gate[0],
            grad_coef.reshape(-1),
        ]
    )
    small_size = small.shape[0]
    padded_size = -(-small_size // 1024) * 1024
    small = jnp.pad(small, (0, padded_size - small_size)).reshape(8, padded_size // 8)
    small = sum_all(jnp.concatenate([small, sum_all(gain_rows, "head")], axis=1), "seq")
    sum_gain = small[:, padded_size // 8 :].reshape(-1)
    small = small[:, : padded_size // 8].reshape(-1)
    taps_size = (tap_count + 1) * taps_wide
    sum_taps = small[:taps_size].reshape(tap_count + 1, taps_wide)
    sum_cmain = sum_taps[:, :inner_width]
    sum_cstate = sum_taps[:, inner_width:].reshape(tap_count + 1, 2, state_local)
    sum_gate = small[taps_size : taps_size + inner_width]
    sum_coef = small[taps_size + inner_width : small_size].reshape(3, local_heads)
    new_gain, first_gain, second_gain = adam_update(
        norm_gain, sum_gain, first_norm_gain, second_norm_gain, rate_vector
    )
    new_cmain, first_cmain, second_cmain = adam_update(
        conv_main, sum_cmain, first_conv_main, second_conv_main, rate_vector
    )
    new_cstate, first_cstate, second_cstate = adam_update(
        conv_state, sum_cstate, first_conv_state, second_conv_state, rate_vector
    )
    new_coef, first_coef, second_coef = adam_update(
        head_coef, sum_coef, first_head_coef, second_head_coef, rate_coef
    )
    new_gate, first_gate, second_gate = adam_update(
        gate_gain, sum_gate, first_gate_gain, second_gate_gain, rate_vector
    )
    return (
        layer_output, input_grad, sum_gain, sum_main, sum_state.reshape(state_form), sum_step,
        sum_cmain, sum_cstate, sum_coef, sum_gate, sum_out, new_gain, new_main, new_state,
        new_step, new_cmain, new_cstate, new_coef, new_gate, new_out, first_gain, first_main,
        first_state.reshape(state_form), first_step, first_cmain, first_cstate, first_coef,
        first_gate, first_out, second_gain, second_main, second_state.reshape(state_form),
        second_step, second_cmain, second_cstate, second_coef, second_gate, second_out,
    )


def solution(mesh):
    return jax.shard_map(
        per_device,
        mesh=mesh,
        in_specs=(
            P("seq", None),
            P("seq", None),
            P(),
            P(None, None, "head"),
            P(None, None, "head"),
            P(None, "head"),
            P(None, "head"),
            P(None, None, "head"),
            P(None, "head"),
            P("head"),
            P("head", None),
            P(),
            P("seq", None, "head"),
            P("seq", None, "head"),
            P("seq", "head"),
            P(None, "head"),
            P(None, None, "head"),
            P(None, "head"),
            P("head"),
            P("head", "seq"),
            P(),
            P("seq", None, "head"),
            P("seq", None, "head"),
            P("seq", "head"),
            P(None, "head"),
            P(None, None, "head"),
            P(None, "head"),
            P("head"),
            P("head", "seq"),
        ),
        out_specs=(
            P("seq", "head"),
            P("seq", None),
            P(),
            P("seq", None, "head"),
            P("seq", None, "head"),
            P("seq", "head"),
            P(None, "head"),
            P(None, None, "head"),
            P(None, "head"),
            P("head"),
            P("head", "seq"),
            P(),
            P(None, None, "head"),
            P(None, None, "head"),
            P(None, "head"),
            P(None, "head"),
            P(None, None, "head"),
            P(None, "head"),
            P("head"),
            P("head", None),
            P(),
            P("seq", None, "head"),
            P("seq", None, "head"),
            P("seq", "head"),
            P(None, "head"),
            P(None, None, "head"),
            P(None, "head"),
            P("head"),
            P("head", "seq"),
            P(),
            P("seq", None, "head"),
            P("seq", None, "head"),
            P("seq", "head"),
            P(None, "head"),
            P(None, None, "head"),
            P(None, "head"),
            P("head"),
            P("head", "seq"),
        ),
        check_vma=False,
    )
```

```python
import functools

import jax
import jax.numpy as jnp
from jax import lax
from jax.experimental import pallas as pl
from jax.experimental.pallas import tpu as pltpu
from jax.sharding import PartitionSpec as P


CHUNK = 128
LANES = 128
HEAD_ROWS = 16

norm_epsilon = 1e-05
beta_first = 0.9
beta_second = 0.95
adam_epsilon = 1e-08
weight_decay = 0.1
adam_step = 2
rate_matrix = 0.005
rate_vector = 0.15
rate_coef = 0.6

NN = ((1,), (0,))
NT = ((1,), (1,))


def swap(value, axis, bit):
    return lax.ppermute(value, axis, [(i, i ^ bit) for i in range(lax.axis_size(axis))])


def shift(value, axis, by):
    count = lax.axis_size(axis)
    return lax.ppermute(value, axis, [(i, (i + by) % count) for i in range(count)])


def from_behind(value, axis, by):
    devices = lax.axis_size(axis)
    pairs = [(i, i + by) for i in range(devices) if 0 <= i + by < devices]
    return lax.ppermute(value, axis, pairs)


def bits_of(axis):
    count, bits = lax.axis_size(axis), []
    while 2 ** len(bits) < count:
        bits.append(2 ** len(bits))
    return bits


def sum_all(value, axis):
    for bit in bits_of(axis):
        value = value + swap(value, axis, bit)
    return value


def bit_of(axis, bit):
    return (lax.axis_index(axis) // bit) % 2


def scatter_rows(value, axis):
    return lax.psum_scatter(value, axis, scatter_dimension=0, tiled=True)


def scatter_relative(keep, send, axis, ahead):
    bits = bits_of(axis)
    rows = keep.shape[1]
    got = swap(send, axis, bits[0])
    dims = (2,) * (len(bits) - 1)
    keep = keep.reshape(dims + keep.shape[1:])
    got = got.reshape(dims + got.shape[1:])
    cuts = [(0, rows // 2), (rows // 2, rows)]
    orders = [bits[1:], bits[1:][::-1]]
    pieces = []
    for (low, high), order in zip(cuts, orders):
        left = list(bits[1:])
        mine = [lax.slice_in_dim(a, low, high, axis=len(dims)) for a in (keep, got)]
        for bit in order:
            dim = len(left) - 1 - left.index(bit)
            sent = sum_of([lax.index_in_dim(a, 1, dim, False) for a in mine])
            if bit == order[-1]:
                sent = after(sent, *ahead)
            held = [lax.index_in_dim(a, 0, dim, False) for a in mine]
            mine = [sum_of(held), swap(sent, axis, bit)]
            left.remove(bit)
        pieces.append(sum_of(mine))
    return jnp.concatenate(pieces, axis=0)


def sum_of(parts):
    return functools.reduce(jnp.add, parts)


def gather_rows(value, axis):
    return lax.all_gather(value, axis, axis=0, tiled=True)


def gather_small(value, axis):
    place = lax.axis_index(axis)
    rows = value.shape[0]
    whole = jnp.zeros((lax.axis_size(axis) * rows,) + value.shape[1:], value.dtype)
    whole = lax.dynamic_update_slice_in_dim(whole, value, place * rows, 0)
    for bit in bits_of(axis):
        base = (place // bit) * bit
        block = lax.dynamic_slice_in_dim(whole, base * rows, bit * rows, 0)
        other = swap(block, axis, bit)
        start = jnp.where(bit_of(axis, bit) == 0, base + bit, base - bit)
        whole = lax.dynamic_update_slice_in_dim(whole, other, start * rows, 0)
    return whole


def after(value, *others):
    return lax.optimization_barrier((value,) + others)[0]


def line_scatter(block_of, axis):
    count, place = lax.axis_size(axis), lax.axis_index(axis)
    blocks = {}

    def term(offset):
        offset = offset % count
        if offset not in blocks:
            blocks[offset] = block_of(lax.rem(place + offset, count))
        return blocks[offset]

    right, left = term(-1), term(1)
    sent = []
    for step in range(1, count):
        sent.append((right, left))
        got_right = lax.ppermute(right, axis, [(i, i + 1) for i in range(step)])
        got_left = lax.ppermute(left, axis, [(count - 1 - i, count - 2 - i) for i in range(step)])
        if step < count - 1:
            right = got_right + term(-step - 1)
            left = got_left + term(step + 1)
    return after(term(0)) + got_right + got_left, sent


def line_gather(value, axis):
    count, place = lax.axis_size(axis), lax.axis_index(axis)
    right = left = value
    from_left, from_right = [], []
    for step in range(1, count):
        right = lax.ppermute(right, axis, [(i, i + 1) for i in range(step - 1, count - 1)])
        left = lax.ppermute(left, axis, [(i + 1, i) for i in range(count - step)])
        from_left.append(right)
        from_right.append(left)
    sent = list(zip(from_left[:-1], from_right[:-1]))
    whole = jnp.zeros((count,) + value.shape, value.dtype)
    whole = lax.dynamic_update_index_in_dim(whole, value, place, 0)
    for step in range(1, count):
        block = jnp.where(place >= step, from_left[step - 1], from_right[count - step - 1])
        whole = lax.dynamic_update_index_in_dim(
            whole, block, lax.rem(place + count - step, count), 0
        )
    return whole, sent


def ring_gather(value, axis):
    count, place = lax.axis_size(axis), lax.axis_index(axis)
    whole = jnp.zeros((count,) + value.shape, value.dtype)
    whole = lax.dynamic_update_index_in_dim(whole, value, place, 0)
    for by in range(1, count):
        whole = lax.dynamic_update_index_in_dim(
            whole, shift(value, axis, by), lax.rem(place + count - by, count), 0
        )
    return whole


def carried_state(decay, part, axis, reverse):
    bits = bits_of(axis)
    half = part.shape[0] // 2
    mine = bit_of(axis, bits[0])

    def later_of(bit):
        high = bit_of(axis, bit) == 1
        return jnp.logical_not(high) if reverse else high

    other = swap(part, axis, bits[0])
    other_decay = swap(decay, axis, bits[0])
    own_half = lax.dynamic_slice_in_dim(part, mine * half, half, 0)
    other_half = lax.dynamic_slice_in_dim(other, mine * half, half, 0)
    later = later_of(bits[0])
    total = jnp.where(
        later, own_half + decay * other_half, other_half + other_decay * own_half
    )
    total_decay = decay * other_decay
    before, before_decay = jnp.zeros_like(total), jnp.ones_like(decay)
    for bit in bits[1:]:
        got, got_decay = swap(total, axis, bit), swap(total_decay, axis, bit)
        ahead = later_of(bit)
        before = jnp.where(ahead, before + before_decay * got, before)
        before_decay = jnp.where(ahead, before_decay * got_decay, before_decay)
        if bit != bits[-1]:
            total = jnp.where(ahead, total + total_decay * got, got + got_decay * total)
            total_decay = total_decay * got_decay
    rest = swap(before, axis, bits[0])
    whole = jnp.concatenate(
        [jnp.where(mine == 0, before, rest), jnp.where(mine == 0, rest, before)], axis=0
    )
    return jnp.where(later, other + other_decay * whole, whole)


def dot(left, right, dims):
    return lax.dot_general(left, right, (dims, ((), ())), preferred_element_type=jnp.float32)


def two(value):
    high = value.astype(jnp.bfloat16)
    return high, (value - high.astype(jnp.float32)).astype(jnp.bfloat16)


def three(value):
    high = value.astype(jnp.bfloat16)
    rest = value - high.astype(jnp.float32)
    mid = rest.astype(jnp.bfloat16)
    return high, mid, (rest - mid.astype(jnp.float32)).astype(jnp.bfloat16)


def mul(left, right, dims=NN):
    (lh, ll), (rh, rl) = two(left), two(right)
    return dot(lh, rh, dims) + (dot(lh, rl, dims) + dot(ll, rh, dims))


def mul_mask(mask, value, dims=NN):
    high, mid, low = three(value)
    return dot(mask, high, dims) + (dot(mask, mid, dims) + dot(mask, low, dims))


def mul_by_mask(value, mask, dims=NN):
    high, mid, low = three(value)
    return dot(high, mask, dims) + (dot(mid, mask, dims) + dot(low, mask, dims))


def head_mask(width, head_size):
    row = lax.broadcasted_iota(jnp.int32, (LANES, width), 0)
    col = lax.broadcasted_iota(jnp.int32, (LANES, width), 1)
    low = row * head_size
    return jnp.where((col >= low) & (col < low + head_size), 1.0, 0.0).astype(jnp.bfloat16)


def order_mask(size, upper):
    row = lax.broadcasted_iota(jnp.int32, (size, size), 0)
    col = lax.broadcasted_iota(jnp.int32, (size, size), 1)
    return (row <= col) if upper else (row >= col)


def soft_plus(value):
    return jnp.maximum(value, 0.0) + jnp.log1p(jnp.exp(-jnp.abs(value)))


def sigmoid(value):
    return 1.0 / (1.0 + jnp.exp(-value))


def states_kernel(
    head_size, x_ref, bt_ref, step_ref, coef_ref,
    dt_ref, dtx_ref, cumx_ref, cumt_ref, st_ref, pre_ref, post_ref,
):
    length, width = x_ref.shape
    count = length // CHUNK
    spread = head_mask(width, head_size)
    lower = jnp.where(order_mask(CHUNK, False), 1.0, 0.0).astype(jnp.bfloat16)
    state = jnp.zeros((bt_ref.shape[0], width), jnp.float32)
    run = jnp.zeros((1, width), jnp.float32)
    rate = -jnp.exp(coef_ref[1:2, :])
    bias = coef_ref[0:1, :]
    runs = []
    for c in range(count):
        at = slice(c * CHUNK, (c + 1) * CHUNK)
        steps = soft_plus(step_ref[at, :] + bias)
        cum = mul_mask(lower, rate * steps)
        dtx = mul_by_mask(steps, spread)
        cumx = mul_by_mask(cum, spread)
        dt_ref[at, :] = steps
        dtx_ref[at, :] = dtx
        cumx_ref[at, :] = cumx
        cumt_ref[:, at] = jnp.transpose(cum)[:HEAD_ROWS, :]
        total = cumx[CHUNK - 1 : CHUNK, :]
        st_ref[c] = state
        pre_ref[c] = jnp.broadcast_to(jnp.exp(run), (8, width))
        state = jnp.exp(total) * state + mul(
            bt_ref[:, at], x_ref[at, :] * dtx * jnp.exp(total - cumx)
        )
        run = run + total
        runs.append(total)
    st_ref[count] = state
    pre_ref[count] = jnp.broadcast_to(jnp.exp(run), (8, width))
    rest = jnp.zeros((1, width), jnp.float32)
    for c in range(count - 1, -1, -1):
        post_ref[c] = jnp.broadcast_to(jnp.exp(rest), (8, width))
        rest = rest + runs[c]


def lane_halves(size, width):
    return lax.broadcasted_iota(jnp.int32, (size, width), 1) < width // 2


def within_kernel(head_size, x_ref, bt_ref, ct_ref, dtx_ref, cumx_ref, cumt_ref, st_ref, y_ref):
    width = x_ref.shape[1]
    pair = 2 * head_size
    reads = jnp.transpose(ct_ref[...])
    scores = mul(reads, bt_ref[...])
    mask = order_mask(CHUNK, False)
    first = lane_halves(CHUNK, pair)
    for p in range(width // pair):
        at = slice(p * pair, (p + 1) * pair)
        cumx = cumx_ref[:, at]
        scaled = x_ref[:, at] * dtx_ref[:, at]
        mixing = []
        for h in range(2):
            row = cumt_ref[2 * p + h : 2 * p + h + 1, :]
            col = cumx[:, h * head_size : h * head_size + 1]
            mixing.append(jnp.exp(jnp.where(mask, col - row, -1e30)) * scores)
        stacked = jnp.concatenate(
            [jnp.where(first, scaled, 0.0), jnp.where(first, 0.0, scaled)], axis=0
        )
        inner = mul(jnp.concatenate(mixing, axis=1), stacked)
        y_ref[:, at] = inner + jnp.exp(cumx) * mul(reads, st_ref[0, :, at])


def gate_kernel(
    y_ref, ct_ref, cumx_ref, pre_ref, start_ref, x_ref, skip_ref, gate_ref, back_ref, gain_ref,
    mixed_ref, sums_ref,
):
    width = x_ref.shape[1]
    reads = jnp.transpose(ct_ref[...])
    carried = jnp.exp(cumx_ref[...]) * pre_ref[0, 0:1, :] * mul(reads, start_ref[...])
    mixed = y_ref[...] + carried + skip_ref[0:1, :] * x_ref[...]
    gate = gate_ref[...]
    gated = mixed * (gate * sigmoid(gate))
    mixed_ref[...] = mixed
    ones = jnp.ones((8, width), jnp.bfloat16)
    sums_ref[0:8, :] = mul_mask(ones, gated * gated, NT)
    sums_ref[8:16, :] = mul_mask(ones, back_ref[...] * gain_ref[0:1, :] * gated, NT)


def turn_kernel(
    full_inner, sums_ref, mixed_ref, gate_ref, back_ref, gain_ref, x_ref, cumx_ref, ct_ref,
    skip_ref,
    normal_ref, dy_ref, bgate_ref, ggate_ref, gskip_ref, g_ref, jump_ref, carry_ref,
):
    step = pl.program_id(0)

    @pl.when(step == 0)
    def _():
        carry_ref[...] = jnp.zeros_like(carry_ref)
        ggate_ref[...] = jnp.zeros_like(ggate_ref)
        gskip_ref[...] = jnp.zeros_like(gskip_ref)

    columns = jnp.transpose(sums_ref[...])
    scale = lax.rsqrt(columns[:, 0:1] / full_inner + norm_epsilon)
    inner = columns[:, 8:9] / full_inner
    mixed = mixed_ref[...]
    gate = gate_ref[...]
    share = sigmoid(gate)
    act = gate * share
    gated = mixed * act
    gain = gain_ref[0:1, :]
    back = back_ref[...]
    scaled = gated * scale
    normal_ref[...] = (scaled * gain).astype(jnp.bfloat16)
    back_gated = scale * (back * gain) - gated * (scale * scale * scale) * inner
    dy = back_gated * act
    dy_ref[...] = dy
    bgate_ref[...] = (back_gated * mixed * (share * (1.0 + gate * (1.0 - share)))).astype(
        jnp.bfloat16
    )
    ggate_ref[...] += jnp.broadcast_to(
        jnp.sum(back * scaled, axis=0, keepdims=True), ggate_ref.shape
    )
    gskip_ref[...] += jnp.broadcast_to(
        jnp.sum(dy * x_ref[...], axis=0, keepdims=True), gskip_ref.shape
    )
    carry = carry_ref[...]
    g_ref[0] = carry
    cumx = cumx_ref[...]
    carry = jnp.exp(cumx[CHUNK - 1 : CHUNK, :]) * carry + mul(ct_ref[...], dy * jnp.exp(cumx))
    carry_ref[...] = carry
    jump_ref[...] = carry


def back_within_kernel(
    head_size, x_ref, bt_ref, ct_ref, dtx_ref, cumx_ref, cumt_ref, st_ref, pre_ref, start_ref,
    dy_ref, g_ref,
    z_ref, db_ref, dc_ref,
):
    width = x_ref.shape[1]
    pair = 2 * head_size
    inputs = jnp.transpose(bt_ref[...])
    scores = mul(inputs, ct_ref[...])
    mask = order_mask(CHUNK, True)
    first = lane_halves(CHUNK, pair)
    grad_scores = jnp.zeros((CHUNK, CHUNK), jnp.float32)
    for p in range(width // pair):
        at = slice(p * pair, (p + 1) * pair)
        cumx = cumx_ref[:, at]
        dy = dy_ref[:, at]
        scaled = x_ref[:, at] * dtx_ref[:, at]
        products = mul(
            jnp.concatenate(
                [jnp.where(first, scaled, 0.0), jnp.where(first, 0.0, scaled)], axis=0
            ),
            dy,
            NT,
        )
        mixing = []
        for h in range(2):
            row = cumt_ref[2 * p + h : 2 * p + h + 1, :]
            col = cumx[:, h * head_size : h * head_size + 1]
            decay = jnp.exp(jnp.where(mask, row - col, -1e30))
            grad_scores = grad_scores + decay * products[h * CHUNK : (h + 1) * CHUNK, :]
            mixing.append(decay * scores)
        stacked = jnp.concatenate([jnp.where(first, dy, 0.0), jnp.where(first, 0.0, dy)], axis=0)
        inner = mul(jnp.concatenate(mixing, axis=1), stacked)
        decay_out = jnp.exp(cumx[CHUNK - 1 : CHUNK, :] - cumx)
        z_ref[:, at] = inner + decay_out * mul(inputs, g_ref[0, :, at])
    cumx = cumx_ref[...]
    scaled = x_ref[...] * dtx_ref[...] * jnp.exp(cumx[CHUNK - 1 : CHUNK, :] - cumx)
    entering = st_ref[0] + pre_ref[0, 0:1, :] * start_ref[...]
    reads = jnp.transpose(ct_ref[...])
    db_ref[...] = mul(grad_scores, reads) + mul(scaled, g_ref[0], NT)
    dc_ref[...] = mul(jnp.transpose(grad_scores), inputs) + mul(
        dy_ref[...] * jnp.exp(cumx), entering, NT
    )


def back_steps_kernel(
    head_size, x_ref, bt_ref, dtx_ref, cumx_ref, dt_ref, step_ref, coef_ref, skip_ref, mixed_ref,
    dy_ref, z_ref, db_ref, dc_ref, g_ref, later_ref, post_ref, end_ref, pre_ref, start_ref,
    dx_ref, dbt_ref, dct_ref, dstep_ref, gcoef_ref,
):
    width = x_ref.shape[1]

    @pl.when(pl.program_id(0) == 0)
    def _():
        gcoef_ref[...] = jnp.zeros_like(gcoef_ref)

    spread = head_mask(width, head_size)
    upper = jnp.where(order_mask(CHUNK, True), 1.0, 0.0).astype(jnp.bfloat16)
    x = x_ref[...]
    dy = dy_ref[...]
    cumx = cumx_ref[...]
    skip = skip_ref[0:1, :]
    dtx = dtx_ref[...]
    later = later_ref[...]
    post = post_ref[0, 0:1, :]
    inputs = jnp.transpose(bt_ref[...])
    decay_out = post * jnp.exp(cumx[CHUNK - 1 : CHUNK, :] - cumx)
    z = z_ref[...] + decay_out * mul(inputs, later)
    dx_ref[...] = dtx * z + skip * dy
    db = db_ref[...] + mul(x * dtx * decay_out, later, NT)
    dbt_ref[...] = jnp.transpose(db)
    dct_ref[...] = jnp.transpose(dc_ref[...])
    steps = dt_ref[...]
    by_step = mul_by_mask(x * z, spread, NT)
    by_out = mul_by_mask(dy * (mixed_ref[...] - skip * x), spread, NT)
    leaving = end_ref[0] + pre_ref[0, 0:1, :] * start_ref[...]
    held = jnp.sum((g_ref[0] + post * later) * leaving, axis=0, keepdims=True)
    held = mul_by_mask(jnp.broadcast_to(held, (8, width)), spread, NT)[0:1, :]
    by_decay = mul_mask(upper, by_out - steps * by_step) + held
    rate = -jnp.exp(coef_ref[1:2, :])
    back = (by_step + rate * by_decay) * sigmoid(step_ref[...] + coef_ref[0:1, :])
    dstep_ref[...] = back
    gcoef_ref[0:8, :] += jnp.broadcast_to(jnp.sum(back, axis=0, keepdims=True), (8, LANES))
    gcoef_ref[8:16, :] += jnp.broadcast_to(
        jnp.sum(by_decay * rate * steps, axis=0, keepdims=True), (8, LANES)
    )


def full(array_shape):
    zeros = (0,) * len(array_shape)
    return pl.BlockSpec(array_shape, lambda i: zeros)


def run(kernel, grid, in_specs, out_specs, out_shapes, args, scratch=(), flops=0):
    return call(kernel, grid, in_specs, out_specs, out_shapes, args, scratch, flops)


def call(kernel, grid, in_specs, out_specs, out_shapes, args, scratch, flops):
    moved = sum(a.size * a.dtype.itemsize for a in args) + sum(
        s.size * s.dtype.itemsize for s in out_shapes
    )
    return pl.pallas_call(
        kernel,
        grid=grid,
        in_specs=in_specs,
        out_specs=out_specs,
        out_shape=out_shapes,
        scratch_shapes=scratch,
        cost_estimate=pl.CostEstimate(flops=flops, bytes_accessed=moved, transcendentals=0),
        compiler_params=pltpu.CompilerParams(
            dimension_semantics=("arbitrary",) * len(grid), vmem_limit_bytes=48 * 2**20
        ),
    )(*args)


def contract(left, right, left_dim, right_dim):
    return lax.dot_general(
        left, right, (((left_dim,), (right_dim,)), ((), ())), preferred_element_type=jnp.float32
    )


def input_norm(source, gain):
    return (
        source * lax.rsqrt(jnp.mean(source * source, axis=1, keepdims=True) + norm_epsilon) * gain
    )


def convolve(padded, tap_table):
    tap_count = tap_table.shape[0] - 1
    length = padded.shape[0] - tap_count + 1
    total = jnp.broadcast_to(tap_table[tap_count], (length, tap_table.shape[1]))
    for offset in range(tap_count):
        total = total + tap_table[offset] * padded[offset : offset + length]
    return jax.nn.silu(total)


def adam_update(weight, gradient, moment_one, moment_two, step_rate):
    first_new = beta_first * moment_one + (1.0 - beta_first) * gradient
    second_new = beta_second * moment_two + (1.0 - beta_second) * gradient * gradient
    first_hat = first_new / (1.0 - beta_first**adam_step)
    second_hat = second_new / (1.0 - beta_second**adam_step)
    updated = weight - step_rate * (
        first_hat / (jnp.sqrt(second_hat) + adam_epsilon) + weight_decay * weight
    )
    return (updated, first_new, second_new)


def cast_kernel(order_ref, weight_ref, gate_ref, value_ref):
    gate_ref[...] = weight_ref[:, 0, :].astype(jnp.bfloat16)
    value_ref[...] = weight_ref[:, 1, :].astype(jnp.bfloat16)


def cast_halves(order, weight):
    rows, _, width = weight.shape
    half = pl.BlockSpec((CHUNK, width), lambda i: (i, 0))
    shape = jax.ShapeDtypeStruct((rows, width), jnp.bfloat16)
    return run(
        cast_kernel,
        (rows // CHUNK,),
        [
            pl.BlockSpec(memory_space=pl.ANY),
            pl.BlockSpec((CHUNK, 2, width), lambda i: (i, 0, 0)),
        ],
        [half, half],
        [shape, shape],
        (order, weight),
    )


def early_kernel(normed_ref, back_ref, grad_ref, normal_ref, out_ref):
    width = back_ref.shape[1]
    out_ref[:, :width] = dot(jnp.transpose(normed_ref[...]), back_ref[...], NN)
    out_ref[:, width:] = dot(jnp.transpose(grad_ref[...]), normal_ref[...], NN)


def early_gradients(normed, back_gate, output_grad, normal_out):
    length, rows = normed.shape
    width = back_gate.shape[1]
    block = 2 * CHUNK
    columns = pl.BlockSpec((length, block), lambda i: (0, i))
    return run(
        early_kernel,
        (rows // block,),
        [columns, full((length, width)), columns, full((length, width))],
        [pl.BlockSpec((block, 2 * width), lambda i: (i, 0))],
        [jax.ShapeDtypeStruct((rows, 2 * width), jnp.float32)],
        (normed, back_gate, output_grad, normal_out),
        flops=4 * length * rows * width,
    )[0]


def late_kernel(place_ref, normed_ref, back_ref, keep_ref, send_ref):
    product = dot(normed_ref[...], back_ref[...], NN)
    odd = lax.rem(pl.program_id(0), 2) == 1

    @pl.when(odd)
    def _():
        send_ref[0] = product

    @pl.when(jnp.logical_not(odd))
    def _():
        keep_ref[0] = product


def late_gradients(place, count, normed_lanes, back_late):
    rows, length = normed_lanes.shape
    width = back_late.shape[1]
    block = rows // count
    half = jax.ShapeDtypeStruct((count // 2, block, width), jnp.float32)
    half_spec = pl.BlockSpec((1, block, width), lambda i, place_ref: (i // 2, 0, 0))
    return pl.pallas_call(
        late_kernel,
        grid_spec=pltpu.PrefetchScalarGridSpec(
            num_scalar_prefetch=1,
            grid=(count,),
            in_specs=[
                pl.BlockSpec((block, length), lambda i, place_ref: (place_ref[0] ^ i, 0)),
                pl.BlockSpec((length, width), lambda i, place_ref: (0, 0)),
            ],
            out_specs=[half_spec, half_spec],
        ),
        out_shape=[half, half],
        cost_estimate=pl.CostEstimate(
            flops=2 * rows * length * width,
            bytes_accessed=4 * rows * width + 2 * length * (rows + width),
            transcendentals=0,
        ),
        compiler_params=pltpu.CompilerParams(
            dimension_semantics=("arbitrary",), vmem_limit_bytes=48 * 2**20
        ),
    )(jnp.full((1,), place, jnp.int32), normed_lanes, back_late)


def adam_turned_kernel(grad_ref, weight_ref, one_ref, two_ref, part_ref, sum_ref, first_ref, second_ref):
    gradient = jnp.transpose(grad_ref[...])
    updated, first_new, second_new = adam_update(
        weight_ref[...], gradient, one_ref[...], two_ref[...], rate_matrix
    )
    part_ref[...] = jnp.transpose(updated)
    sum_ref[...] = gradient
    first_ref[...] = first_new
    second_ref[...] = second_new


def adam_turned(gradient, weight, moment_one, moment_two):
    rows, columns = weight.shape
    whole = [full((rows, columns))] * 3
    shape = jax.ShapeDtypeStruct((rows, columns), jnp.float32)
    return run(
        adam_turned_kernel,
        (1,),
        [full((columns, rows))] + whole,
        [full((columns, rows))] + whole,
        [jax.ShapeDtypeStruct((columns, rows), jnp.float32)] + [shape] * 3,
        (gradient, weight, moment_one, moment_two),
    )


def turn_block_kernel(in_ref, out_ref):
    out_ref[...] = jnp.transpose(in_ref[...])


def turned(array):
    rows, columns = array.shape
    block = 2 * CHUNK
    return run(
        turn_block_kernel,
        (rows // block,),
        [pl.BlockSpec((block, columns), lambda i: (i, 0))],
        [pl.BlockSpec((columns, block), lambda i: (0, i))],
        [jax.ShapeDtypeStruct((columns, rows), array.dtype)],
        (array,),
    )[0]


def rows_of_eight(vector):
    return jnp.broadcast_to(vector[None, :], (8, vector.shape[0]))


def layer_step(
    layer_input, output_grad, norm_gain, proj_main, proj_state, proj_step, conv_main, conv_state,
    head_coef, gate_gain, proj_out, first_norm_gain, first_proj_main, first_proj_state,
    first_proj_step, first_conv_main, first_conv_state, first_head_coef, first_gate_gain,
    first_proj_out, second_norm_gain, second_proj_main, second_proj_state, second_proj_step,
    second_conv_main, second_conv_state, second_head_coef, second_gate_gain, second_proj_out,
):
    f32, bf16 = jnp.float32, jnp.bfloat16
    length, model_width = layer_input.shape
    local_heads = proj_step.shape[1]
    inner_width = proj_main.shape[2]
    head_size = inner_width // local_heads
    state_local = proj_state.shape[2]
    tap_count = conv_main.shape[0] - 1
    head_count = lax.axis_size("head")
    seq_count = lax.axis_size("seq")
    seq_index = lax.axis_index("seq")
    head_index = lax.axis_index("head")
    state_size = state_local * head_count
    full_inner = inner_width * head_count
    chunks = length // CHUNK
    chunk_row = pl.BlockSpec((CHUNK, inner_width), lambda i: (i, 0))
    chunk_lane = pl.BlockSpec((state_size, CHUNK), lambda i: (0, i))
    chunk_head = pl.BlockSpec((HEAD_ROWS, CHUNK), lambda i: (0, i))
    chunk_small = pl.BlockSpec((CHUNK, LANES), lambda i: (i, 0))
    chunk_state = pl.BlockSpec((CHUNK, state_size), lambda i: (i, 0))
    state_block = pl.BlockSpec((1, state_size, inner_width), lambda i: (i, 0, 0))
    next_state = pl.BlockSpec((1, state_size, inner_width), lambda i: (i + 1, 0, 0))
    row_block = pl.BlockSpec((1, 8, inner_width), lambda i: (i, 0, 0))
    next_row = pl.BlockSpec((1, 8, inner_width), lambda i: (i + 1, 0, 0))
    state_full = full((state_size, inner_width))
    row_full = full((8, inner_width))
    row_shape = jax.ShapeDtypeStruct((length, inner_width), f32)
    small_shape = jax.ShapeDtypeStruct((length, LANES), f32)
    state_shape = jax.ShapeDtypeStruct((state_size, inner_width), f32)
    scan_flops = 2 * 3 * length * inner_width * (2 * CHUNK + state_size)

    halo = 16
    rim = halo - (tap_count - 1)
    source = layer_input.astype(f32)
    rim_source = from_behind(source[length - halo :], "seq", 1)
    normed = input_norm(source, norm_gain).astype(bf16)
    normed_long = jnp.concatenate([input_norm(rim_source, norm_gain).astype(bf16), normed], axis=0)
    state_weight = proj_state.reshape(model_width, 2 * state_local).astype(bf16)
    step_weight = proj_step.astype(bf16)
    step_wide = jnp.pad(step_weight, ((0, 0), (0, LANES - local_heads)))
    out_weight = proj_out.astype(bf16)
    coef_wide = jnp.pad(head_coef, ((0, 8 - head_coef.shape[0]), (0, LANES - local_heads)))
    skip_wide = rows_of_eight(jnp.repeat(head_coef[2], head_size))
    gain_wide = rows_of_eight(gate_gain)

    state_pre = jnp.dot(normed_long, state_weight, preferred_element_type=f32)
    state_taps = conv_state.reshape(tap_count + 1, 2 * state_local)
    state_active, state_pull = jax.vjp(convolve, state_pre[rim:], state_taps)
    state_lanes = state_active.T
    pair_lanes = ring_gather(state_lanes, "head")
    gate_weight, value_weight = cast_halves(state_lanes, proj_main)
    value_pre = jnp.dot(normed_long, value_weight, preferred_element_type=f32)
    values, value_pull = jax.vjp(convolve, value_pre[rim:], conv_main)
    step_pre = jnp.dot(normed, step_wide, preferred_element_type=f32)
    gate_pre = jnp.dot(normed, gate_weight, preferred_element_type=f32)
    pair_lanes = pair_lanes.reshape(head_count, 2, state_local, length)
    input_lanes = pair_lanes[:, 0].reshape(state_size, length)
    output_lanes = pair_lanes[:, 1].reshape(state_size, length)

    steps, steps_wide, cum_wide, cum_lanes, states, before, beyond = run(
        functools.partial(states_kernel, head_size),
        (1,),
        [full(a.shape) for a in (values, input_lanes, step_pre, coef_wide)],
        [
            full((length, LANES)),
            full((length, inner_width)),
            full((length, inner_width)),
            full((HEAD_ROWS, length)),
            full((chunks + 1, state_size, inner_width)),
            full((chunks + 1, 8, inner_width)),
            full((chunks, 8, inner_width)),
        ],
        [
            small_shape,
            row_shape,
            row_shape,
            jax.ShapeDtypeStruct((HEAD_ROWS, length), f32),
            jax.ShapeDtypeStruct((chunks + 1, state_size, inner_width), f32),
            jax.ShapeDtypeStruct((chunks + 1, 8, inner_width), f32),
            jax.ShapeDtypeStruct((chunks, 8, inner_width), f32),
        ],
        (values, input_lanes, step_pre, coef_wide),
        flops=scan_flops // 3,
    )
    through = before[chunks, 0:1]
    start_state = carried_state(through, states[chunks], "seq", False)
    local_out = run(
        functools.partial(within_kernel, head_size),
        (chunks,),
        [chunk_row, chunk_lane, chunk_lane, chunk_row, chunk_row, chunk_head, state_block],
        [chunk_row],
        [row_shape],
        (values, input_lanes, output_lanes, steps_wide, cum_wide, cum_lanes, states),
        flops=scan_flops,
    )[0]
    back_normal = contract(output_grad, out_weight, 1, 1)
    mixed, sums = run(
        gate_kernel,
        (chunks,),
        [
            chunk_row, chunk_lane, chunk_row, row_block, state_full, chunk_row, row_full,
            chunk_row, chunk_row, row_full,
        ],
        [chunk_row, pl.BlockSpec((16, CHUNK), lambda i: (0, i))],
        [row_shape, jax.ShapeDtypeStruct((16, length), f32)],
        (
            local_out, output_lanes, cum_wide, before, start_state, values, skip_wide,
            gate_pre, back_normal, gain_wide,
        ),
        flops=scan_flops // 4,
    )
    sums = sum_all(sums, "head")
    reverse_row = pl.BlockSpec((CHUNK, inner_width), lambda i: (chunks - 1 - i, 0))
    reverse_lane = pl.BlockSpec((state_size, CHUNK), lambda i: (0, chunks - 1 - i))
    normal_out, back_mixed, back_gate, grad_gate, grad_skip, later_local, state_jump = run(
        functools.partial(turn_kernel, float(full_inner)),
        (chunks,),
        [
            pl.BlockSpec((16, CHUNK), lambda i: (0, chunks - 1 - i)),
            reverse_row, reverse_row, reverse_row, row_full, reverse_row, reverse_row,
            reverse_lane, row_full,
        ],
        [
            reverse_row, reverse_row, reverse_row, row_full, row_full,
            pl.BlockSpec((1, state_size, inner_width), lambda i: (chunks - 1 - i, 0, 0)),
            state_full,
        ],
        [
            jax.ShapeDtypeStruct((length, inner_width), bf16),
            row_shape,
            jax.ShapeDtypeStruct((length, inner_width), bf16),
            jax.ShapeDtypeStruct((8, inner_width), f32),
            jax.ShapeDtypeStruct((8, inner_width), f32),
            jax.ShapeDtypeStruct((chunks, state_size, inner_width), f32),
            state_shape,
        ],
        (
            sums, mixed, gate_pre, back_normal, gain_wide, values, cum_wide, output_lanes,
            skip_wide,
        ),
        scratch=[pltpu.VMEM((state_size, inner_width), f32)],
        flops=scan_flops // 4,
    )
    later_grad = carried_state(through, state_jump, "seq", True)

    col_count = model_width // head_count

    def out_block(index):
        columns = lax.dynamic_slice_in_dim(out_weight, index * col_count, col_count, 1)
        return jnp.dot(normal_out, columns, preferred_element_type=f32)

    out_cols, out_sent = line_scatter(out_block, "head")
    sum_early = scatter_rows(
        early_gradients(normed, back_gate, output_grad, after(normal_out, *out_sent[0])), "seq"
    )
    back_tied = after(back_mixed, *out_sent[1])
    z_local, db_local, dc_local = run(
        functools.partial(back_within_kernel, head_size),
        (chunks,),
        [
            chunk_row, chunk_lane, chunk_lane, chunk_row, chunk_row, chunk_head, state_block,
            row_block, state_full, chunk_row, state_block,
        ],
        [chunk_row, chunk_state, chunk_state],
        [
            row_shape,
            jax.ShapeDtypeStruct((length, state_size), f32),
            jax.ShapeDtypeStruct((length, state_size), f32),
        ],
        (
            values, input_lanes, output_lanes, steps_wide, cum_wide, cum_lanes, states, before,
            start_state, back_tied, later_local,
        ),
        flops=2 * scan_flops,
    )
    z_local = after(z_local, *out_sent[2])
    back_values, back_in, back_out, back_step_pre, grad_coef_rows = run(
        functools.partial(back_steps_kernel, head_size),
        (chunks,),
        [
            chunk_row, chunk_lane, chunk_row, chunk_row, chunk_small, chunk_small,
            full(coef_wide.shape), row_full, chunk_row, chunk_row, chunk_row, chunk_state,
            chunk_state, state_block, state_full, row_block, next_state, next_row, state_full,
        ],
        [chunk_row, chunk_lane, chunk_lane, chunk_small, full((16, LANES))],
        [
            row_shape,
            jax.ShapeDtypeStruct((state_size, length), f32),
            jax.ShapeDtypeStruct((state_size, length), f32),
            small_shape,
            jax.ShapeDtypeStruct((16, LANES), f32),
        ],
        (
            values, input_lanes, steps_wide, cum_wide, steps, step_pre, coef_wide, skip_wide,
            mixed, back_mixed, z_local, db_local, dc_local, later_local, later_grad, beyond, states,
            before, start_state,
        ),
        flops=scan_flops // 2,
    )
    grad_coef = jnp.stack(
        [
            grad_coef_rows[0, :local_heads],
            grad_coef_rows[8, :local_heads],
            jnp.sum(grad_skip[0].reshape(local_heads, head_size), axis=1),
        ]
    )
    back_pair = jnp.stack([back_in, back_out]).reshape(2, head_count, state_local, length)

    def pair_block(index):
        return lax.dynamic_index_in_dim(back_pair, index, 1, False)

    back_local_pair = pair_block(head_index)
    for by in range(1, head_count):
        back_local_pair = back_local_pair + shift(
            pair_block(lax.rem(head_index + by, head_count)), "head", by
        )
    value_padded, value_taps_grad = value_pull(back_values)
    state_padded, state_taps_grad = state_pull(
        back_local_pair.reshape(2 * state_local, length).T
    )
    grad_taps = jnp.concatenate([value_taps_grad, state_taps_grad], axis=1)
    back_padded = jnp.concatenate([value_padded, state_padded], axis=1)
    rim_back = from_behind(back_padded[: tap_count - 1], "seq", -1)
    back_conv = back_padded[tap_count - 1 :]
    rim_start = length - tap_count + 1
    back_conv = jnp.concatenate([back_conv[:rim_start], back_conv[rim_start:] + rim_back], axis=0)
    back_late = jnp.concatenate([back_conv, back_step_pre[:, :local_heads]], axis=1).astype(bf16)
    residual_cols = lax.dynamic_slice_in_dim(source, head_index * col_count, col_count, 1)
    layer_output = (residual_cols + out_cols).astype(bf16)
    late_weight = jnp.concatenate([value_weight, state_weight, step_weight], axis=1)
    shard_rows = length // head_count

    row_size = lax.rsqrt(jnp.mean(source * source, axis=1, keepdims=True) + norm_epsilon)
    unit = source * row_size
    grad_gain = []

    def normed_block(index):
        gate_rows = lax.dynamic_slice_in_dim(back_gate, index * shard_rows, shard_rows, 0)
        late_rows = lax.dynamic_slice_in_dim(back_late, index * shard_rows, shard_rows, 0)
        block = contract(gate_rows, gate_weight, 1, 1) + contract(late_rows, late_weight, 1, 1)
        unit_rows = lax.dynamic_slice_in_dim(unit, index * shard_rows, shard_rows, 0)
        block = after(block)
        grad_gain.append(jnp.sum(block * unit_rows, axis=0))
        return block

    back_normed, normed_sent = line_scatter(normed_block, "head")
    late_keep, late_send = late_gradients(
        seq_index, seq_count, normed.T, after(back_late, out_cols, *normed_sent[0])
    )
    sum_late = scatter_relative(late_keep, late_send, "seq", normed_sent[1])
    sum_late = after(sum_late, *normed_sent[2])
    sum_early = after(sum_early, *normed_sent[0])
    sum_gate_half = sum_early[:, :inner_width]
    sum_out_turned = sum_early[:, inner_width:]
    own_source = lax.dynamic_slice_in_dim(source, head_index * shard_rows, shard_rows, 0)
    _, norm_pull = jax.vjp(lambda rows: input_norm(rows, norm_gain), own_source)
    (back_source,) = norm_pull(back_normed)

    def own_rows(array, along):
        piece_len = array.shape[along] // seq_count
        return lax.dynamic_slice_in_dim(array, seq_index * piece_len, piece_len, along)

    part_out, sum_out, first_out, second_out = adam_turned(
        sum_out_turned, own_rows(proj_out, 1), first_proj_out, second_proj_out
    )
    new_out = turned(gather_rows(part_out, "seq"))

    sum_main = jnp.stack([sum_gate_half, sum_late[:, :inner_width]], axis=1)
    part_main, first_main, second_main = adam_update(
        own_rows(proj_main, 0), sum_main, first_proj_main, second_proj_main, rate_matrix
    )
    new_main = gather_rows(part_main, "seq")
    sum_state = sum_late[:, inner_width : inner_width + 2 * state_local]
    part_state, first_state, second_state = adam_update(
        own_rows(proj_state, 0).reshape(-1, 2 * state_local),
        sum_state,
        first_proj_state.reshape(-1, 2 * state_local),
        second_proj_state.reshape(-1, 2 * state_local),
        rate_matrix,
    )
    sum_step = sum_late[:, inner_width + 2 * state_local :]
    part_step, first_step, second_step = adam_update(
        own_rows(proj_step, 0), sum_step, first_proj_step, second_proj_step, rate_matrix
    )
    new_small = gather_small(jnp.concatenate([part_state, part_step], axis=1), "seq")
    new_state = new_small[:, : 2 * state_local].reshape(model_width, 2, state_local)
    new_step = new_small[:, 2 * state_local :]
    state_form = (-1, 2, state_local)

    taps_wide = inner_width + 2 * state_local
    gain_rows = sum_of(grad_gain).reshape(8, model_width // 8)
    small = jnp.concatenate(
        [
            grad_taps.reshape(-1),
            grad_gate[0],
            grad_coef.reshape(-1),
        ]
    )
    small_size = small.shape[0]
    padded_size = -(-small_size // 1024) * 1024
    small = jnp.pad(small, (0, padded_size - small_size)).reshape(8, padded_size // 8)
    small = sum_all(jnp.concatenate([small, gain_rows], axis=1), "seq")
    sum_gain = small[:, padded_size // 8 :]
    for bit in bits_of("head"):
        got_gain = swap(sum_gain, "head", bit)
        sum_gain = sum_gain + got_gain
    sum_gain = sum_gain.reshape(-1)
    small = small[:, : padded_size // 8].reshape(-1)
    taps_size = (tap_count + 1) * taps_wide
    sum_taps = small[:taps_size].reshape(tap_count + 1, taps_wide)
    back_rows, _ = line_gather(after(back_source, sum_gain), "head")
    back_rows = back_rows.reshape(length, model_width)
    input_grad = (output_grad.astype(f32) + back_rows).astype(bf16)
    sum_cmain = sum_taps[:, :inner_width]
    sum_cstate = sum_taps[:, inner_width:].reshape(tap_count + 1, 2, state_local)
    sum_gate = small[taps_size : taps_size + inner_width]
    sum_coef = small[taps_size + inner_width : small_size].reshape(3, local_heads)
    new_gain, first_gain, second_gain = adam_update(
        norm_gain, sum_gain, first_norm_gain, second_norm_gain, rate_vector
    )
    new_cmain, first_cmain, second_cmain = adam_update(
        conv_main, sum_cmain, first_conv_main, second_conv_main, rate_vector
    )
    new_cstate, first_cstate, second_cstate = adam_update(
        conv_state, sum_cstate, first_conv_state, second_conv_state, rate_vector
    )
    new_coef, first_coef, second_coef = adam_update(
        head_coef, sum_coef, first_head_coef, second_head_coef, rate_coef
    )
    new_gate, first_gate, second_gate = adam_update(
        gate_gain, sum_gate, first_gate_gain, second_gate_gain, rate_vector
    )
    return (
        layer_output, input_grad, sum_gain, sum_main, sum_state.reshape(state_form), sum_step,
        sum_cmain, sum_cstate, sum_coef, sum_gate, sum_out, new_gain, new_main, new_state,
        new_step, new_cmain, new_cstate, new_coef, new_gate, new_out, first_gain, first_main,
        first_state.reshape(state_form), first_step, first_cmain, first_cstate, first_coef,
        first_gate, first_out, second_gain, second_main, second_state.reshape(state_form),
        second_step, second_cmain, second_cstate, second_coef, second_gate, second_out,
    )


def solution(mesh):
    return jax.shard_map(
        layer_step,
        mesh=mesh,
        in_specs=(
            P("seq", None),
            P("seq", None),
            P(),
            P(None, None, "head"),
            P(None, None, "head"),
            P(None, "head"),
            P(None, "head"),
            P(None, None, "head"),
            P(None, "head"),
            P("head"),
            P("head", None),
            P(),
            P("seq", None, "head"),
            P("seq", None, "head"),
            P("seq", "head"),
            P(None, "head"),
            P(None, None, "head"),
            P(None, "head"),
            P("head"),
            P("head", "seq"),
            P(),
            P("seq", None, "head"),
            P("seq", None, "head"),
            P("seq", "head"),
            P(None, "head"),
            P(None, None, "head"),
            P(None, "head"),
            P("head"),
            P("head", "seq"),
        ),
        out_specs=(
            P("seq", "head"),
            P("seq", None),
            P(),
            P("seq", None, "head"),
            P("seq", None, "head"),
            P("seq", "head"),
            P(None, "head"),
            P(None, None, "head"),
            P(None, "head"),
            P("head"),
            P("head", "seq"),
            P(),
            P(None, None, "head"),
            P(None, None, "head"),
            P(None, "head"),
            P(None, "head"),
            P(None, None, "head"),
            P(None, "head"),
            P("head"),
            P("head", None),
            P(),
            P("seq", None, "head"),
            P("seq", None, "head"),
            P("seq", "head"),
            P(None, "head"),
            P(None, None, "head"),
            P(None, "head"),
            P("head"),
            P("head", "seq"),
            P(),
            P("seq", None, "head"),
            P("seq", None, "head"),
            P("seq", "head"),
            P(None, "head"),
            P(None, None, "head"),
            P(None, "head"),
            P("head"),
            P("head", "seq"),
        ),
        check_vma=False,
    )
```

```python
import functools

import jax
import jax.numpy as jnp
from jax import lax
from jax.experimental import pallas as pl
from jax.experimental.layout import Layout, with_layout_constraint
from jax.experimental.pallas import tpu as pltpu
from jax.sharding import PartitionSpec as P


CHUNK = 128
LANES = 128
HEAD_ROWS = 16

norm_epsilon = 1e-05
beta_first = 0.9
beta_second = 0.95
adam_epsilon = 1e-08
weight_decay = 0.1
adam_step = 2
rate_matrix = 0.005
rate_vector = 0.15
rate_coef = 0.6

NN = ((1,), (0,))
NT = ((1,), (1,))


def swap(value, axis, bit):
    return lax.ppermute(value, axis, [(i, i ^ bit) for i in range(lax.axis_size(axis))])


def shift(value, axis, by):
    count = lax.axis_size(axis)
    return lax.ppermute(value, axis, [(i, (i + by) % count) for i in range(count)])


def from_behind(value, axis, by):
    devices = lax.axis_size(axis)
    pairs = [(i, i + by) for i in range(devices) if 0 <= i + by < devices]
    return lax.ppermute(value, axis, pairs)


def bits_of(axis):
    count, bits = lax.axis_size(axis), []
    while 2 ** len(bits) < count:
        bits.append(2 ** len(bits))
    return bits


def sum_all(value, axis):
    for bit in bits_of(axis):
        value = value + swap(value, axis, bit)
    return value


def bit_of(axis, bit):
    return (lax.axis_index(axis) // bit) % 2


def scatter_rows(value, axis):
    return lax.psum_scatter(value, axis, scatter_dimension=0, tiled=True)


def scatter_relative(keep, send, axis, ahead):
    bits = bits_of(axis)
    rows = keep.shape[1]
    got = swap(send, axis, bits[0])
    dims = (2,) * (len(bits) - 1)
    keep = keep.reshape(dims + keep.shape[1:])
    got = got.reshape(dims + got.shape[1:])
    cuts = [(0, rows // 2), (rows // 2, rows)]
    orders = [bits[1:], bits[1:][::-1]]
    pieces = []
    for (low, high), order in zip(cuts, orders):
        left = list(bits[1:])
        mine = [lax.slice_in_dim(a, low, high, axis=len(dims)) for a in (keep, got)]
        for bit in order:
            dim = len(left) - 1 - left.index(bit)
            sent = sum_of([lax.index_in_dim(a, 1, dim, False) for a in mine])
            if bit == order[-1]:
                sent = after(sent, *ahead)
            held = [lax.index_in_dim(a, 0, dim, False) for a in mine]
            mine = [sum_of(held), swap(sent, axis, bit)]
            left.remove(bit)
        pieces.append(sum_of(mine))
    return jnp.concatenate(pieces, axis=0)


def sum_of(parts):
    return functools.reduce(jnp.add, parts)


def gather_rows(value, axis):
    return lax.all_gather(value, axis, axis=0, tiled=True)


def gather_small(value, axis):
    place = lax.axis_index(axis)
    rows = value.shape[0]
    whole = jnp.zeros((lax.axis_size(axis) * rows,) + value.shape[1:], value.dtype)
    whole = lax.dynamic_update_slice_in_dim(whole, value, place * rows, 0)
    for bit in bits_of(axis):
        base = (place // bit) * bit
        block = lax.dynamic_slice_in_dim(whole, base * rows, bit * rows, 0)
        other = swap(block, axis, bit)
        start = jnp.where(bit_of(axis, bit) == 0, base + bit, base - bit)
        whole = lax.dynamic_update_slice_in_dim(whole, other, start * rows, 0)
    return whole


def plain(value):
    return with_layout_constraint(value, Layout(tuple(range(value.ndim))))


def after(value, *others):
    return lax.optimization_barrier((value,) + others)[0]


def line_scatter(block_of, axis):
    count, place = lax.axis_size(axis), lax.axis_index(axis)
    blocks = {}

    def term(offset):
        offset = offset % count
        if offset not in blocks:
            blocks[offset] = block_of(lax.rem(place + offset, count))
        return blocks[offset]

    right, left = term(-1), term(1)
    sent = []
    for step in range(1, count):
        sent.append((right, left))
        got_right = lax.ppermute(right, axis, [(i, i + 1) for i in range(step)])
        got_left = lax.ppermute(left, axis, [(count - 1 - i, count - 2 - i) for i in range(step)])
        if step < count - 1:
            right = got_right + term(-step - 1)
            left = got_left + after(term(step + 1))
    return after(term(0)) + got_right + got_left, sent


def line_gather(value, axis):
    count, place = lax.axis_size(axis), lax.axis_index(axis)
    right = left = value
    from_left, from_right = [], []
    for step in range(1, count):
        right = lax.ppermute(right, axis, [(i, i + 1) for i in range(step - 1, count - 1)])
        left = lax.ppermute(left, axis, [(i + 1, i) for i in range(count - step)])
        from_left.append(right)
        from_right.append(left)
    sent = list(zip(from_left[:-1], from_right[:-1]))
    whole = jnp.zeros((count,) + value.shape, value.dtype)
    whole = lax.dynamic_update_index_in_dim(whole, value, place, 0)
    for step in range(1, count):
        block = jnp.where(place >= step, from_left[step - 1], from_right[count - step - 1])
        whole = lax.dynamic_update_index_in_dim(
            whole, block, lax.rem(place + count - step, count), 0
        )
    return whole, sent


def ring_gather(value, axis):
    count, place = lax.axis_size(axis), lax.axis_index(axis)
    whole = jnp.zeros((count,) + value.shape, value.dtype)
    whole = lax.dynamic_update_index_in_dim(whole, value, place, 0)
    for by in range(1, count):
        whole = lax.dynamic_update_index_in_dim(
            whole, shift(value, axis, by), lax.rem(place + count - by, count), 0
        )
    return whole


def carried_state(decay, part, axis, reverse):
    bits = bits_of(axis)
    half = part.shape[0] // 2
    mine = bit_of(axis, bits[0])

    def later_of(bit):
        high = bit_of(axis, bit) == 1
        return jnp.logical_not(high) if reverse else high

    other = swap(part, axis, bits[0])
    other_decay = swap(decay, axis, bits[0])
    own_half = lax.dynamic_slice_in_dim(part, mine * half, half, 0)
    other_half = lax.dynamic_slice_in_dim(other, mine * half, half, 0)
    later = later_of(bits[0])
    total = jnp.where(
        later, own_half + decay * other_half, other_half + other_decay * own_half
    )
    total_decay = decay * other_decay
    before, before_decay = jnp.zeros_like(total), jnp.ones_like(decay)
    for bit in bits[1:]:
        got, got_decay = swap(total, axis, bit), swap(total_decay, axis, bit)
        ahead = later_of(bit)
        before = jnp.where(ahead, before + before_decay * got, before)
        before_decay = jnp.where(ahead, before_decay * got_decay, before_decay)
        if bit != bits[-1]:
            total = jnp.where(ahead, total + total_decay * got, got + got_decay * total)
            total_decay = total_decay * got_decay
    rest = swap(before, axis, bits[0])
    whole = jnp.concatenate(
        [jnp.where(mine == 0, before, rest), jnp.where(mine == 0, rest, before)], axis=0
    )
    return jnp.where(later, other + other_decay * whole, whole)


def dot(left, right, dims):
    return lax.dot_general(left, right, (dims, ((), ())), preferred_element_type=jnp.float32)


def two(value):
    high = value.astype(jnp.bfloat16)
    return high, (value - high.astype(jnp.float32)).astype(jnp.bfloat16)


def three(value):
    high = value.astype(jnp.bfloat16)
    rest = value - high.astype(jnp.float32)
    mid = rest.astype(jnp.bfloat16)
    return high, mid, (rest - mid.astype(jnp.float32)).astype(jnp.bfloat16)


def mul(left, right, dims=NN):
    (lh, ll), (rh, rl) = two(left), two(right)
    return dot(lh, rh, dims) + (dot(lh, rl, dims) + dot(ll, rh, dims))


def mul_mask(mask, value, dims=NN):
    high, mid, low = three(value)
    return dot(mask, high, dims) + (dot(mask, mid, dims) + dot(mask, low, dims))


def mul_by_mask(value, mask, dims=NN):
    high, mid, low = three(value)
    return dot(high, mask, dims) + (dot(mid, mask, dims) + dot(low, mask, dims))


def head_mask(width, head_size):
    row = lax.broadcasted_iota(jnp.int32, (LANES, width), 0)
    col = lax.broadcasted_iota(jnp.int32, (LANES, width), 1)
    low = row * head_size
    return jnp.where((col >= low) & (col < low + head_size), 1.0, 0.0).astype(jnp.bfloat16)


def order_mask(size, upper):
    row = lax.broadcasted_iota(jnp.int32, (size, size), 0)
    col = lax.broadcasted_iota(jnp.int32, (size, size), 1)
    return (row <= col) if upper else (row >= col)


def soft_plus(value):
    return jnp.maximum(value, 0.0) + jnp.log1p(jnp.exp(-jnp.abs(value)))


def sigmoid(value):
    return 1.0 / (1.0 + jnp.exp(-value))


def states_kernel(
    head_size, x_ref, bt_ref, step_ref, coef_ref,
    dt_ref, dtx_ref, cumx_ref, cumt_ref, st_ref, pre_ref, post_ref,
):
    length, width = x_ref.shape
    count = length // CHUNK
    spread = head_mask(width, head_size)
    lower = jnp.where(order_mask(CHUNK, False), 1.0, 0.0).astype(jnp.bfloat16)
    state = jnp.zeros((bt_ref.shape[0], width), jnp.float32)
    run = jnp.zeros((1, width), jnp.float32)
    rate = -jnp.exp(coef_ref[1:2, :])
    bias = coef_ref[0:1, :]
    runs = []
    for c in range(count):
        at = slice(c * CHUNK, (c + 1) * CHUNK)
        steps = soft_plus(step_ref[at, :] + bias)
        cum = mul_mask(lower, rate * steps)
        dtx = mul_by_mask(steps, spread)
        cumx = mul_by_mask(cum, spread)
        dt_ref[at, :] = steps
        dtx_ref[at, :] = dtx
        cumx_ref[at, :] = cumx
        cumt_ref[:, at] = jnp.transpose(cum)[:HEAD_ROWS, :]
        total = cumx[CHUNK - 1 : CHUNK, :]
        st_ref[c] = state
        pre_ref[c] = jnp.broadcast_to(jnp.exp(run), (8, width))
        state = jnp.exp(total) * state + mul(
            bt_ref[:, at], x_ref[at, :] * dtx * jnp.exp(total - cumx)
        )
        run = run + total
        runs.append(total)
    st_ref[count] = state
    pre_ref[count] = jnp.broadcast_to(jnp.exp(run), (8, width))
    rest = jnp.zeros((1, width), jnp.float32)
    for c in range(count - 1, -1, -1):
        post_ref[c] = jnp.broadcast_to(jnp.exp(rest), (8, width))
        rest = rest + runs[c]


def lane_halves(size, width):
    return lax.broadcasted_iota(jnp.int32, (size, width), 1) < width // 2


def within_kernel(head_size, x_ref, bt_ref, ct_ref, dtx_ref, cumx_ref, cumt_ref, st_ref, y_ref):
    width = x_ref.shape[1]
    pair = 2 * head_size
    reads = jnp.transpose(ct_ref[...])
    scores = mul(reads, bt_ref[...])
    mask = order_mask(CHUNK, False)
    first = lane_halves(CHUNK, pair)
    for p in range(width // pair):
        at = slice(p * pair, (p + 1) * pair)
        cumx = cumx_ref[:, at]
        scaled = x_ref[:, at] * dtx_ref[:, at]
        mixing = []
        for h in range(2):
            row = cumt_ref[2 * p + h : 2 * p + h + 1, :]
            col = cumx[:, h * head_size : h * head_size + 1]
            mixing.append(jnp.exp(jnp.where(mask, col - row, -1e30)) * scores)
        stacked = jnp.concatenate(
            [jnp.where(first, scaled, 0.0), jnp.where(first, 0.0, scaled)], axis=0
        )
        inner = mul(jnp.concatenate(mixing, axis=1), stacked)
        y_ref[:, at] = inner + jnp.exp(cumx) * mul(reads, st_ref[0, :, at])


def gate_kernel(
    y_ref, ct_ref, cumx_ref, pre_ref, start_ref, x_ref, skip_ref, gate_ref, back_ref, gain_ref,
    mixed_ref, sums_ref,
):
    width = x_ref.shape[1]
    reads = jnp.transpose(ct_ref[...])
    carried = jnp.exp(cumx_ref[...]) * pre_ref[0, 0:1, :] * mul(reads, start_ref[...])
    mixed = y_ref[...] + carried + skip_ref[0:1, :] * x_ref[...]
    gate = gate_ref[...]
    gated = mixed * (gate * sigmoid(gate))
    mixed_ref[...] = mixed
    ones = jnp.ones((8, width), jnp.bfloat16)
    sums_ref[0:8, :] = mul_mask(ones, gated * gated, NT)
    sums_ref[8:16, :] = mul_mask(ones, back_ref[...] * gain_ref[0:1, :] * gated, NT)


def turn_kernel(
    full_inner, sums_ref, mixed_ref, gate_ref, back_ref, gain_ref, x_ref, cumx_ref, ct_ref,
    skip_ref,
    normal_ref, dy_ref, bgate_ref, ggate_ref, gskip_ref, g_ref, jump_ref, carry_ref,
):
    step = pl.program_id(0)

    @pl.when(step == 0)
    def _():
        carry_ref[...] = jnp.zeros_like(carry_ref)
        ggate_ref[...] = jnp.zeros_like(ggate_ref)
        gskip_ref[...] = jnp.zeros_like(gskip_ref)

    columns = jnp.transpose(sums_ref[...])
    scale = lax.rsqrt(columns[:, 0:1] / full_inner + norm_epsilon)
    inner = columns[:, 8:9] / full_inner
    mixed = mixed_ref[...]
    gate = gate_ref[...]
    share = sigmoid(gate)
    act = gate * share
    gated = mixed * act
    gain = gain_ref[0:1, :]
    back = back_ref[...]
    scaled = gated * scale
    normal_ref[...] = (scaled * gain).astype(jnp.bfloat16)
    back_gated = scale * (back * gain) - gated * (scale * scale * scale) * inner
    dy = back_gated * act
    dy_ref[...] = dy
    bgate_ref[...] = (back_gated * mixed * (share * (1.0 + gate * (1.0 - share)))).astype(
        jnp.bfloat16
    )
    ggate_ref[...] += jnp.broadcast_to(
        jnp.sum(back * scaled, axis=0, keepdims=True), ggate_ref.shape
    )
    gskip_ref[...] += jnp.broadcast_to(
        jnp.sum(dy * x_ref[...], axis=0, keepdims=True), gskip_ref.shape
    )
    carry = carry_ref[...]
    g_ref[0] = carry
    cumx = cumx_ref[...]
    carry = jnp.exp(cumx[CHUNK - 1 : CHUNK, :]) * carry + mul(ct_ref[...], dy * jnp.exp(cumx))
    carry_ref[...] = carry
    jump_ref[...] = carry


def back_within_kernel(
    head_size, x_ref, bt_ref, ct_ref, dtx_ref, cumx_ref, cumt_ref, st_ref, pre_ref, start_ref,
    dy_ref, g_ref,
    z_ref, db_ref, dc_ref,
):
    width = x_ref.shape[1]
    pair = 2 * head_size
    inputs = jnp.transpose(bt_ref[...])
    scores = mul(inputs, ct_ref[...])
    mask = order_mask(CHUNK, True)
    first = lane_halves(CHUNK, pair)
    grad_scores = jnp.zeros((CHUNK, CHUNK), jnp.float32)
    for p in range(width // pair):
        at = slice(p * pair, (p + 1) * pair)
        cumx = cumx_ref[:, at]
        dy = dy_ref[:, at]
        scaled = x_ref[:, at] * dtx_ref[:, at]
        products = mul(
            jnp.concatenate(
                [jnp.where(first, scaled, 0.0), jnp.where(first, 0.0, scaled)], axis=0
            ),
            dy,
            NT,
        )
        mixing = []
        for h in range(2):
            row = cumt_ref[2 * p + h : 2 * p + h + 1, :]
            col = cumx[:, h * head_size : h * head_size + 1]
            decay = jnp.exp(jnp.where(mask, row - col, -1e30))
            grad_scores = grad_scores + decay * products[h * CHUNK : (h + 1) * CHUNK, :]
            mixing.append(decay * scores)
        stacked = jnp.concatenate([jnp.where(first, dy, 0.0), jnp.where(first, 0.0, dy)], axis=0)
        inner = mul(jnp.concatenate(mixing, axis=1), stacked)
        decay_out = jnp.exp(cumx[CHUNK - 1 : CHUNK, :] - cumx)
        z_ref[:, at] = inner + decay_out * mul(inputs, g_ref[0, :, at])
    cumx = cumx_ref[...]
    scaled = x_ref[...] * dtx_ref[...] * jnp.exp(cumx[CHUNK - 1 : CHUNK, :] - cumx)
    entering = st_ref[0] + pre_ref[0, 0:1, :] * start_ref[...]
    reads = jnp.transpose(ct_ref[...])
    db_ref[...] = mul(grad_scores, reads) + mul(scaled, g_ref[0], NT)
    dc_ref[...] = mul(jnp.transpose(grad_scores), inputs) + mul(
        dy_ref[...] * jnp.exp(cumx), entering, NT
    )


def back_steps_kernel(
    head_size, x_ref, bt_ref, dtx_ref, cumx_ref, dt_ref, step_ref, coef_ref, skip_ref, mixed_ref,
    dy_ref, z_ref, db_ref, dc_ref, g_ref, later_ref, post_ref, end_ref, pre_ref, start_ref,
    dx_ref, dbt_ref, dct_ref, dstep_ref, gcoef_ref,
):
    width = x_ref.shape[1]

    @pl.when(pl.program_id(0) == 0)
    def _():
        gcoef_ref[...] = jnp.zeros_like(gcoef_ref)

    spread = head_mask(width, head_size)
    upper = jnp.where(order_mask(CHUNK, True), 1.0, 0.0).astype(jnp.bfloat16)
    x = x_ref[...]
    dy = dy_ref[...]
    cumx = cumx_ref[...]
    skip = skip_ref[0:1, :]
    dtx = dtx_ref[...]
    later = later_ref[...]
    post = post_ref[0, 0:1, :]
    inputs = jnp.transpose(bt_ref[...])
    decay_out = post * jnp.exp(cumx[CHUNK - 1 : CHUNK, :] - cumx)
    z = z_ref[...] + decay_out * mul(inputs, later)
    dx_ref[...] = dtx * z + skip * dy
    db = db_ref[...] + mul(x * dtx * decay_out, later, NT)
    dbt_ref[...] = jnp.transpose(db)
    dct_ref[...] = jnp.transpose(dc_ref[...])
    steps = dt_ref[...]
    by_step = mul_by_mask(x * z, spread, NT)
    by_out = mul_by_mask(dy * (mixed_ref[...] - skip * x), spread, NT)
    leaving = end_ref[0] + pre_ref[0, 0:1, :] * start_ref[...]
    held = jnp.sum((g_ref[0] + post * later) * leaving, axis=0, keepdims=True)
    held = mul_by_mask(jnp.broadcast_to(held, (8, width)), spread, NT)[0:1, :]
    by_decay = mul_mask(upper, by_out - steps * by_step) + held
    rate = -jnp.exp(coef_ref[1:2, :])
    back = (by_step + rate * by_decay) * sigmoid(step_ref[...] + coef_ref[0:1, :])
    dstep_ref[...] = back
    gcoef_ref[0:8, :] += jnp.broadcast_to(jnp.sum(back, axis=0, keepdims=True), (8, LANES))
    gcoef_ref[8:16, :] += jnp.broadcast_to(
        jnp.sum(by_decay * rate * steps, axis=0, keepdims=True), (8, LANES)
    )


def full(array_shape):
    zeros = (0,) * len(array_shape)
    return pl.BlockSpec(array_shape, lambda i: zeros)


def run(kernel, grid, in_specs, out_specs, out_shapes, args, scratch=(), flops=0):
    return call(kernel, grid, in_specs, out_specs, out_shapes, args, scratch, flops)


def call(kernel, grid, in_specs, out_specs, out_shapes, args, scratch, flops):
    moved = sum(a.size * a.dtype.itemsize for a in args) + sum(
        s.size * s.dtype.itemsize for s in out_shapes
    )
    return pl.pallas_call(
        kernel,
        grid=grid,
        in_specs=in_specs,
        out_specs=out_specs,
        out_shape=out_shapes,
        scratch_shapes=scratch,
        cost_estimate=pl.CostEstimate(flops=flops, bytes_accessed=moved, transcendentals=0),
        compiler_params=pltpu.CompilerParams(
            dimension_semantics=("arbitrary",) * len(grid), vmem_limit_bytes=48 * 2**20
        ),
    )(*args)


def contract(left, right, left_dim, right_dim):
    return lax.dot_general(
        left, right, (((left_dim,), (right_dim,)), ((), ())), preferred_element_type=jnp.float32
    )


def input_norm(source, gain):
    return (
        source * lax.rsqrt(jnp.mean(source * source, axis=1, keepdims=True) + norm_epsilon) * gain
    )


def convolve(padded, tap_table):
    tap_count = tap_table.shape[0] - 1
    length = padded.shape[0] - tap_count + 1
    total = jnp.broadcast_to(tap_table[tap_count], (length, tap_table.shape[1]))
    for offset in range(tap_count):
        total = total + tap_table[offset] * padded[offset : offset + length]
    return jax.nn.silu(total)


def adam_update(weight, gradient, moment_one, moment_two, step_rate):
    step, first_new, second_new = adam_step_of(weight, gradient, moment_one, moment_two, step_rate)
    return (weight - step, first_new, second_new)


def adam_step_of(weight, gradient, moment_one, moment_two, step_rate):
    first_new = beta_first * moment_one + (1.0 - beta_first) * gradient
    second_new = beta_second * moment_two + (1.0 - beta_second) * gradient * gradient
    first_hat = first_new / (1.0 - beta_first**adam_step)
    second_hat = second_new / (1.0 - beta_second**adam_step)
    step = step_rate * (
        first_hat / (jnp.sqrt(second_hat) + adam_epsilon) + weight_decay * weight
    )
    return (step, first_new, second_new)


def early_kernel(normed_ref, back_ref, grad_ref, normal_ref, out_ref):
    width = back_ref.shape[1]
    out_ref[:, :width] = dot(jnp.transpose(normed_ref[...]), back_ref[...], NN)
    out_ref[:, width:] = dot(jnp.transpose(grad_ref[...]), normal_ref[...], NN)


def early_gradients(normed, back_gate, output_grad, normal_out):
    length, rows = normed.shape
    width = back_gate.shape[1]
    block = 2 * CHUNK
    columns = pl.BlockSpec((length, block), lambda i: (0, i))
    return run(
        early_kernel,
        (rows // block,),
        [columns, full((length, width)), columns, full((length, width))],
        [pl.BlockSpec((block, 2 * width), lambda i: (i, 0))],
        [jax.ShapeDtypeStruct((rows, 2 * width), jnp.float32)],
        (normed, back_gate, output_grad, normal_out),
        flops=4 * length * rows * width,
    )[0]


def late_kernel(place_ref, normed_ref, back_ref, keep_ref, send_ref):
    product = dot(normed_ref[...], back_ref[...], NN)
    odd = lax.rem(pl.program_id(0), 2) == 1

    @pl.when(odd)
    def _():
        send_ref[0] = product

    @pl.when(jnp.logical_not(odd))
    def _():
        keep_ref[0] = product


def late_gradients(place, count, normed_lanes, back_late):
    rows, length = normed_lanes.shape
    width = back_late.shape[1]
    block = rows // count
    half = jax.ShapeDtypeStruct((count // 2, block, width), jnp.float32)
    half_spec = pl.BlockSpec((1, block, width), lambda i, place_ref: (i // 2, 0, 0))
    return pl.pallas_call(
        late_kernel,
        grid_spec=pltpu.PrefetchScalarGridSpec(
            num_scalar_prefetch=1,
            grid=(count,),
            in_specs=[
                pl.BlockSpec((block, length), lambda i, place_ref: (place_ref[0] ^ i, 0)),
                pl.BlockSpec((length, width), lambda i, place_ref: (0, 0)),
            ],
            out_specs=[half_spec, half_spec],
        ),
        out_shape=[half, half],
        cost_estimate=pl.CostEstimate(
            flops=2 * rows * length * width,
            bytes_accessed=4 * rows * width + 2 * length * (rows + width),
            transcendentals=0,
        ),
        compiler_params=pltpu.CompilerParams(
            dimension_semantics=("arbitrary",), vmem_limit_bytes=48 * 2**20
        ),
    )(jnp.full((1,), place, jnp.int32), normed_lanes, back_late)


def adam_turned_kernel(grad_ref, weight_ref, one_ref, two_ref, part_ref, sum_ref, first_ref, second_ref):
    gradient = jnp.transpose(grad_ref[...])
    updated, first_new, second_new = adam_update(
        weight_ref[...], gradient, one_ref[...], two_ref[...], rate_matrix
    )
    part_ref[...] = jnp.transpose(updated)
    sum_ref[...] = gradient
    first_ref[...] = first_new
    second_ref[...] = second_new


def adam_turned(gradient, weight, moment_one, moment_two):
    rows, columns = weight.shape
    whole = [full((rows, columns))] * 3
    shape = jax.ShapeDtypeStruct((rows, columns), jnp.float32)
    return run(
        adam_turned_kernel,
        (1,),
        [full((columns, rows))] + whole,
        [full((columns, rows))] + whole,
        [jax.ShapeDtypeStruct((columns, rows), jnp.float32)] + [shape] * 3,
        (gradient, weight, moment_one, moment_two),
    )


def turn_block_kernel(in_ref, out_ref):
    out_ref[...] = jnp.transpose(in_ref[...])


def turned(array):
    rows, columns = array.shape
    block = 2 * CHUNK
    return run(
        turn_block_kernel,
        (rows // block,),
        [pl.BlockSpec((block, columns), lambda i: (i, 0))],
        [pl.BlockSpec((columns, block), lambda i: (0, i))],
        [jax.ShapeDtypeStruct((columns, rows), array.dtype)],
        (array,),
    )[0]


def rows_of_eight(vector):
    return jnp.broadcast_to(vector[None, :], (8, vector.shape[0]))


def layer_step(
    layer_input, output_grad, norm_gain, proj_main, proj_state, proj_step, conv_main, conv_state,
    head_coef, gate_gain, proj_out, first_norm_gain, first_proj_main, first_proj_state,
    first_proj_step, first_conv_main, first_conv_state, first_head_coef, first_gate_gain,
    first_proj_out, second_norm_gain, second_proj_main, second_proj_state, second_proj_step,
    second_conv_main, second_conv_state, second_head_coef, second_gate_gain, second_proj_out,
):
    f32, bf16 = jnp.float32, jnp.bfloat16
    length, model_width = layer_input.shape
    local_heads = proj_step.shape[1]
    inner_width = proj_main.shape[2]
    head_size = inner_width // local_heads
    state_local = proj_state.shape[2]
    tap_count = conv_main.shape[0] - 1
    head_count = lax.axis_size("head")
    seq_count = lax.axis_size("seq")
    seq_index = lax.axis_index("seq")
    head_index = lax.axis_index("head")
    state_size = state_local * head_count
    full_inner = inner_width * head_count
    chunks = length // CHUNK
    chunk_row = pl.BlockSpec((CHUNK, inner_width), lambda i: (i, 0))
    chunk_lane = pl.BlockSpec((state_size, CHUNK), lambda i: (0, i))
    chunk_head = pl.BlockSpec((HEAD_ROWS, CHUNK), lambda i: (0, i))
    chunk_small = pl.BlockSpec((CHUNK, LANES), lambda i: (i, 0))
    chunk_state = pl.BlockSpec((CHUNK, state_size), lambda i: (i, 0))
    state_block = pl.BlockSpec((1, state_size, inner_width), lambda i: (i, 0, 0))
    next_state = pl.BlockSpec((1, state_size, inner_width), lambda i: (i + 1, 0, 0))
    row_block = pl.BlockSpec((1, 8, inner_width), lambda i: (i, 0, 0))
    next_row = pl.BlockSpec((1, 8, inner_width), lambda i: (i + 1, 0, 0))
    state_full = full((state_size, inner_width))
    row_full = full((8, inner_width))
    row_shape = jax.ShapeDtypeStruct((length, inner_width), f32)
    small_shape = jax.ShapeDtypeStruct((length, LANES), f32)
    state_shape = jax.ShapeDtypeStruct((state_size, inner_width), f32)
    scan_flops = 2 * 3 * length * inner_width * (2 * CHUNK + state_size)

    halo = 16
    rim = halo - (tap_count - 1)
    source = plain(layer_input.astype(f32))
    rim_source = from_behind(source[length - halo :], "seq", 1)
    normed = plain(input_norm(source, norm_gain).astype(bf16))
    normed_long = jnp.concatenate([input_norm(rim_source, norm_gain).astype(bf16), normed], axis=0)
    state_weight = proj_state.reshape(model_width, 2 * state_local).astype(bf16)
    step_weight = proj_step.astype(bf16)
    step_wide = jnp.pad(step_weight, ((0, 0), (0, LANES - local_heads)))
    out_weight = after(proj_out.astype(bf16))
    coef_wide = jnp.pad(head_coef, ((0, 8 - head_coef.shape[0]), (0, LANES - local_heads)))
    skip_wide = rows_of_eight(jnp.repeat(head_coef[2], head_size))
    gain_wide = rows_of_eight(gate_gain)

    state_pre = jnp.dot(normed_long, state_weight, preferred_element_type=f32)
    state_taps = conv_state.reshape(tap_count + 1, 2 * state_local)
    state_active, state_pull = jax.vjp(convolve, state_pre[rim:], state_taps)
    state_lanes = state_active.T
    pair_lanes = ring_gather(state_lanes, "head")
    halves = after(jnp.transpose(proj_main, (1, 0, 2)).astype(bf16), state_lanes)
    gate_weight, value_weight = halves[0], halves[1]
    value_pre = jnp.dot(normed_long, value_weight, preferred_element_type=f32)
    values, value_pull = jax.vjp(convolve, value_pre[rim:], conv_main)
    step_pre = jnp.dot(normed, step_wide, preferred_element_type=f32)
    gate_pre = jnp.dot(normed, gate_weight, preferred_element_type=f32)
    pair_lanes = pair_lanes.reshape(head_count, 2, state_local, length)
    input_lanes = pair_lanes[:, 0].reshape(state_size, length)
    output_lanes = pair_lanes[:, 1].reshape(state_size, length)

    steps, steps_wide, cum_wide, cum_lanes, states, before, beyond = run(
        functools.partial(states_kernel, head_size),
        (1,),
        [full(a.shape) for a in (values, input_lanes, step_pre, coef_wide)],
        [
            full((length, LANES)),
            full((length, inner_width)),
            full((length, inner_width)),
            full((HEAD_ROWS, length)),
            full((chunks + 1, state_size, inner_width)),
            full((chunks + 1, 8, inner_width)),
            full((chunks, 8, inner_width)),
        ],
        [
            small_shape,
            row_shape,
            row_shape,
            jax.ShapeDtypeStruct((HEAD_ROWS, length), f32),
            jax.ShapeDtypeStruct((chunks + 1, state_size, inner_width), f32),
            jax.ShapeDtypeStruct((chunks + 1, 8, inner_width), f32),
            jax.ShapeDtypeStruct((chunks, 8, inner_width), f32),
        ],
        (values, input_lanes, step_pre, coef_wide),
        flops=scan_flops // 3,
    )
    through = before[chunks, 0:1]
    start_state = carried_state(through, states[chunks], "seq", False)
    local_out = run(
        functools.partial(within_kernel, head_size),
        (chunks,),
        [chunk_row, chunk_lane, chunk_lane, chunk_row, chunk_row, chunk_head, state_block],
        [chunk_row],
        [row_shape],
        (values, input_lanes, output_lanes, steps_wide, cum_wide, cum_lanes, states),
        flops=scan_flops,
    )[0]
    back_normal = contract(output_grad, out_weight, 1, 1)
    mixed, sums = run(
        gate_kernel,
        (chunks,),
        [
            chunk_row, chunk_lane, chunk_row, row_block, state_full, chunk_row, row_full,
            chunk_row, chunk_row, row_full,
        ],
        [chunk_row, pl.BlockSpec((16, CHUNK), lambda i: (0, i))],
        [row_shape, jax.ShapeDtypeStruct((16, length), f32)],
        (
            local_out, output_lanes, cum_wide, before, start_state, values, skip_wide,
            gate_pre, back_normal, gain_wide,
        ),
        flops=scan_flops // 4,
    )
    sums = sum_all(sums, "head")
    reverse_row = pl.BlockSpec((CHUNK, inner_width), lambda i: (chunks - 1 - i, 0))
    reverse_lane = pl.BlockSpec((state_size, CHUNK), lambda i: (0, chunks - 1 - i))
    normal_out, back_mixed, back_gate, grad_gate, grad_skip, later_local, state_jump = run(
        functools.partial(turn_kernel, float(full_inner)),
        (chunks,),
        [
            pl.BlockSpec((16, CHUNK), lambda i: (0, chunks - 1 - i)),
            reverse_row, reverse_row, reverse_row, row_full, reverse_row, reverse_row,
            reverse_lane, row_full,
        ],
        [
            reverse_row, reverse_row, reverse_row, row_full, row_full,
            pl.BlockSpec((1, state_size, inner_width), lambda i: (chunks - 1 - i, 0, 0)),
            state_full,
        ],
        [
            jax.ShapeDtypeStruct((length, inner_width), bf16),
            row_shape,
            jax.ShapeDtypeStruct((length, inner_width), bf16),
            jax.ShapeDtypeStruct((8, inner_width), f32),
            jax.ShapeDtypeStruct((8, inner_width), f32),
            jax.ShapeDtypeStruct((chunks, state_size, inner_width), f32),
            state_shape,
        ],
        (
            sums, mixed, gate_pre, back_normal, gain_wide, values, cum_wide, output_lanes,
            skip_wide,
        ),
        scratch=[pltpu.VMEM((state_size, inner_width), f32)],
        flops=scan_flops // 4,
    )
    later_grad = carried_state(through, state_jump, "seq", True)

    col_count = model_width // head_count

    def out_block(index):
        columns = lax.dynamic_slice_in_dim(out_weight, index * col_count, col_count, 1)
        return plain(jnp.dot(normal_out, columns, preferred_element_type=f32))

    out_cols, out_sent = line_scatter(out_block, "head")
    sum_early = scatter_rows(
        early_gradients(normed, back_gate, output_grad, after(normal_out, *out_sent[0])), "seq"
    )
    back_tied = after(back_mixed, *out_sent[1])
    z_local, db_local, dc_local = run(
        functools.partial(back_within_kernel, head_size),
        (chunks,),
        [
            chunk_row, chunk_lane, chunk_lane, chunk_row, chunk_row, chunk_head, state_block,
            row_block, state_full, chunk_row, state_block,
        ],
        [chunk_row, chunk_state, chunk_state],
        [
            row_shape,
            jax.ShapeDtypeStruct((length, state_size), f32),
            jax.ShapeDtypeStruct((length, state_size), f32),
        ],
        (
            values, input_lanes, output_lanes, steps_wide, cum_wide, cum_lanes, states, before,
            start_state, back_tied, later_local,
        ),
        flops=2 * scan_flops,
    )
    z_local = after(z_local, *out_sent[2])
    back_values, back_in, back_out, back_step_pre, grad_coef_rows = run(
        functools.partial(back_steps_kernel, head_size),
        (chunks,),
        [
            chunk_row, chunk_lane, chunk_row, chunk_row, chunk_small, chunk_small,
            full(coef_wide.shape), row_full, chunk_row, chunk_row, chunk_row, chunk_state,
            chunk_state, state_block, state_full, row_block, next_state, next_row, state_full,
        ],
        [chunk_row, chunk_lane, chunk_lane, chunk_small, full((16, LANES))],
        [
            row_shape,
            jax.ShapeDtypeStruct((state_size, length), f32),
            jax.ShapeDtypeStruct((state_size, length), f32),
            small_shape,
            jax.ShapeDtypeStruct((16, LANES), f32),
        ],
        (
            values, input_lanes, steps_wide, cum_wide, steps, step_pre, coef_wide, skip_wide,
            mixed, back_mixed, z_local, db_local, dc_local, later_local, later_grad, beyond, states,
            before, start_state,
        ),
        flops=scan_flops // 2,
    )
    grad_coef = jnp.stack(
        [
            grad_coef_rows[0, :local_heads],
            grad_coef_rows[8, :local_heads],
            jnp.sum(grad_skip[0].reshape(local_heads, head_size), axis=1),
        ]
    )
    back_pair = jnp.stack([back_in, back_out]).reshape(2, head_count, state_local, length)

    def pair_block(index):
        return lax.dynamic_index_in_dim(back_pair, index, 1, False)

    back_local_pair = pair_block(head_index)
    for by in range(1, head_count):
        back_local_pair = back_local_pair + shift(
            pair_block(lax.rem(head_index + by, head_count)), "head", by
        )
    value_padded, value_taps_grad = value_pull(back_values)
    state_padded, state_taps_grad = state_pull(
        back_local_pair.reshape(2 * state_local, length).T
    )
    grad_taps = jnp.concatenate([value_taps_grad, state_taps_grad], axis=1)
    back_padded = jnp.concatenate([value_padded, state_padded], axis=1)
    rim_back = from_behind(back_padded[: tap_count - 1], "seq", -1)
    back_conv = back_padded[tap_count - 1 :]
    rim_start = length - tap_count + 1
    back_conv = jnp.concatenate([back_conv[:rim_start], back_conv[rim_start:] + rim_back], axis=0)
    back_late = jnp.concatenate([back_conv, back_step_pre[:, :local_heads]], axis=1).astype(bf16)
    residual_cols = lax.dynamic_slice_in_dim(source, head_index * col_count, col_count, 1)
    layer_output = plain((residual_cols + out_cols).astype(bf16))
    late_weight = jnp.concatenate([value_weight, state_weight, step_weight], axis=1)
    shard_rows = length // head_count

    row_size = lax.rsqrt(jnp.mean(source * source, axis=1, keepdims=True) + norm_epsilon)
    unit = source * row_size
    grad_gain = []

    def normed_block(index):
        gate_rows = lax.dynamic_slice_in_dim(back_gate, index * shard_rows, shard_rows, 0)
        late_rows = lax.dynamic_slice_in_dim(back_late, index * shard_rows, shard_rows, 0)
        block = contract(gate_rows, gate_weight, 1, 1) + contract(late_rows, late_weight, 1, 1)
        unit_rows = lax.dynamic_slice_in_dim(unit, index * shard_rows, shard_rows, 0)
        block = plain(after(block))
        grad_gain.append(jnp.sum(block * unit_rows, axis=0))
        return block

    back_normed, normed_sent = line_scatter(normed_block, "head")
    late_keep, late_send = late_gradients(
        seq_index, seq_count, normed.T, after(back_late, out_cols, *normed_sent[0])
    )
    sum_late = scatter_relative(late_keep, late_send, "seq", normed_sent[1])
    sum_late = after(sum_late, *normed_sent[2])
    sum_early = after(sum_early, *normed_sent[0])
    sum_gate_half = sum_early[:, :inner_width]
    sum_out_turned = sum_early[:, inner_width:]
    own_source = lax.dynamic_slice_in_dim(source, head_index * shard_rows, shard_rows, 0)
    _, norm_pull = jax.vjp(lambda rows: input_norm(rows, norm_gain), own_source)
    (back_source,) = norm_pull(back_normed)

    def own_rows(array, along):
        piece_len = array.shape[along] // seq_count
        return lax.dynamic_slice_in_dim(array, seq_index * piece_len, piece_len, along)

    part_out, sum_out, first_out, second_out = adam_turned(
        sum_out_turned, own_rows(proj_out, 1), first_proj_out, second_proj_out
    )
    new_out = turned(gather_rows(part_out, "seq"))

    sum_main = jnp.stack([sum_gate_half, sum_late[:, :inner_width]], axis=1)
    step_main, first_main, second_main = adam_step_of(
        own_rows(proj_main, 0), sum_main, first_proj_main, second_proj_main, rate_matrix
    )
    step_main = plain(gather_rows(plain(step_main), "seq"))
    new_main = proj_main - step_main
    new_main = plain(new_main)
    sum_state = sum_late[:, inner_width : inner_width + 2 * state_local]
    part_state, first_state, second_state = adam_update(
        own_rows(proj_state, 0).reshape(-1, 2 * state_local),
        sum_state,
        first_proj_state.reshape(-1, 2 * state_local),
        second_proj_state.reshape(-1, 2 * state_local),
        rate_matrix,
    )
    sum_step = sum_late[:, inner_width + 2 * state_local :]
    part_step, first_step, second_step = adam_update(
        own_rows(proj_step, 0), sum_step, first_proj_step, second_proj_step, rate_matrix
    )
    new_small = gather_small(jnp.concatenate([part_state, part_step], axis=1), "seq")
    new_state = new_small[:, : 2 * state_local].reshape(model_width, 2, state_local)
    new_step = new_small[:, 2 * state_local :]
    state_form = (-1, 2, state_local)

    taps_wide = inner_width + 2 * state_local
    gain_rows = sum_of(grad_gain).reshape(8, model_width // 8)
    small = jnp.concatenate(
        [
            grad_taps.reshape(-1),
            grad_gate[0],
            grad_coef.reshape(-1),
        ]
    )
    small_size = small.shape[0]
    padded_size = -(-small_size // 1024) * 1024
    small = jnp.pad(small, (0, padded_size - small_size)).reshape(8, padded_size // 8)
    small = sum_all(jnp.concatenate([small, gain_rows], axis=1), "seq")
    sum_gain = small[:, padded_size // 8 :]
    for bit in bits_of("head"):
        got_gain = swap(sum_gain, "head", bit)
        sum_gain = sum_gain + got_gain
    sum_gain = sum_gain.reshape(-1)
    small = small[:, : padded_size // 8].reshape(-1)
    taps_size = (tap_count + 1) * taps_wide
    sum_taps = small[:taps_size].reshape(tap_count + 1, taps_wide)
    back_rows, _ = line_gather(after(back_source, sum_gain), "head")
    back_rows = back_rows.reshape(length, model_width)
    input_grad = plain((output_grad.astype(f32) + plain(back_rows)).astype(bf16))
    sum_cmain = sum_taps[:, :inner_width]
    sum_cstate = sum_taps[:, inner_width:].reshape(tap_count + 1, 2, state_local)
    sum_gate = small[taps_size : taps_size + inner_width]
    sum_coef = small[taps_size + inner_width : small_size].reshape(3, local_heads)
    new_gain, first_gain, second_gain = adam_update(
        norm_gain, sum_gain, first_norm_gain, second_norm_gain, rate_vector
    )
    new_cmain, first_cmain, second_cmain = adam_update(
        conv_main, sum_cmain, first_conv_main, second_conv_main, rate_vector
    )
    new_cstate, first_cstate, second_cstate = adam_update(
        conv_state, sum_cstate, first_conv_state, second_conv_state, rate_vector
    )
    new_coef, first_coef, second_coef = adam_update(
        head_coef, sum_coef, first_head_coef, second_head_coef, rate_coef
    )
    new_gate, first_gate, second_gate = adam_update(
        gate_gain, sum_gate, first_gate_gain, second_gate_gain, rate_vector
    )
    return (
        layer_output, input_grad, sum_gain, sum_main, sum_state.reshape(state_form), sum_step,
        sum_cmain, sum_cstate, sum_coef, sum_gate, sum_out, new_gain, new_main, new_state,
        new_step, new_cmain, new_cstate, new_coef, new_gate, new_out, first_gain, first_main,
        first_state.reshape(state_form), first_step, first_cmain, first_cstate, first_coef,
        first_gate, first_out, second_gain, second_main, second_state.reshape(state_form),
        second_step, second_cmain, second_cstate, second_coef, second_gate, second_out,
    )


def solution(mesh):
    return jax.shard_map(
        layer_step,
        mesh=mesh,
        in_specs=(
            P("seq", None),
            P("seq", None),
            P(),
            P(None, None, "head"),
            P(None, None, "head"),
            P(None, "head"),
            P(None, "head"),
            P(None, None, "head"),
            P(None, "head"),
            P("head"),
            P("head", None),
            P(),
            P("seq", None, "head"),
            P("seq", None, "head"),
            P("seq", "head"),
            P(None, "head"),
            P(None, None, "head"),
            P(None, "head"),
            P("head"),
            P("head", "seq"),
            P(),
            P("seq", None, "head"),
            P("seq", None, "head"),
            P("seq", "head"),
            P(None, "head"),
            P(None, None, "head"),
            P(None, "head"),
            P("head"),
            P("head", "seq"),
        ),
        out_specs=(
            P("seq", "head"),
            P("seq", None),
            P(),
            P("seq", None, "head"),
            P("seq", None, "head"),
            P("seq", "head"),
            P(None, "head"),
            P(None, None, "head"),
            P(None, "head"),
            P("head"),
            P("head", "seq"),
            P(),
            P(None, None, "head"),
            P(None, None, "head"),
            P(None, "head"),
            P(None, "head"),
            P(None, None, "head"),
            P(None, "head"),
            P("head"),
            P("head", None),
            P(),
            P("seq", None, "head"),
            P("seq", None, "head"),
            P("seq", "head"),
            P(None, "head"),
            P(None, None, "head"),
            P(None, "head"),
            P("head"),
            P("head", "seq"),
            P(),
            P("seq", None, "head"),
            P("seq", None, "head"),
            P("seq", "head"),
            P(None, "head"),
            P(None, None, "head"),
            P(None, "head"),
            P("head"),
            P("head", "seq"),
        ),
        check_vma=False,
    )
```

```python
import functools

import jax
import jax.numpy as jnp
from jax import lax
from jax.experimental import pallas as pl
from jax.experimental.layout import Layout, with_layout_constraint
from jax.experimental.pallas import tpu as pltpu
from jax.sharding import PartitionSpec as P


CHUNK = 128
LANES = 128
HEAD_ROWS = 16

norm_epsilon = 1e-05
beta_first = 0.9
beta_second = 0.95
adam_epsilon = 1e-08
weight_decay = 0.1
adam_step = 2
rate_matrix = 0.005
rate_vector = 0.15
rate_coef = 0.6

NN = ((1,), (0,))
NT = ((1,), (1,))


def swap(value, axis, bit):
    return lax.ppermute(value, axis, [(i, i ^ bit) for i in range(lax.axis_size(axis))])


def shift(value, axis, by):
    count = lax.axis_size(axis)
    return lax.ppermute(value, axis, [(i, (i + by) % count) for i in range(count)])


def from_behind(value, axis, by):
    devices = lax.axis_size(axis)
    pairs = [(i, i + by) for i in range(devices) if 0 <= i + by < devices]
    return lax.ppermute(value, axis, pairs)


def bits_of(axis):
    count, bits = lax.axis_size(axis), []
    while 2 ** len(bits) < count:
        bits.append(2 ** len(bits))
    return bits


def sum_all(value, axis):
    for bit in bits_of(axis):
        value = value + swap(value, axis, bit)
    return value


def bit_of(axis, bit):
    return (lax.axis_index(axis) // bit) % 2


def scatter_rows(value, axis):
    return lax.psum_scatter(value, axis, scatter_dimension=0, tiled=True)


def scatter_relative(keep, send, axis, ahead):
    bits = bits_of(axis)
    rows = keep.shape[1]
    got = swap(send, axis, bits[0])
    dims = (2,) * (len(bits) - 1)
    keep = keep.reshape(dims + keep.shape[1:])
    got = got.reshape(dims + got.shape[1:])
    cuts = [(0, rows // 2), (rows // 2, rows)]
    orders = [bits[1:], bits[1:][::-1]]
    pieces = []
    for (low, high), order in zip(cuts, orders):
        left = list(bits[1:])
        mine = [lax.slice_in_dim(a, low, high, axis=len(dims)) for a in (keep, got)]
        for bit in order:
            dim = len(left) - 1 - left.index(bit)
            sent = sum_of([lax.index_in_dim(a, 1, dim, False) for a in mine])
            held = [lax.index_in_dim(a, 0, dim, False) for a in mine]
            moved = swap(sent, axis, bit)
            mine = [sum_of(held), after(moved, *ahead) if bit == order[0] else moved]
            left.remove(bit)
        pieces.append(sum_of(mine))
    return jnp.concatenate(pieces, axis=0)


def sum_of(parts):
    return functools.reduce(jnp.add, parts)


def gather_rows(value, axis):
    return lax.all_gather(value, axis, axis=0, tiled=True)


def gather_small(value, axis):
    place = lax.axis_index(axis)
    rows = value.shape[0]
    whole = jnp.zeros((lax.axis_size(axis) * rows,) + value.shape[1:], value.dtype)
    whole = lax.dynamic_update_slice_in_dim(whole, value, place * rows, 0)
    for bit in bits_of(axis):
        base = (place // bit) * bit
        block = lax.dynamic_slice_in_dim(whole, base * rows, bit * rows, 0)
        other = swap(block, axis, bit)
        start = jnp.where(bit_of(axis, bit) == 0, base + bit, base - bit)
        whole = lax.dynamic_update_slice_in_dim(whole, other, start * rows, 0)
    return whole


def plain(value):
    return with_layout_constraint(value, Layout(tuple(range(value.ndim))))


def after(value, *others):
    return lax.optimization_barrier((value,) + others)[0]


def line_scatter(block_of, axis):
    count, place = lax.axis_size(axis), lax.axis_index(axis)
    blocks = {}

    def term(offset):
        offset = offset % count
        if offset not in blocks:
            blocks[offset] = block_of(lax.rem(place + offset, count))
        return blocks[offset]

    right, left = term(-1), term(1)
    sent = []
    for step in range(1, count):
        sent.append((right, left))
        got_right = lax.ppermute(right, axis, [(i, i + 1) for i in range(step)])
        got_left = lax.ppermute(left, axis, [(count - 1 - i, count - 2 - i) for i in range(step)])
        if step < count - 1:
            right = got_right + term(-step - 1)
            left = got_left + after(term(step + 1))
    return after(term(0)) + got_right + got_left, sent


def line_gather(value, axis):
    count, place = lax.axis_size(axis), lax.axis_index(axis)
    right = left = value
    from_left, from_right = [], []
    for step in range(1, count):
        right = lax.ppermute(right, axis, [(i, i + 1) for i in range(step - 1, count - 1)])
        left = lax.ppermute(left, axis, [(i + 1, i) for i in range(count - step)])
        from_left.append(right)
        from_right.append(left)
    sent = list(zip(from_left[:-1], from_right[:-1]))
    whole = jnp.zeros((count,) + value.shape, value.dtype)
    whole = lax.dynamic_update_index_in_dim(whole, value, place, 0)
    for step in range(1, count):
        block = jnp.where(place >= step, from_left[step - 1], from_right[count - step - 1])
        whole = lax.dynamic_update_index_in_dim(
            whole, block, lax.rem(place + count - step, count), 0
        )
    return whole, sent


def ring_gather(value, axis):
    count, place = lax.axis_size(axis), lax.axis_index(axis)
    whole = jnp.zeros((count,) + value.shape, value.dtype)
    whole = lax.dynamic_update_index_in_dim(whole, value, place, 0)
    for by in range(1, count):
        whole = lax.dynamic_update_index_in_dim(
            whole, shift(value, axis, by), lax.rem(place + count - by, count), 0
        )
    return whole


def carried_state(decay, part, axis, reverse):
    bits = bits_of(axis)
    half = part.shape[0] // 2
    mine = bit_of(axis, bits[0])

    def later_of(bit):
        high = bit_of(axis, bit) == 1
        return jnp.logical_not(high) if reverse else high

    other = swap(part, axis, bits[0])
    other_decay = swap(decay, axis, bits[0])
    own_half = lax.dynamic_slice_in_dim(part, mine * half, half, 0)
    other_half = lax.dynamic_slice_in_dim(other, mine * half, half, 0)
    later = later_of(bits[0])
    total = jnp.where(
        later, own_half + decay * other_half, other_half + other_decay * own_half
    )
    total_decay = decay * other_decay
    before, before_decay = jnp.zeros_like(total), jnp.ones_like(decay)
    for bit in bits[1:]:
        got, got_decay = swap(total, axis, bit), swap(total_decay, axis, bit)
        ahead = later_of(bit)
        before = jnp.where(ahead, before + before_decay * got, before)
        before_decay = jnp.where(ahead, before_decay * got_decay, before_decay)
        if bit != bits[-1]:
            total = jnp.where(ahead, total + total_decay * got, got + got_decay * total)
            total_decay = total_decay * got_decay
    rest = swap(before, axis, bits[0])
    whole = jnp.concatenate(
        [jnp.where(mine == 0, before, rest), jnp.where(mine == 0, rest, before)], axis=0
    )
    return jnp.where(later, other + other_decay * whole, whole)


def dot(left, right, dims):
    return lax.dot_general(left, right, (dims, ((), ())), preferred_element_type=jnp.float32)


def two(value):
    high = value.astype(jnp.bfloat16)
    return high, (value - high.astype(jnp.float32)).astype(jnp.bfloat16)


def three(value):
    high = value.astype(jnp.bfloat16)
    rest = value - high.astype(jnp.float32)
    mid = rest.astype(jnp.bfloat16)
    return high, mid, (rest - mid.astype(jnp.float32)).astype(jnp.bfloat16)


def mul(left, right, dims=NN):
    (lh, ll), (rh, rl) = two(left), two(right)
    return dot(lh, rh, dims) + (dot(lh, rl, dims) + dot(ll, rh, dims))


def mul_mask(mask, value, dims=NN):
    high, mid, low = three(value)
    return dot(mask, high, dims) + (dot(mask, mid, dims) + dot(mask, low, dims))


def mul_by_mask(value, mask, dims=NN):
    high, mid, low = three(value)
    return dot(high, mask, dims) + (dot(mid, mask, dims) + dot(low, mask, dims))


def head_mask(width, head_size):
    row = lax.broadcasted_iota(jnp.int32, (LANES, width), 0)
    col = lax.broadcasted_iota(jnp.int32, (LANES, width), 1)
    low = row * head_size
    return jnp.where((col >= low) & (col < low + head_size), 1.0, 0.0).astype(jnp.bfloat16)


def order_mask(size, upper):
    row = lax.broadcasted_iota(jnp.int32, (size, size), 0)
    col = lax.broadcasted_iota(jnp.int32, (size, size), 1)
    return (row <= col) if upper else (row >= col)


def soft_plus(value):
    return jnp.maximum(value, 0.0) + jnp.log1p(jnp.exp(-jnp.abs(value)))


def sigmoid(value):
    return 1.0 / (1.0 + jnp.exp(-value))


def states_kernel(
    head_size, x_ref, bt_ref, step_ref, coef_ref,
    dt_ref, dtx_ref, cumx_ref, cumt_ref, st_ref, pre_ref, post_ref,
):
    length, width = x_ref.shape
    count = length // CHUNK
    spread = head_mask(width, head_size)
    lower = jnp.where(order_mask(CHUNK, False), 1.0, 0.0).astype(jnp.bfloat16)
    state = jnp.zeros((bt_ref.shape[0], width), jnp.float32)
    run = jnp.zeros((1, width), jnp.float32)
    rate = -jnp.exp(coef_ref[1:2, :])
    bias = coef_ref[0:1, :]
    runs = []
    for c in range(count):
        at = slice(c * CHUNK, (c + 1) * CHUNK)
        steps = soft_plus(step_ref[at, :] + bias)
        cum = mul_mask(lower, rate * steps)
        dtx = mul_by_mask(steps, spread)
        cumx = mul_by_mask(cum, spread)
        dt_ref[at, :] = steps
        dtx_ref[at, :] = dtx
        cumx_ref[at, :] = cumx
        cumt_ref[:, at] = jnp.transpose(cum)[:HEAD_ROWS, :]
        total = cumx[CHUNK - 1 : CHUNK, :]
        st_ref[c] = state
        pre_ref[c] = jnp.broadcast_to(jnp.exp(run), (8, width))
        state = jnp.exp(total) * state + mul(
            bt_ref[:, at], x_ref[at, :] * dtx * jnp.exp(total - cumx)
        )
        run = run + total
        runs.append(total)
    st_ref[count] = state
    pre_ref[count] = jnp.broadcast_to(jnp.exp(run), (8, width))
    rest = jnp.zeros((1, width), jnp.float32)
    for c in range(count - 1, -1, -1):
        post_ref[c] = jnp.broadcast_to(jnp.exp(rest), (8, width))
        rest = rest + runs[c]


def lane_halves(size, width):
    return lax.broadcasted_iota(jnp.int32, (size, width), 1) < width // 2


def within_kernel(head_size, x_ref, bt_ref, ct_ref, dtx_ref, cumx_ref, cumt_ref, st_ref, y_ref):
    width = x_ref.shape[1]
    pair = 2 * head_size
    reads = jnp.transpose(ct_ref[...])
    scores = mul(reads, bt_ref[...])
    mask = order_mask(CHUNK, False)
    first = lane_halves(CHUNK, pair)
    for p in range(width // pair):
        at = slice(p * pair, (p + 1) * pair)
        cumx = cumx_ref[:, at]
        scaled = x_ref[:, at] * dtx_ref[:, at]
        mixing = []
        for h in range(2):
            row = cumt_ref[2 * p + h : 2 * p + h + 1, :]
            col = cumx[:, h * head_size : h * head_size + 1]
            mixing.append(jnp.exp(jnp.where(mask, col - row, -1e30)) * scores)
        stacked = jnp.concatenate(
            [jnp.where(first, scaled, 0.0), jnp.where(first, 0.0, scaled)], axis=0
        )
        inner = mul(jnp.concatenate(mixing, axis=1), stacked)
        y_ref[:, at] = inner + jnp.exp(cumx) * mul(reads, st_ref[0, :, at])


def gate_kernel(
    y_ref, ct_ref, cumx_ref, pre_ref, start_ref, x_ref, skip_ref, gate_ref, back_ref, gain_ref,
    mixed_ref, sums_ref,
):
    width = x_ref.shape[1]
    reads = jnp.transpose(ct_ref[...])
    carried = jnp.exp(cumx_ref[...]) * pre_ref[0, 0:1, :] * mul(reads, start_ref[...])
    mixed = y_ref[...] + carried + skip_ref[0:1, :] * x_ref[...]
    gate = gate_ref[...]
    gated = mixed * (gate * sigmoid(gate))
    mixed_ref[...] = mixed
    ones = jnp.ones((8, width), jnp.bfloat16)
    sums_ref[0:8, :] = mul_mask(ones, gated * gated, NT)
    sums_ref[8:16, :] = mul_mask(ones, back_ref[...] * gain_ref[0:1, :] * gated, NT)


def turn_kernel(
    full_inner, sums_ref, mixed_ref, gate_ref, back_ref, gain_ref, x_ref, cumx_ref, ct_ref,
    skip_ref,
    normal_ref, dy_ref, bgate_ref, ggate_ref, gskip_ref, g_ref, jump_ref, carry_ref,
):
    step = pl.program_id(0)

    @pl.when(step == 0)
    def _():
        carry_ref[...] = jnp.zeros_like(carry_ref)
        ggate_ref[...] = jnp.zeros_like(ggate_ref)
        gskip_ref[...] = jnp.zeros_like(gskip_ref)

    columns = jnp.transpose(sums_ref[...])
    scale = lax.rsqrt(columns[:, 0:1] / full_inner + norm_epsilon)
    inner = columns[:, 8:9] / full_inner
    mixed = mixed_ref[...]
    gate = gate_ref[...]
    share = sigmoid(gate)
    act = gate * share
    gated = mixed * act
    gain = gain_ref[0:1, :]
    back = back_ref[...]
    scaled = gated * scale
    normal_ref[...] = (scaled * gain).astype(jnp.bfloat16)
    back_gated = scale * (back * gain) - gated * (scale * scale * scale) * inner
    dy = back_gated * act
    dy_ref[...] = dy
    bgate_ref[...] = (back_gated * mixed * (share * (1.0 + gate * (1.0 - share)))).astype(
        jnp.bfloat16
    )
    ggate_ref[...] += jnp.broadcast_to(
        jnp.sum(back * scaled, axis=0, keepdims=True), ggate_ref.shape
    )
    gskip_ref[...] += jnp.broadcast_to(
        jnp.sum(dy * x_ref[...], axis=0, keepdims=True), gskip_ref.shape
    )
    carry = carry_ref[...]
    g_ref[0] = carry
    cumx = cumx_ref[...]
    carry = jnp.exp(cumx[CHUNK - 1 : CHUNK, :]) * carry + mul(ct_ref[...], dy * jnp.exp(cumx))
    carry_ref[...] = carry
    jump_ref[...] = carry


def back_within_kernel(
    head_size, x_ref, bt_ref, ct_ref, dtx_ref, cumx_ref, cumt_ref, st_ref, pre_ref, start_ref,
    dy_ref, g_ref,
    z_ref, db_ref, dc_ref,
):
    width = x_ref.shape[1]
    pair = 2 * head_size
    inputs = jnp.transpose(bt_ref[...])
    scores = mul(inputs, ct_ref[...])
    mask = order_mask(CHUNK, True)
    first = lane_halves(CHUNK, pair)
    grad_scores = jnp.zeros((CHUNK, CHUNK), jnp.float32)
    for p in range(width // pair):
        at = slice(p * pair, (p + 1) * pair)
        cumx = cumx_ref[:, at]
        dy = dy_ref[:, at]
        scaled = x_ref[:, at] * dtx_ref[:, at]
        products = mul(
            jnp.concatenate(
                [jnp.where(first, scaled, 0.0), jnp.where(first, 0.0, scaled)], axis=0
            ),
            dy,
            NT,
        )
        mixing = []
        for h in range(2):
            row = cumt_ref[2 * p + h : 2 * p + h + 1, :]
            col = cumx[:, h * head_size : h * head_size + 1]
            decay = jnp.exp(jnp.where(mask, row - col, -1e30))
            grad_scores = grad_scores + decay * products[h * CHUNK : (h + 1) * CHUNK, :]
            mixing.append(decay * scores)
        stacked = jnp.concatenate([jnp.where(first, dy, 0.0), jnp.where(first, 0.0, dy)], axis=0)
        inner = mul(jnp.concatenate(mixing, axis=1), stacked)
        decay_out = jnp.exp(cumx[CHUNK - 1 : CHUNK, :] - cumx)
        z_ref[:, at] = inner + decay_out * mul(inputs, g_ref[0, :, at])
    cumx = cumx_ref[...]
    scaled = x_ref[...] * dtx_ref[...] * jnp.exp(cumx[CHUNK - 1 : CHUNK, :] - cumx)
    entering = st_ref[0] + pre_ref[0, 0:1, :] * start_ref[...]
    reads = jnp.transpose(ct_ref[...])
    db_ref[...] = mul(grad_scores, reads) + mul(scaled, g_ref[0], NT)
    dc_ref[...] = mul(jnp.transpose(grad_scores), inputs) + mul(
        dy_ref[...] * jnp.exp(cumx), entering, NT
    )


def back_steps_kernel(
    head_size, x_ref, bt_ref, dtx_ref, cumx_ref, dt_ref, step_ref, coef_ref, skip_ref, mixed_ref,
    dy_ref, z_ref, db_ref, dc_ref, g_ref, later_ref, post_ref, end_ref, pre_ref, start_ref,
    dx_ref, dbt_ref, dct_ref, dstep_ref, gcoef_ref,
):
    width = x_ref.shape[1]

    @pl.when(pl.program_id(0) == 0)
    def _():
        gcoef_ref[...] = jnp.zeros_like(gcoef_ref)

    spread = head_mask(width, head_size)
    upper = jnp.where(order_mask(CHUNK, True), 1.0, 0.0).astype(jnp.bfloat16)
    x = x_ref[...]
    dy = dy_ref[...]
    cumx = cumx_ref[...]
    skip = skip_ref[0:1, :]
    dtx = dtx_ref[...]
    later = later_ref[...]
    post = post_ref[0, 0:1, :]
    inputs = jnp.transpose(bt_ref[...])
    decay_out = post * jnp.exp(cumx[CHUNK - 1 : CHUNK, :] - cumx)
    z = z_ref[...] + decay_out * mul(inputs, later)
    dx_ref[...] = dtx * z + skip * dy
    db = db_ref[...] + mul(x * dtx * decay_out, later, NT)
    dbt_ref[...] = jnp.transpose(db)
    dct_ref[...] = jnp.transpose(dc_ref[...])
    steps = dt_ref[...]
    by_step = mul_by_mask(x * z, spread, NT)
    by_out = mul_by_mask(dy * (mixed_ref[...] - skip * x), spread, NT)
    leaving = end_ref[0] + pre_ref[0, 0:1, :] * start_ref[...]
    held = jnp.sum((g_ref[0] + post * later) * leaving, axis=0, keepdims=True)
    held = mul_by_mask(jnp.broadcast_to(held, (8, width)), spread, NT)[0:1, :]
    by_decay = mul_mask(upper, by_out - steps * by_step) + held
    rate = -jnp.exp(coef_ref[1:2, :])
    back = (by_step + rate * by_decay) * sigmoid(step_ref[...] + coef_ref[0:1, :])
    dstep_ref[...] = back
    gcoef_ref[0:8, :] += jnp.broadcast_to(jnp.sum(back, axis=0, keepdims=True), (8, LANES))
    gcoef_ref[8:16, :] += jnp.broadcast_to(
        jnp.sum(by_decay * rate * steps, axis=0, keepdims=True), (8, LANES)
    )


def full(array_shape):
    zeros = (0,) * len(array_shape)
    return pl.BlockSpec(array_shape, lambda i: zeros)


def run(kernel, grid, in_specs, out_specs, out_shapes, args, scratch=(), flops=0):
    return call(kernel, grid, in_specs, out_specs, out_shapes, args, scratch, flops)


def call(kernel, grid, in_specs, out_specs, out_shapes, args, scratch, flops):
    moved = sum(a.size * a.dtype.itemsize for a in args) + sum(
        s.size * s.dtype.itemsize for s in out_shapes
    )
    return pl.pallas_call(
        kernel,
        grid=grid,
        in_specs=in_specs,
        out_specs=out_specs,
        out_shape=out_shapes,
        scratch_shapes=scratch,
        cost_estimate=pl.CostEstimate(flops=flops, bytes_accessed=moved, transcendentals=0),
        compiler_params=pltpu.CompilerParams(
            dimension_semantics=("arbitrary",) * len(grid), vmem_limit_bytes=48 * 2**20
        ),
    )(*args)


def contract(left, right, left_dim, right_dim):
    return lax.dot_general(
        left, right, (((left_dim,), (right_dim,)), ((), ())), preferred_element_type=jnp.float32
    )


def input_norm(source, gain):
    return (
        source * lax.rsqrt(jnp.mean(source * source, axis=1, keepdims=True) + norm_epsilon) * gain
    )


def convolve(padded, tap_table):
    tap_count = tap_table.shape[0] - 1
    length = padded.shape[0] - tap_count + 1
    total = jnp.broadcast_to(tap_table[tap_count], (length, tap_table.shape[1]))
    for offset in range(tap_count):
        total = total + tap_table[offset] * padded[offset : offset + length]
    return jax.nn.silu(total)


def adam_update(weight, gradient, moment_one, moment_two, step_rate):
    step, first_new, second_new = adam_step_of(weight, gradient, moment_one, moment_two, step_rate)
    return (weight - step, first_new, second_new)


def adam_step_of(weight, gradient, moment_one, moment_two, step_rate):
    first_new = beta_first * moment_one + (1.0 - beta_first) * gradient
    second_new = beta_second * moment_two + (1.0 - beta_second) * gradient * gradient
    first_hat = first_new / (1.0 - beta_first**adam_step)
    second_hat = second_new / (1.0 - beta_second**adam_step)
    step = step_rate * (
        first_hat / (jnp.sqrt(second_hat) + adam_epsilon) + weight_decay * weight
    )
    return (step, first_new, second_new)


def early_kernel(normed_ref, back_ref, grad_ref, normal_ref, out_ref):
    width = back_ref.shape[1]
    out_ref[:, :width] = dot(jnp.transpose(normed_ref[...]), back_ref[...], NN)
    out_ref[:, width:] = dot(jnp.transpose(grad_ref[...]), normal_ref[...], NN)


def early_gradients(normed, back_gate, output_grad, normal_out):
    length, rows = normed.shape
    width = back_gate.shape[1]
    block = 2 * CHUNK
    columns = pl.BlockSpec((length, block), lambda i: (0, i))
    return run(
        early_kernel,
        (rows // block,),
        [columns, full((length, width)), columns, full((length, width))],
        [pl.BlockSpec((block, 2 * width), lambda i: (i, 0))],
        [jax.ShapeDtypeStruct((rows, 2 * width), jnp.float32)],
        (normed, back_gate, output_grad, normal_out),
        flops=4 * length * rows * width,
    )[0]


def late_kernel(place_ref, normed_ref, back_ref, keep_ref, send_ref):
    product = dot(normed_ref[...], back_ref[...], NN)
    odd = lax.rem(pl.program_id(0), 2) == 1

    @pl.when(odd)
    def _():
        send_ref[0] = product

    @pl.when(jnp.logical_not(odd))
    def _():
        keep_ref[0] = product


def late_gradients(place, count, normed_lanes, back_late):
    rows, length = normed_lanes.shape
    width = back_late.shape[1]
    block = rows // count
    half = jax.ShapeDtypeStruct((count // 2, block, width), jnp.float32)
    half_spec = pl.BlockSpec((1, block, width), lambda i, place_ref: (i // 2, 0, 0))
    return pl.pallas_call(
        late_kernel,
        grid_spec=pltpu.PrefetchScalarGridSpec(
            num_scalar_prefetch=1,
            grid=(count,),
            in_specs=[
                pl.BlockSpec((block, length), lambda i, place_ref: (place_ref[0] ^ i, 0)),
                pl.BlockSpec((length, width), lambda i, place_ref: (0, 0)),
            ],
            out_specs=[half_spec, half_spec],
        ),
        out_shape=[half, half],
        cost_estimate=pl.CostEstimate(
            flops=2 * rows * length * width,
            bytes_accessed=4 * rows * width + 2 * length * (rows + width),
            transcendentals=0,
        ),
        compiler_params=pltpu.CompilerParams(
            dimension_semantics=("arbitrary",), vmem_limit_bytes=48 * 2**20
        ),
    )(jnp.full((1,), place, jnp.int32), normed_lanes, back_late)


def adam_turned_kernel(grad_ref, weight_ref, one_ref, two_ref, part_ref, sum_ref, first_ref, second_ref):
    gradient = jnp.transpose(grad_ref[...])
    updated, first_new, second_new = adam_update(
        weight_ref[...], gradient, one_ref[...], two_ref[...], rate_matrix
    )
    part_ref[...] = jnp.transpose(updated)
    sum_ref[...] = gradient
    first_ref[...] = first_new
    second_ref[...] = second_new


def adam_turned(gradient, weight, moment_one, moment_two):
    rows, columns = weight.shape
    whole = [full((rows, columns))] * 3
    shape = jax.ShapeDtypeStruct((rows, columns), jnp.float32)
    return run(
        adam_turned_kernel,
        (1,),
        [full((columns, rows))] + whole,
        [full((columns, rows))] + whole,
        [jax.ShapeDtypeStruct((columns, rows), jnp.float32)] + [shape] * 3,
        (gradient, weight, moment_one, moment_two),
    )


def turn_block_kernel(in_ref, out_ref):
    out_ref[...] = jnp.transpose(in_ref[...])


def turned(array):
    rows, columns = array.shape
    block = 2 * CHUNK
    return run(
        turn_block_kernel,
        (rows // block,),
        [pl.BlockSpec((block, columns), lambda i: (i, 0))],
        [pl.BlockSpec((columns, block), lambda i: (0, i))],
        [jax.ShapeDtypeStruct((columns, rows), array.dtype)],
        (array,),
    )[0]


def rows_of_eight(vector):
    return jnp.broadcast_to(vector[None, :], (8, vector.shape[0]))


def layer_step(
    layer_input, output_grad, norm_gain, proj_main, proj_state, proj_step, conv_main, conv_state,
    head_coef, gate_gain, proj_out, first_norm_gain, first_proj_main, first_proj_state,
    first_proj_step, first_conv_main, first_conv_state, first_head_coef, first_gate_gain,
    first_proj_out, second_norm_gain, second_proj_main, second_proj_state, second_proj_step,
    second_conv_main, second_conv_state, second_head_coef, second_gate_gain, second_proj_out,
):
    f32, bf16 = jnp.float32, jnp.bfloat16
    length, model_width = layer_input.shape
    local_heads = proj_step.shape[1]
    inner_width = proj_main.shape[2]
    head_size = inner_width // local_heads
    state_local = proj_state.shape[2]
    tap_count = conv_main.shape[0] - 1
    head_count = lax.axis_size("head")
    seq_count = lax.axis_size("seq")
    seq_index = lax.axis_index("seq")
    head_index = lax.axis_index("head")
    state_size = state_local * head_count
    full_inner = inner_width * head_count
    chunks = length // CHUNK
    chunk_row = pl.BlockSpec((CHUNK, inner_width), lambda i: (i, 0))
    chunk_lane = pl.BlockSpec((state_size, CHUNK), lambda i: (0, i))
    chunk_head = pl.BlockSpec((HEAD_ROWS, CHUNK), lambda i: (0, i))
    chunk_small = pl.BlockSpec((CHUNK, LANES), lambda i: (i, 0))
    chunk_state = pl.BlockSpec((CHUNK, state_size), lambda i: (i, 0))
    state_block = pl.BlockSpec((1, state_size, inner_width), lambda i: (i, 0, 0))
    next_state = pl.BlockSpec((1, state_size, inner_width), lambda i: (i + 1, 0, 0))
    row_block = pl.BlockSpec((1, 8, inner_width), lambda i: (i, 0, 0))
    next_row = pl.BlockSpec((1, 8, inner_width), lambda i: (i + 1, 0, 0))
    state_full = full((state_size, inner_width))
    row_full = full((8, inner_width))
    row_shape = jax.ShapeDtypeStruct((length, inner_width), f32)
    small_shape = jax.ShapeDtypeStruct((length, LANES), f32)
    state_shape = jax.ShapeDtypeStruct((state_size, inner_width), f32)
    scan_flops = 2 * 3 * length * inner_width * (2 * CHUNK + state_size)

    halo = 16
    rim = halo - (tap_count - 1)
    source = plain(layer_input.astype(f32))
    rim_source = from_behind(source[length - halo :], "seq", 1)
    normed = plain(input_norm(source, norm_gain).astype(bf16))
    normed_long = jnp.concatenate([input_norm(rim_source, norm_gain).astype(bf16), normed], axis=0)
    state_weight = proj_state.reshape(model_width, 2 * state_local).astype(bf16)
    step_weight = proj_step.astype(bf16)
    step_wide = jnp.pad(step_weight, ((0, 0), (0, LANES - local_heads)))
    out_weight = after(proj_out.astype(bf16))
    coef_wide = jnp.pad(head_coef, ((0, 8 - head_coef.shape[0]), (0, LANES - local_heads)))
    skip_wide = rows_of_eight(jnp.repeat(head_coef[2], head_size))
    gain_wide = rows_of_eight(gate_gain)

    state_pre = jnp.dot(normed_long, state_weight, preferred_element_type=f32)
    state_taps = conv_state.reshape(tap_count + 1, 2 * state_local)
    state_active, state_pull = jax.vjp(convolve, state_pre[rim:], state_taps)
    state_lanes = state_active.T
    pair_lanes = ring_gather(state_lanes, "head")
    halves = after(jnp.transpose(proj_main, (1, 0, 2)).astype(bf16), state_lanes)
    gate_weight, value_weight = halves[0], halves[1]
    value_pre = jnp.dot(normed_long, value_weight, preferred_element_type=f32)
    values, value_pull = jax.vjp(convolve, value_pre[rim:], conv_main)
    step_pre = jnp.dot(normed, step_wide, preferred_element_type=f32)
    gate_pre = jnp.dot(normed, gate_weight, preferred_element_type=f32)
    pair_lanes = pair_lanes.reshape(head_count, 2, state_local, length)
    input_lanes = pair_lanes[:, 0].reshape(state_size, length)
    output_lanes = pair_lanes[:, 1].reshape(state_size, length)

    steps, steps_wide, cum_wide, cum_lanes, states, before, beyond = run(
        functools.partial(states_kernel, head_size),
        (1,),
        [full(a.shape) for a in (values, input_lanes, step_pre, coef_wide)],
        [
            full((length, LANES)),
            full((length, inner_width)),
            full((length, inner_width)),
            full((HEAD_ROWS, length)),
            full((chunks + 1, state_size, inner_width)),
            full((chunks + 1, 8, inner_width)),
            full((chunks, 8, inner_width)),
        ],
        [
            small_shape,
            row_shape,
            row_shape,
            jax.ShapeDtypeStruct((HEAD_ROWS, length), f32),
            jax.ShapeDtypeStruct((chunks + 1, state_size, inner_width), f32),
            jax.ShapeDtypeStruct((chunks + 1, 8, inner_width), f32),
            jax.ShapeDtypeStruct((chunks, 8, inner_width), f32),
        ],
        (values, input_lanes, step_pre, coef_wide),
        flops=scan_flops // 3,
    )
    through = before[chunks, 0:1]
    start_state = carried_state(through, states[chunks], "seq", False)
    local_out = run(
        functools.partial(within_kernel, head_size),
        (chunks,),
        [chunk_row, chunk_lane, chunk_lane, chunk_row, chunk_row, chunk_head, state_block],
        [chunk_row],
        [row_shape],
        (values, input_lanes, output_lanes, steps_wide, cum_wide, cum_lanes, states),
        flops=scan_flops,
    )[0]
    back_normal = contract(output_grad, out_weight, 1, 1)
    mixed, sums = run(
        gate_kernel,
        (chunks,),
        [
            chunk_row, chunk_lane, chunk_row, row_block, state_full, chunk_row, row_full,
            chunk_row, chunk_row, row_full,
        ],
        [chunk_row, pl.BlockSpec((16, CHUNK), lambda i: (0, i))],
        [row_shape, jax.ShapeDtypeStruct((16, length), f32)],
        (
            local_out, output_lanes, cum_wide, before, start_state, values, skip_wide,
            gate_pre, back_normal, gain_wide,
        ),
        flops=scan_flops // 4,
    )
    sums = sum_all(sums, "head")
    reverse_row = pl.BlockSpec((CHUNK, inner_width), lambda i: (chunks - 1 - i, 0))
    reverse_lane = pl.BlockSpec((state_size, CHUNK), lambda i: (0, chunks - 1 - i))
    normal_out, back_mixed, back_gate, grad_gate, grad_skip, later_local, state_jump = run(
        functools.partial(turn_kernel, float(full_inner)),
        (chunks,),
        [
            pl.BlockSpec((16, CHUNK), lambda i: (0, chunks - 1 - i)),
            reverse_row, reverse_row, reverse_row, row_full, reverse_row, reverse_row,
            reverse_lane, row_full,
        ],
        [
            reverse_row, reverse_row, reverse_row, row_full, row_full,
            pl.BlockSpec((1, state_size, inner_width), lambda i: (chunks - 1 - i, 0, 0)),
            state_full,
        ],
        [
            jax.ShapeDtypeStruct((length, inner_width), bf16),
            row_shape,
            jax.ShapeDtypeStruct((length, inner_width), bf16),
            jax.ShapeDtypeStruct((8, inner_width), f32),
            jax.ShapeDtypeStruct((8, inner_width), f32),
            jax.ShapeDtypeStruct((chunks, state_size, inner_width), f32),
            state_shape,
        ],
        (
            sums, mixed, gate_pre, back_normal, gain_wide, values, cum_wide, output_lanes,
            skip_wide,
        ),
        scratch=[pltpu.VMEM((state_size, inner_width), f32)],
        flops=scan_flops // 4,
    )
    later_grad = carried_state(through, state_jump, "seq", True)

    col_count = model_width // head_count

    def out_block(index):
        columns = lax.dynamic_slice_in_dim(out_weight, index * col_count, col_count, 1)
        return plain(jnp.dot(normal_out, columns, preferred_element_type=f32))

    out_cols, out_sent = line_scatter(out_block, "head")
    sum_early = scatter_rows(
        early_gradients(normed, back_gate, output_grad, after(normal_out, *out_sent[0])), "seq"
    )
    back_tied = after(back_mixed, *out_sent[1])
    z_local, db_local, dc_local = run(
        functools.partial(back_within_kernel, head_size),
        (chunks,),
        [
            chunk_row, chunk_lane, chunk_lane, chunk_row, chunk_row, chunk_head, state_block,
            row_block, state_full, chunk_row, state_block,
        ],
        [chunk_row, chunk_state, chunk_state],
        [
            row_shape,
            jax.ShapeDtypeStruct((length, state_size), f32),
            jax.ShapeDtypeStruct((length, state_size), f32),
        ],
        (
            values, input_lanes, output_lanes, steps_wide, cum_wide, cum_lanes, states, before,
            start_state, back_tied, later_local,
        ),
        flops=2 * scan_flops,
    )
    z_local = after(z_local, *out_sent[2])
    back_values, back_in, back_out, back_step_pre, grad_coef_rows = run(
        functools.partial(back_steps_kernel, head_size),
        (chunks,),
        [
            chunk_row, chunk_lane, chunk_row, chunk_row, chunk_small, chunk_small,
            full(coef_wide.shape), row_full, chunk_row, chunk_row, chunk_row, chunk_state,
            chunk_state, state_block, state_full, row_block, next_state, next_row, state_full,
        ],
        [chunk_row, chunk_lane, chunk_lane, chunk_small, full((16, LANES))],
        [
            row_shape,
            jax.ShapeDtypeStruct((state_size, length), f32),
            jax.ShapeDtypeStruct((state_size, length), f32),
            small_shape,
            jax.ShapeDtypeStruct((16, LANES), f32),
        ],
        (
            values, input_lanes, steps_wide, cum_wide, steps, step_pre, coef_wide, skip_wide,
            mixed, back_mixed, z_local, db_local, dc_local, later_local, later_grad, beyond, states,
            before, start_state,
        ),
        flops=scan_flops // 2,
    )
    grad_coef = jnp.stack(
        [
            grad_coef_rows[0, :local_heads],
            grad_coef_rows[8, :local_heads],
            jnp.sum(grad_skip[0].reshape(local_heads, head_size), axis=1),
        ]
    )
    back_pair = jnp.stack([back_in, back_out]).reshape(2, head_count, state_local, length)

    def pair_block(index):
        return lax.dynamic_index_in_dim(back_pair, index, 1, False)

    back_local_pair = pair_block(head_index)
    for by in range(1, head_count):
        back_local_pair = back_local_pair + shift(
            pair_block(lax.rem(head_index + by, head_count)), "head", by
        )
    value_padded, value_taps_grad = value_pull(back_values)
    state_padded, state_taps_grad = state_pull(
        back_local_pair.reshape(2 * state_local, length).T
    )
    grad_taps = jnp.concatenate([value_taps_grad, state_taps_grad], axis=1)
    back_padded = jnp.concatenate([value_padded, state_padded], axis=1)
    rim_back = from_behind(back_padded[: tap_count - 1], "seq", -1)
    back_conv = back_padded[tap_count - 1 :]
    rim_start = length - tap_count + 1
    back_conv = jnp.concatenate([back_conv[:rim_start], back_conv[rim_start:] + rim_back], axis=0)
    back_late = jnp.concatenate([back_conv, back_step_pre[:, :local_heads]], axis=1).astype(bf16)
    residual_cols = lax.dynamic_slice_in_dim(source, head_index * col_count, col_count, 1)
    layer_output = plain((residual_cols + out_cols).astype(bf16))
    late_weight = jnp.concatenate([value_weight, state_weight, step_weight], axis=1)
    shard_rows = length // head_count

    row_size = lax.rsqrt(jnp.mean(source * source, axis=1, keepdims=True) + norm_epsilon)
    unit = source * row_size
    grad_gain = []

    def normed_block(index):
        gate_rows = lax.dynamic_slice_in_dim(back_gate, index * shard_rows, shard_rows, 0)
        late_rows = lax.dynamic_slice_in_dim(back_late, index * shard_rows, shard_rows, 0)
        block = contract(gate_rows, gate_weight, 1, 1) + contract(late_rows, late_weight, 1, 1)
        unit_rows = lax.dynamic_slice_in_dim(unit, index * shard_rows, shard_rows, 0)
        block = plain(after(block))
        grad_gain.append(jnp.sum(block * unit_rows, axis=0))
        return block

    back_normed, normed_sent = line_scatter(normed_block, "head")
    late_keep, late_send = late_gradients(
        seq_index, seq_count, normed.T, after(back_late, out_cols, *normed_sent[0])
    )
    sum_late = scatter_relative(late_keep, late_send, "seq", normed_sent[1])
    sum_late = after(sum_late, *normed_sent[2])
    sum_early = after(sum_early, *normed_sent[0])
    sum_gate_half = sum_early[:, :inner_width]
    sum_out_turned = sum_early[:, inner_width:]
    own_source = lax.dynamic_slice_in_dim(source, head_index * shard_rows, shard_rows, 0)
    _, norm_pull = jax.vjp(lambda rows: input_norm(rows, norm_gain), own_source)
    (back_source,) = norm_pull(back_normed)

    def own_rows(array, along):
        piece_len = array.shape[along] // seq_count
        return lax.dynamic_slice_in_dim(array, seq_index * piece_len, piece_len, along)

    part_out, sum_out, first_out, second_out = adam_turned(
        sum_out_turned, own_rows(proj_out, 1), first_proj_out, second_proj_out
    )
    new_out = turned(gather_rows(part_out, "seq"))

    sum_main = jnp.stack([sum_gate_half, sum_late[:, :inner_width]], axis=1)
    step_main, first_main, second_main = adam_step_of(
        own_rows(proj_main, 0), sum_main, first_proj_main, second_proj_main, rate_matrix
    )
    step_main = plain(gather_rows(plain(step_main), "seq"))
    new_main = proj_main - step_main
    new_main = plain(new_main)
    sum_state = sum_late[:, inner_width : inner_width + 2 * state_local]
    part_state, first_state, second_state = adam_update(
        own_rows(proj_state, 0).reshape(-1, 2 * state_local),
        sum_state,
        first_proj_state.reshape(-1, 2 * state_local),
        second_proj_state.reshape(-1, 2 * state_local),
        rate_matrix,
    )
    sum_step = sum_late[:, inner_width + 2 * state_local :]
    part_step, first_step, second_step = adam_update(
        own_rows(proj_step, 0), sum_step, first_proj_step, second_proj_step, rate_matrix
    )
    new_small = gather_small(jnp.concatenate([part_state, part_step], axis=1), "seq")
    new_state = new_small[:, : 2 * state_local].reshape(model_width, 2, state_local)
    new_step = new_small[:, 2 * state_local :]
    state_form = (-1, 2, state_local)

    taps_wide = inner_width + 2 * state_local
    gain_rows = sum_of(grad_gain).reshape(8, model_width // 8)
    small = jnp.concatenate(
        [
            grad_taps.reshape(-1),
            grad_gate[0],
            grad_coef.reshape(-1),
        ]
    )
    small_size = small.shape[0]
    padded_size = -(-small_size // 1024) * 1024
    small = jnp.pad(small, (0, padded_size - small_size)).reshape(8, padded_size // 8)
    small = sum_all(jnp.concatenate([small, gain_rows], axis=1), "seq")
    sum_gain = small[:, padded_size // 8 :]
    for bit in bits_of("head"):
        got_gain = swap(sum_gain, "head", bit)
        sum_gain = sum_gain + got_gain
    sum_gain = sum_gain.reshape(-1)
    small = small[:, : padded_size // 8].reshape(-1)
    taps_size = (tap_count + 1) * taps_wide
    sum_taps = small[:taps_size].reshape(tap_count + 1, taps_wide)
    back_rows, _ = line_gather(after(back_source, sum_gain), "head")
    back_rows = back_rows.reshape(length, model_width)
    input_grad = plain((output_grad.astype(f32) + plain(back_rows)).astype(bf16))
    sum_cmain = sum_taps[:, :inner_width]
    sum_cstate = sum_taps[:, inner_width:].reshape(tap_count + 1, 2, state_local)
    sum_gate = small[taps_size : taps_size + inner_width]
    sum_coef = small[taps_size + inner_width : small_size].reshape(3, local_heads)
    new_gain, first_gain, second_gain = adam_update(
        norm_gain, sum_gain, first_norm_gain, second_norm_gain, rate_vector
    )
    new_cmain, first_cmain, second_cmain = adam_update(
        conv_main, sum_cmain, first_conv_main, second_conv_main, rate_vector
    )
    new_cstate, first_cstate, second_cstate = adam_update(
        conv_state, sum_cstate, first_conv_state, second_conv_state, rate_vector
    )
    new_coef, first_coef, second_coef = adam_update(
        head_coef, sum_coef, first_head_coef, second_head_coef, rate_coef
    )
    new_gate, first_gate, second_gate = adam_update(
        gate_gain, sum_gate, first_gate_gain, second_gate_gain, rate_vector
    )
    return (
        layer_output, input_grad, sum_gain, sum_main, sum_state.reshape(state_form), sum_step,
        sum_cmain, sum_cstate, sum_coef, sum_gate, sum_out, new_gain, new_main, new_state,
        new_step, new_cmain, new_cstate, new_coef, new_gate, new_out, first_gain, first_main,
        first_state.reshape(state_form), first_step, first_cmain, first_cstate, first_coef,
        first_gate, first_out, second_gain, second_main, second_state.reshape(state_form),
        second_step, second_cmain, second_cstate, second_coef, second_gate, second_out,
    )


def solution(mesh):
    return jax.shard_map(
        layer_step,
        mesh=mesh,
        in_specs=(
            P("seq", None),
            P("seq", None),
            P(),
            P(None, None, "head"),
            P(None, None, "head"),
            P(None, "head"),
            P(None, "head"),
            P(None, None, "head"),
            P(None, "head"),
            P("head"),
            P("head", None),
            P(),
            P("seq", None, "head"),
            P("seq", None, "head"),
            P("seq", "head"),
            P(None, "head"),
            P(None, None, "head"),
            P(None, "head"),
            P("head"),
            P("head", "seq"),
            P(),
            P("seq", None, "head"),
            P("seq", None, "head"),
            P("seq", "head"),
            P(None, "head"),
            P(None, None, "head"),
            P(None, "head"),
            P("head"),
            P("head", "seq"),
        ),
        out_specs=(
            P("seq", "head"),
            P("seq", None),
            P(),
            P("seq", None, "head"),
            P("seq", None, "head"),
            P("seq", "head"),
            P(None, "head"),
            P(None, None, "head"),
            P(None, "head"),
            P("head"),
            P("head", "seq"),
            P(),
            P(None, None, "head"),
            P(None, None, "head"),
            P(None, "head"),
            P(None, "head"),
            P(None, None, "head"),
            P(None, "head"),
            P("head"),
            P("head", None),
            P(),
            P("seq", None, "head"),
            P("seq", None, "head"),
            P("seq", "head"),
            P(None, "head"),
            P(None, None, "head"),
            P(None, "head"),
            P("head"),
            P("head", "seq"),
            P(),
            P("seq", None, "head"),
            P("seq", None, "head"),
            P("seq", "head"),
            P(None, "head"),
            P(None, None, "head"),
            P(None, "head"),
            P("head"),
            P("head", "seq"),
        ),
        check_vma=False,
    )
```
